32 devices in a mesh: rows: 8 (over z, x), heads: 4 (over y, core).
Axes of the slice: x: 2, y: 2, z: 4, core: 2. Of those that a mesh axis runs over, the one named last changes fastest.
Arguments:
- pixels: bfloat16 [8192, 1024], P('rows'), may hold values from -6 to 6
- crop_ids: int32 [8192], P('rows'), may hold values from 0 to 3, never falling along the last dimension, each value on 1 to 4096 neighbouring positions
- first_gain: float32 [1024], replicated, may hold values from 0.1 to 1.9
- query_weight: bfloat16 [1024, 1024], P(None, 'heads'), may hold values from -0.1875 to 0.1875
- key_weight: bfloat16 [1024, 1024], P(None, 'heads'), may hold values from -0.1875 to 0.1875
- value_weight: bfloat16 [1024, 1024], P(None, 'heads'), may hold values from -0.1875 to 0.1875
- out_weight: bfloat16 [1024, 1024], P('heads'), may hold values from -0.75 to 0.75
- second_gain: float32 [1024], replicated, may hold values from 0.1 to 1.9
- up_weight: bfloat16 [1024, 4096], P(None, 'heads'), may hold values from -0.1875 to 0.1875
- down_weight: bfloat16 [4096, 1024], P('heads'), may hold values from -0.09375 to 0.09375
- cotangent: bfloat16 [8192, 1024], P('rows'), may hold values from -6 to 6
Outputs:
- result: bfloat16 [8192, 1024], P('rows')
- pixel_gradient: float32 [8192, 1024], P('rows')
- first_gain_gradient: float32 [1024], P('rows')
- query_gradient: float32 [1024, 1024], P('rows', 'heads')
- key_gradient: float32 [1024, 1024], P('rows', 'heads')
- value_gradient: float32 [1024, 1024], P('rows', 'heads')
- out_gradient: float32 [1024, 1024], P('heads', 'rows')
- second_gain_gradient: float32 [1024], P('rows')
- up_gradient: float32 [1024, 4096], P('rows', 'heads')
- down_gradient: float32 [4096, 1024], P('heads', 'rows')
The draws below stay inside these ranges and needn't reach their ends.
Inputs may be any that keep to these rules, and one draw needn't show every extreme that they name: `crop_ids`: crop ids never fall along the tokens; each crop holds 1 to 4096 consecutive tokens, and one holds exactly 4096.
All inputs are finite; a program needn't handle non-finite values.
Results may differ from the reference program's by a relative error of at most 0.017.
Values sent between devices are 32-bit elements; how exact they have to be, the bound alone decides.
A program may use at most 128 MiB of HBM per device.

```python
import math
import jax
import jax.numpy as jnp
import numpy as np
from jax import lax

D = 1024
HEADS = 16
HEAD = 64
FF = 4096
TOK_DEV = 1024
CROPS = 4
TOKENS = 8192
CROP_MOST = 4096
N_ROWS = 8


def levels(key, extent, cuts, low, top_value):
    def one(axis_at, blocks):
        heights = jax.random.uniform(jax.random.fold_in(jax.random.fold_in(key, 6), axis_at), (blocks,), jnp.float32, low / len(cuts), top_value / len(cuts))
        return jnp.repeat(jnp.exp(heights), extent[axis_at] // blocks).reshape((-1,) + (1,) * (len(extent) - axis_at - 1))

    level = one(*cuts[0])
    for cut in cuts[1:]:
        level = level * one(*cut)
    return level


def profile(amount, total, limit, slope):
    loads = [(1 << 20) // math.isqrt(rank ** slope) + 1 for rank in range(2, amount + 1)]
    rest, holding = total - limit - (amount - 1), [1] * (amount - 1)
    while rest > 0:
        candidates = [i for i in range(amount - 1) if holding[i] < limit]
        whole, remaining = sum([loads[i] for i in candidates]), rest
        for i in candidates:
            extra = min(limit - holding[i], max(1, remaining * loads[i] // whole), rest)
            holding[i] = holding[i] + extra
            rest = rest - extra
    return np.array([limit] + holding)


def uneven(rng, amount, total, bound, slope):
    if amount == 2:
        one = jax.random.randint(rng, (), max(1, total - bound), min(bound, total - 1) + 1)
        return jnp.stack([one, total - one])
    lengths = jnp.asarray(profile(amount, total, bound, slope), jnp.int32)
    pairs = (amount - 1) // 2
    donor, receiver = lengths[1:1 + 2 * pairs:2], lengths[2:2 + 2 * pairs:2]
    room = jnp.minimum(donor - 1, bound - receiver)
    moved = jax.random.randint(jax.random.fold_in(rng, 1), (pairs,), 0, 1 << 20) % (room + 1)
    lengths = lengths.at[1:1 + 2 * pairs:2].set(donor - moved).at[2:2 + 2 * pairs:2].set(receiver + moved)
    return lengths[jax.random.permutation(jax.random.fold_in(rng, 2), amount)]


def bell_draw(stream_key, shape, scale, bound, cuts=(), dtype=jnp.bfloat16):
    level = levels(stream_key, shape, cuts, -0.22, 0.18) if cuts else 1.0
    drawn = jax.random.normal(stream_key, shape, jnp.float32) * scale * level
    return jnp.minimum(jnp.maximum(drawn, -bound), bound).astype(dtype)


def setup_inputs(seed: int = 0) -> dict:
    key_of = jax.random.split(jax.random.key(seed), 12)
    pixels = bell_draw(key_of[0], (TOKENS, D), 1.0, 6.0, ((0, 8),))
    crop_ids = jnp.searchsorted(jnp.cumsum(uneven(key_of[1], CROPS, TOKENS, CROP_MOST, 2)), jnp.arange(TOKENS), side="right").astype(jnp.int32)
    first_gain = jnp.clip(1.0 + 0.18 * jax.random.normal(key_of[2], (D,), jnp.float32), 0.1, 1.9)
    query_weight = bell_draw(key_of[3], (D, D), D ** -0.5, 0.1875, ((1, 4),))
    key_weight = bell_draw(key_of[4], (D, D), D ** -0.5, 0.1875, ((1, 4),))
    value_weight = bell_draw(key_of[5], (D, D), D ** -0.5, 0.1875, ((1, 4),))
    out_weight = bell_draw(key_of[6], (D, D), (D // 16) ** -0.5, 0.75, ((0, 4),))
    second_gain = jnp.clip(1.0 + 0.18 * jax.random.normal(key_of[7], (D,), jnp.float32), 0.1, 1.9)
    up_weight = bell_draw(key_of[8], (D, FF), D ** -0.5, 0.1875, ((1, 4),))
    down_weight = bell_draw(key_of[9], (FF, D), FF ** -0.5, 0.09375, ((0, 4),))
    cotangent = bell_draw(key_of[10], (TOKENS, D), 1.0, 6.0, ((0, 8),))
    return dict(pixels=pixels, crop_ids=crop_ids, first_gain=first_gain, query_weight=query_weight, key_weight=key_weight, value_weight=value_weight, out_weight=out_weight, second_gain=second_gain, up_weight=up_weight, down_weight=down_weight, cotangent=cotangent)


@jax.custom_vjp
def low(v):
    return lax.optimization_barrier(v.astype(jnp.bfloat16)).astype(jnp.float32)

@jax.custom_vjp
def low_back(v):
    return v

def low_keep(v):
    return (low(v), None)

def low_pass(kept, grad):
    return (grad,)

def back_keep(v):
    return (v, None)

def back_low(kept, grad):
    return (low(grad),)
low.defvjp(low_keep, low_pass)
low_back.defvjp(back_keep, back_low)
EPSILON = 1e-05
PRECISE = lax.Precision.HIGHEST

def layer_norm(value, gain):
    middle = lax.optimization_barrier(jnp.mean(value, axis=-1, keepdims=True))
    centred = value - middle
    spread = lax.optimization_barrier(jnp.mean(centred * centred, axis=-1, keepdims=True))
    return centred * lax.rsqrt(spread + EPSILON) * gain

def feature(value):
    return jax.nn.elu(value) + 1.0

def product(left, right):
    return jnp.dot(left, right, precision=PRECISE)

def attend_block(running, pieces):
    prefix_state, totals, latest = running
    query_feature, key_feature, values, labels = pieces
    length = labels.shape[0]
    places = jnp.arange(length)
    allowed = (places[:, None] >= places[None, :]) & (labels[:, None] == labels[None, :])
    scores = jnp.einsum('ihe,jhe->hij', query_feature, key_feature, precision=PRECISE)
    scores = low_back(jnp.where(allowed[None], scores, 0.0))
    inner_total = lax.optimization_barrier(jnp.sum(scores, axis=2)).T
    numerator = jnp.einsum('hij,jhe->ihe', low(scores), values, precision=PRECISE)
    matching = (labels == latest).astype(jnp.float32)
    numerator = numerator + matching[:, None, None] * jnp.einsum('ihe,hef->ihf', query_feature, low(prefix_state), precision=PRECISE)
    denominator = inner_total + matching[:, None] * jnp.einsum('ihe,he->ih', query_feature, totals, precision=PRECISE)
    numerator = low_back(numerator)
    attended = numerator / denominator[:, :, None]
    ending = labels[length - 1]
    tail_mask = (labels == ending).astype(jnp.float32)
    block_state = low_back(jnp.einsum('ihe,ihf->hef', key_feature * tail_mask[:, None, None], values, precision=PRECISE))
    block_total = jnp.einsum('ihe,i->he', key_feature, tail_mask, precision=PRECISE)
    carried = (latest == ending).astype(jnp.float32)
    return ((block_state + carried * prefix_state, block_total + carried * totals, ending), attended)

def forward(pixels, first_gain, query_weight, key_weight, value_weight, out_weight, second_gain, up_weight, down_weight, labels):
    normed = low(layer_norm(pixels, first_gain))
    query_feature = low(feature(low_back(product(normed, query_weight))))
    key_feature = low(feature(low_back(product(normed, key_weight))))
    values = low(low_back(product(normed, value_weight)))
    blocked = (N_ROWS, TOK_DEV, HEADS, HEAD)
    pieces = (query_feature.reshape(blocked), key_feature.reshape(blocked), values.reshape(blocked), labels.reshape(N_ROWS, TOK_DEV))
    start = (jnp.zeros((HEADS, HEAD, HEAD), jnp.float32), jnp.zeros((HEADS, HEAD), jnp.float32), jnp.float32(-1.0))
    unused, attended = lax.scan(jax.checkpoint(attend_block), start, pieces)
    attended = low(attended.reshape(TOKENS, D))
    hidden = pixels + low_back(product(attended, out_weight))
    normed_again = low(layer_norm(hidden, second_gain))
    upward = low_back(product(normed_again, up_weight))
    middle = low(jax.nn.gelu(upward))
    return hidden + low_back(product(middle, down_weight))

def reference(pixels, crop_ids, first_gain, query_weight, key_weight, value_weight, out_weight, second_gain, up_weight, down_weight, cotangent):
    labels = crop_ids.astype(jnp.float32)

    def layer(pixel_values, gain_one, query_values, key_values, value_values, out_values, gain_two, up_values, down_values):
        return forward(pixel_values, gain_one, query_values, key_values, value_values, out_values, gain_two, up_values, down_values, labels)
    output, pull_back = jax.vjp(layer, pixels.astype(jnp.float32), first_gain.astype(jnp.float32), query_weight.astype(jnp.float32), key_weight.astype(jnp.float32), value_weight.astype(jnp.float32), out_weight.astype(jnp.float32), second_gain.astype(jnp.float32), up_weight.astype(jnp.float32), down_weight.astype(jnp.float32))
    gradients = pull_back(cotangent.astype(jnp.float32))
    return (output.astype(jnp.bfloat16), gradients[0], gradients[1], gradients[2], gradients[3], gradients[4], gradients[5], gradients[6], gradients[7], gradients[8])
```

```python
import functools
import math

import jax
import jax.numpy as jnp
from jax import lax
from jax.experimental import pallas as pl
from jax.experimental.pallas import tpu as pltpu
from jax.sharding import PartitionSpec as P

HEAD = 64
EPSILON = 1e-05
MESH = pl.DeviceIdType.MESH
LOW = jnp.bfloat16
WIDE = jnp.float32
LANES = 128
TILE = 256


def dot(left, right):
    return jnp.dot(left, right, preferred_element_type=WIDE)


def dot_left(left, right):
    return lax.dot_general(left, right, (((0,), (0,)), ((), ())), preferred_element_type=WIDE)


def dot_right(left, right):
    return lax.dot_general(left, right, (((1,), (1,)), ((), ())), preferred_element_type=WIDE)


def normalise(value):
    middle = jnp.mean(value, axis=-1, keepdims=True)
    centred = value - middle
    spread = jnp.mean(centred * centred, axis=-1, keepdims=True)
    scale = lax.rsqrt(spread + EPSILON)
    return centred * scale, scale


def normalise_back(unit, scale, gain, grad):
    scaled = grad * gain
    along = jnp.mean(scaled * unit, axis=-1, keepdims=True)
    return scale * (scaled - jnp.mean(scaled, axis=-1, keepdims=True) - unit * along)


class Sizes:
    def __init__(self, rows, heads, tokens, model, width, units):
        self.rows, self.heads = rows, heads
        self.ny = heads // 2
        self.nx = self.ny if rows % self.ny == 0 else 1
        self.nz = rows // self.nx
        self.tokens, self.model, self.width, self.units = tokens, model, width, units
        self.chunk = min(TILE, tokens)
        self.chunks = tokens // self.chunk
        self.sub = self.chunk // heads
        self.here = width // HEAD
        self.pairs = width // LANES
        self.tiles = (self.pairs + 1) // 2
        self.message = self.tiles * LANES + 8
        self.cut = model // rows


class Place:
    def __init__(self, sizes):
        s = self.s = sizes
        self.row = lax.axis_index("rows")
        self.head = lax.axis_index("heads")
        self.y, self.c = self.head // 2, lax.rem(self.head, 2)
        self.x, self.z = lax.rem(self.row, s.nx), self.row // s.nx

    def other(self):
        return (self.row, self.y * 2 + 1 - self.c)

    def group(self, step):
        return lax.rem(self.y + self.s.ny - step, self.s.ny) * 2 + self.c

    def along_y(self, step):
        return (self.row, lax.rem(self.y + step, self.s.ny) * 2 + self.c)

    def along_x(self, step):
        return (self.z * self.s.nx + lax.rem(self.x + step, self.s.nx), self.head)

    def along_z(self, step):
        return (lax.rem(self.z + step, self.s.nz) * self.s.nx + self.x, self.head)

    def along_rows(self, step):
        return (lax.rem(self.row + step, self.s.rows), self.head)

    def along_heads(self, step):
        return (self.row, lax.rem(self.head + step, self.s.heads))

    def meet(self):
        barrier = pltpu.get_barrier_semaphore()
        for step in range(1, self.s.heads):
            pl.semaphore_signal(barrier, inc=1, device_id=self.along_heads(step), device_id_type=MESH)
        for step in range(1, self.s.rows):
            pl.semaphore_signal(barrier, inc=1, device_id=self.along_rows(step), device_id_type=MESH)
        pl.semaphore_wait(barrier, self.s.heads + self.s.rows - 2)


def remote(source, target, send, receive, device):
    return pltpu.make_async_remote_copy(
        src_ref=source, dst_ref=target, send_sem=send, recv_sem=receive, device_id=device, device_id_type=MESH
    )


class Gather:
    def __init__(self, place, view, send, receive, own=None):
        self.p, self.view, self.send, self.receive = place, view, send, receive
        self.own = own

    def copy(self, group, k, slot, device):
        source = self.view(group, k)
        return remote(source, self.view(group, k), self.send.at[slot, k], self.receive.at[group, k], device)

    def own_copy(self, k, slot, device):
        group = self.p.head
        source = self.view(group, k) if self.own is None else self.own(k)
        return remote(source, self.view(group, k), self.send.at[slot, k], self.receive.at[group, k], device)

    def start(self, k):
        for step in range(1, self.p.s.ny):
            self.own_copy(k, step, self.p.along_y(step)).start()
        self.own_copy(k, 0, self.p.other()).start()

    def forward(self, k):
        ny = self.p.s.ny
        for step in range(1, ny):
            group = self.p.group(step)
            self.copy(group, k, 0, self.p.along_y(step)).wait_recv()
            self.copy(group, k, ny - 1 + step, self.p.other()).start()

    def finish(self, k):
        for step in range(self.p.s.ny):
            own = self.p.group(step)
            group = own + 1 - 2 * self.p.c
            self.copy(group, k, 0, self.p.other()).wait_recv()

    def sent(self, k):
        ny = self.p.s.ny
        for step in range(ny):
            self.own_copy(k, step, self.p.other()).wait_send()
        for step in range(1, ny):
            self.copy(self.p.group(step), k, ny - 1 + step, self.p.other()).wait_send()


class Reduce:
    def __init__(self, place, parts, near, far, sems):
        self.p, self.parts, self.near, self.far = place, parts, near, far
        self.near_send, self.near_recv, self.far_send, self.far_recv = sems

    def near_copy(self, k):
        return remote(
            self.parts.at[k, 1 - self.p.c],
            self.near.at[k],
            self.near_send.at[k],
            self.near_recv.at[k],
            self.p.other(),
        )

    def far_copy(self, k, step):
        share = lax.rem(self.p.y + step, self.p.s.ny)
        return remote(
            self.near.at[k, share],
            self.far.at[step - 1, k],
            self.far_send.at[step - 1, k],
            self.far_recv.at[step - 1, k],
            self.p.along_y(step),
        )

    def start(self, k):
        self.near_copy(k).start()

    def middle(self, k):
        self.near_copy(k).wait_recv()
        for step in range(self.p.s.ny):
            share = lax.rem(self.p.y + self.p.s.ny - 1 - step, self.p.s.ny)
            self.near[k, share] = self.near[k, share] + self.parts[k, self.p.c, share]
        for step in range(1, self.p.s.ny):
            self.far_copy(k, step).start()

    def total(self, k):
        value = self.near[k, self.p.y]
        for step in range(1, self.p.s.ny):
            self.far_copy(k, step).wait_recv()
            value = value + self.far[step - 1, k]
        return value

    def near_sent(self, k):
        self.near_copy(k).wait_send()

    def far_sent(self, k):
        for step in range(1, self.p.s.ny):
            self.far_copy(k, step).wait_send()


def iota(shape, axis):
    return lax.broadcasted_iota(jnp.int32, shape, axis)


def head_lanes(width, head):
    lanes = iota((1, width), 1) // HEAD
    return (lanes == head).astype(WIDE)


def only(value, lanes):
    return (value.astype(WIDE) * lanes).astype(LOW)


def block_ones(width):
    return (iota((width, width), 0) // HEAD == iota((width, width), 1) // HEAD).astype(WIDE).astype(LOW)


def over_heads(product, ones):
    high = product.astype(LOW)
    rest = (product - high.astype(WIDE)).astype(LOW)
    return dot(high, ones) + dot(rest, ones)


def same_head():
    return iota((LANES, LANES), 0) // HEAD == iota((LANES, LANES), 1) // HEAD


def write_message(s, message, state, total, label):
    same = same_head()
    for tile in range(s.tiles):
        first = 2 * tile * LANES
        block = jnp.where(same, state[first : first + LANES, first : first + LANES], 0.0)
        if 2 * tile + 1 < s.pairs:
            second = first + LANES
            more = jnp.where(same, state[second : second + LANES, second : second + LANES], 0.0)
            block = block + pltpu.roll(more, HEAD, 1)
        message[tile * LANES : (tile + 1) * LANES, :] = block
    at = iota((8, LANES), 0)
    tail = jnp.where(at == s.pairs, label, 0.0)
    for pair in range(s.pairs):
        tail = tail + jnp.where(at == pair, total[:, pair * LANES : (pair + 1) * LANES], 0.0)
    message[s.tiles * LANES :, :] = tail


def join_messages(place, messages, state_low, first, have_first, earlier):
    s = place.s
    tail_at = s.tiles * LANES
    label = jnp.where(have_first, messages[first, tail_at + s.pairs : tail_at + s.pairs + 1, :], -1.0)

    def one(step, carry):
        block, tail = carry
        counts = (place.row - step >= 0) if earlier else (place.row - step < 0)
        here = messages[step, tail_at + s.pairs : tail_at + s.pairs + 1, :]
        weight = jnp.where(counts, (here == label).astype(WIDE), 0.0)
        return (
            block + messages[step, 0:tail_at, :] * weight,
            tail + messages[step, tail_at : tail_at + 8, :] * weight,
        )

    start = (jnp.zeros((tail_at, LANES), WIDE), jnp.zeros((8, LANES), WIDE))
    block, tail = lax.fori_loop(1, s.rows, one, start)
    same = same_head()
    state_low[...] = jnp.zeros_like(state_low)
    for tile in range(s.tiles):
        part = block[tile * LANES : (tile + 1) * LANES]
        first_at = 2 * tile * LANES
        state_low[first_at : first_at + LANES, first_at : first_at + LANES] = jnp.where(same, part, 0.0).astype(LOW)
        if 2 * tile + 1 < s.pairs:
            at = first_at + LANES
            more = pltpu.roll(jnp.where(same, 0.0, part), HEAD, 1)
            state_low[at : at + LANES, at : at + LANES] = more.astype(LOW)
    total = jnp.concatenate([tail[pair : pair + 1] for pair in range(s.pairs)], axis=1)
    return total, label[:, 0:1]


def send_messages(place, messages, send, receive):
    for step in range(1, place.s.rows):
        remote(
            messages.at[0], messages.at[step], send.at[step], receive.at[step], place.along_rows(step)
        ).start()


def take_messages(place, messages, send, receive):
    for step in range(1, place.s.rows):
        copy = remote(messages.at[0], messages.at[step], send.at[step], receive.at[step], place.along_rows(step))
        copy.wait()


def block_mask(s, labels_down, labels_across, i, j, turned):
    shape = (s.chunk, s.chunk)
    down, across = iota(shape, 0), iota(shape, 1)
    if turned:
        ordered = (i * s.chunk + across) >= (j * s.chunk + down)
        equal = labels_down[chunk_rows(s, j), :] == labels_across[i]
    else:
        ordered = (i * s.chunk + down) >= (j * s.chunk + across)
        equal = labels_down[chunk_rows(s, i), :] == labels_across[j]
    return jnp.where(ordered & equal, 1.0, 0.0)


def chunk_rows(s, k):
    return pl.ds(pl.multiple_of(k * s.chunk, s.chunk), s.chunk)


def forward_kernel(
    s,
    pixels,
    labels_down,
    labels_across,
    first_gain,
    query_weight,
    key_weight,
    value_weight,
    out_weight,
    second_gain,
    up_weight,
    down_weight,
    cotangent,
    normed,
    query_feature,
    key_feature,
    values,
    attended,
    denominator,
    key_sum,
    hidden_low,
    hidden_share,
    gradient_share,
    pixel_share,
    gain_part,
    prefix_low,
    latest,
    middle,
    wide_gradient,
    gathered,
    weight_wide,
    weight_full,
    joined,
    hidden,
    normed_again,
    upward_low,
    low_wide,
    parts,
    near,
    far,
    messages,
    state,
    total,
    ones,
    staging,
    weight_send,
    weight_recv,
    att_send,
    att_recv,
    low_send,
    low_recv,
    message_send,
    message_recv,
    near_send,
    near_recv,
    far_send,
    far_recv,
    staging_sem,
):
    p = Place(s)
    weight_wide[p.head, 0] = out_weight[...].astype(WIDE)
    p.meet()
    weights = Gather(p, lambda g, k: weight_wide.at[g, k], weight_send, weight_recv)
    weights.start(0)

    last = labels_across[s.chunks - 1][:, s.chunk - 1 : s.chunk]
    state[...] = jnp.zeros_like(state)
    total[...] = jnp.zeros_like(total)
    ones[...] = block_ones(s.width)

    @pl.loop(0, s.chunks)
    def _(k):
        at = chunk_rows(s, k)
        unit, scale = normalise(pixels[k].reshape(s.chunk, s.model).astype(WIDE))
        low = (unit * first_gain[...]).astype(LOW)
        normed[at, :] = low
        for weight, out in ((query_weight, query_feature), (key_weight, key_feature)):
            raw = dot(low, weight[...])
            out[at, :] = jnp.where(raw > 0, raw + 1.0, jnp.exp(jnp.minimum(raw, 0.0))).astype(LOW)
        values[at, :] = dot(low, value_weight[...]).astype(LOW)
        ending = (labels_down[at, :] == last).astype(WIDE)
        kept = key_feature[at, :].astype(WIDE) * ending
        state[...] += dot_left(kept.astype(LOW), values[at, :])
        total[0:1, :] += jnp.sum(kept, axis=0, keepdims=True)

    write_message(s, messages.at[0], state, total[0:1, :], last)
    send_messages(p, messages, message_send, message_recv)

    @pl.loop(0, s.chunks)
    def _(i):
        at = chunk_rows(s, i)
        attended[at, :] = jnp.zeros((s.chunk, s.width), WIDE)
        key_sum[at, :] = jnp.zeros((s.chunk, s.width), WIDE)

        def over(j, carry):
            to = chunk_rows(s, j)
            mask = block_mask(s, labels_down, labels_across, i, j, False)
            key_sum[at, :] += dot(mask.astype(LOW), key_feature[to, :])
            numerator = attended[at, :]
            for head in range(s.here):
                lanes = head_lanes(s.width, head)
                scores = dot_right(only(query_feature[at, :], lanes), key_feature[to, :])
                numerator = numerator + dot((scores * mask).astype(LOW), only(values[to, :], lanes))
            attended[at, :] = numerator
            return carry

        lax.fori_loop(0, i + 1, over, 0)

    take_messages(p, messages, message_send, message_recv)
    prefix_total, label = join_messages(p, messages, prefix_low, 1, p.row > 0, True)
    latest[...] = jnp.broadcast_to(label, latest.shape)

    attention = Gather(p, lambda g, k: gathered.at[g, k], att_send, att_recv)

    @pl.loop(0, s.chunks)
    def _(i):
        at = chunk_rows(s, i)
        matching = (labels_down[at, :] == latest[0:1, 0:1]).astype(WIDE)
        query = query_feature[at, :].astype(WIDE)
        numerator = attended[at, :] + dot((query * matching).astype(LOW), prefix_low[...])
        sums = key_sum[at, :] + matching * prefix_total
        key_sum[at, :] = sums
        below = over_heads(query * sums, ones[...])
        denominator[at, :] = below
        value = numerator / below
        attended[at, :] = value
        gathered[p.head, i] = value.astype(LOW).astype(WIDE)
        attention.start(i)

    weights.forward(0)
    attention.forward(0)
    weights.finish(0)
    weights.sent(0)
    for group in range(s.heads):
        weight_full[group * s.width : (group + 1) * s.width, :] = weight_wide[group, 0].astype(LOW)

    hidden_gather = Gather(p, lambda g, k: low_wide.at[k, lax.rem(g, 2), g // 2], low_send, low_recv)
    reduced = Reduce(p, parts, near, far, (near_send, near_recv, far_send, far_recv))
    gain_part[...] = jnp.zeros_like(gain_part)

    def feed_forward(k):
        at = chunk_rows(s, k)
        attention.finish(k)
        for group in range(s.heads):
            joined[:, group * s.width : (group + 1) * s.width] = gathered[group, k].astype(LOW)
        shares = (2, s.ny, s.sub, TILE)
        for tile in range(s.model // TILE):
            cols = slice(tile * TILE, (tile + 1) * TILE)
            product = dot(joined[...], weight_full[:, cols])
            hidden[:, :, :, cols] = product.reshape(shares) + pixels[k, :, :, :, cols].astype(WIDE)
        hidden_share[k] = hidden[p.c, p.y]
        unit, scale = normalise(hidden[...].reshape(s.chunk, s.model))
        normed_again[at, :] = (unit * second_gain[...]).astype(LOW)

        @pl.when(k + 1 < s.chunks)
        def _():
            attention.forward(k + 1)

        low = normed_again[at, :]
        back = cotangent[k].reshape(s.chunk, s.model)
        for tile in range(s.units // TILE):
            cols = slice(tile * TILE, (tile + 1) * TILE)
            upward = dot(low, up_weight[:, cols])
            middle_back = dot_right(back, down_weight[cols, :])
            root = math.sqrt(2.0 / math.pi)
            square = upward * upward
            bent = jnp.tanh(root * upward * (1.0 + 0.044715 * square))
            half = 0.5 + 0.5 * bent
            slope = half + 0.5 * upward * (1.0 - bent * bent) * (root * (1.0 + 3.0 * 0.044715 * square))
            middle[at, cols] = (upward * half).astype(LOW)
            upward_low[at, cols] = (middle_back * slope).astype(LOW)
        low = upward_low[at, :]
        for tile in range(s.model // TILE):
            cols = slice(tile * TILE, (tile + 1) * TILE)
            parts[k, :, :, :, cols] = dot_right(low, up_weight[cols, :]).reshape(shares)
        reduced.start(k)

    def second_norm_back(k):
        grad = reduced.total(k)
        unit, scale = normalise(hidden_share[k])
        gain_part[0:1, :] += jnp.sum(grad * unit, axis=0, keepdims=True)
        part = normalise_back(unit, scale, second_gain[...], grad)
        value = cotangent[k, p.c, p.y].astype(WIDE) + part
        gradient_share[k] = value
        low_wide[k, p.c, p.y] = value.astype(LOW).astype(WIDE)
        hidden_gather.start(k)

    def staged(piece, job):
        return pltpu.make_async_copy(staging.at[job], wide_gradient.at[job, piece], staging_sem.at[job])

    def outer(job, left, right):
        for piece in range(s.nz):
            block = left(slice(piece * s.model // s.nz, (piece + 1) * s.model // s.nz))
            if piece > 0:
                staged(piece - 1, job).wait()
            for tile in range(s.units // TILE):
                cols = slice(tile * TILE, (tile + 1) * TILE)
                staging[job, :, :, cols] = dot_left(block, right[:, cols]).reshape(s.nx, s.cut, TILE)
            staged(piece, job).start()

    @pl.loop(0, s.chunks + 3)
    def _(k):
        @pl.when(k < s.chunks)
        def _():
            feed_forward(k)

        @pl.when((k >= 1) & (k <= s.chunks))
        def _():
            reduced.middle(k - 1)

        @pl.when(k == s.chunks)
        def _():
            outer(0, lambda cols: normed_again[:, cols], upward_low)

        @pl.when((k >= 2) & (k <= s.chunks + 1))
        def _():
            second_norm_back(k - 2)

        @pl.when(k == s.chunks + 1)
        def _():
            outer(1, lambda cols: cotangent_rows(s, cotangent, cols), middle)

        @pl.when((k >= 3) & (k <= s.chunks + 2))
        def _():
            hidden_gather.forward(k - 3)

    for k in range(s.chunks):
        pixel_share[k] = pixels[k, p.c, p.y]
        hidden_gather.finish(k)
        hidden_low[k * s.chunk : (k + 1) * s.chunk, :] = low_wide[k].reshape(s.chunk, s.model).astype(LOW)
    for job in range(2):
        staged(s.nz - 1, job).wait()
    for k in range(s.chunks):
        attention.sent(k)
        hidden_gather.sent(k)
        reduced.near_sent(k)
        reduced.far_sent(k)


def cotangent_rows(s, cotangent, cols):
    return cotangent[:, :, :, :, cols].reshape(s.tokens, cols.stop - cols.start)


class Scatter:
    def __init__(self, place, source, near, far, sems):
        self.p, self.source, self.near, self.far = place, source, near, far
        self.near_send, self.near_recv, self.far_send, self.far_recv = sems

    def piece(self, turn):
        return lax.rem(self.p.z + turn + 1, self.p.s.nz)

    def near_copy(self, turn, step):
        to = lax.rem(self.p.x + step, self.p.s.nx)
        return remote(
            self.source.at[self.piece(turn), to],
            self.near.at[step - 1, turn],
            self.near_send.at[step - 1, turn],
            self.near_recv.at[step - 1, turn],
            self.p.along_x(step),
        )

    def far_copy(self, turn):
        return remote(
            self.near.at[0, turn],
            self.far.at[turn],
            self.far_send.at[turn],
            self.far_recv.at[turn],
            self.p.along_z(turn + 1),
        )

    def start(self, turn):
        for step in range(1, self.p.s.nx):
            self.near_copy(turn, step).start()

    def middle(self, turn, own):
        value = own
        for step in range(1, self.p.s.nx):
            self.near_copy(turn, step).wait_recv()
            value = value + self.near[step - 1, turn]
        self.near[0, turn] = value
        if turn < self.p.s.nz - 1:
            self.far_copy(turn).start()

    def total(self):
        value = self.near[0, self.p.s.nz - 1]
        for turn in range(self.p.s.nz - 1):
            self.far_copy(turn).wait_recv()
            value = value + self.far[turn]
        return value

    def sent(self):
        for turn in range(self.p.s.nz):
            for step in range(1, self.p.s.nx):
                self.near_copy(turn, step).wait_send()
        for turn in range(self.p.s.nz - 1):
            self.far_copy(turn).wait_send()


def backward_kernel(
    s,
    labels_down,
    labels_across,
    normed,
    query_feature,
    key_feature,
    values,
    attended,
    denominator,
    key_sum,
    hidden_low,
    hidden_share,
    gradient_share,
    pixel_share,
    gain_part,
    prefix_low,
    latest,
    middle,
    down_weight,
    query_weight,
    key_weight,
    value_weight,
    out_weight,
    first_gain,
    wide_gradient,
    result,
    gains,
    up_out,
    down_out,
    narrow_out,
    pixel_gradient,
    result_wide,
    parts,
    near_two,
    far_two,
    near_four,
    far_four,
    result_own,
    pixel_own,
    numerator_low,
    denominator_back,
    spread_back,
    query_back,
    key_back,
    value_back,
    narrow_low,
    suffix_low,
    state,
    total,
    ones,
    messages,
    narrow_gradient,
    own_wide,
    near_up,
    far_up,
    near_down,
    far_down,
    near_narrow,
    far_narrow,
    gain_heads,
    gain_x,
    gain_z,
    message_send,
    message_recv,
    two_near_send,
    two_near_recv,
    two_far_send,
    two_far_recv,
    four_near_send,
    four_near_recv,
    four_far_send,
    four_far_recv,
    result_send,
    result_recv,
    pixel_send,
    pixel_recv,
    scatter_near_send,
    scatter_near_recv,
    scatter_far_send,
    scatter_far_recv,
    gain_send,
    gain_recv,
    own_sem,
    result_sem,
    pixel_sem,
    read_sem,
):
    p = Place(s)
    p.meet()

    def scatter(job, source, near, far):
        sems = (
            scatter_near_send.at[job],
            scatter_near_recv.at[job],
            scatter_far_send.at[job],
            scatter_far_recv.at[job],
        )
        return Scatter(p, source, near, far, sems)

    up = scatter(0, wide_gradient.at[0], near_up, far_up)
    down = scatter(1, wide_gradient.at[1], near_down, far_down)
    narrow = scatter(2, narrow_gradient, near_narrow, far_narrow)
    for job in (up, down):
        for turn in range(s.nz):
            job.start(turn)

    wide_jobs = (up, down)

    def own_load(at):
        job, turn = at // s.nz, at % s.nz
        source = wide_gradient.at[job, wide_jobs[job].piece(turn), p.x]
        return pltpu.make_async_copy(source, own_wide.at[at % 2], own_sem.at[at % 2])

    def wide_middle(at):
        own_load(at).wait()
        wide_jobs[at // s.nz].middle(at % s.nz, own_wide[at % 2])
        if at + 2 < 2 * s.nz:
            own_load(at + 2).start()

    own_load(0).start()
    own_load(1).start()
    two = Reduce(p, parts, near_two, far_two, (two_near_send, two_near_recv, two_far_send, two_far_recv))
    four = Reduce(p, parts, near_four, far_four, (four_near_send, four_near_recv, four_far_send, four_far_recv))
    result_gather = Gather(
        p,
        lambda g, k: result_wide.at[k, lax.rem(g, 2), g // 2],
        result_send,
        result_recv,
        lambda k: result_own.at[k],
    )
    pixel_gather = Gather(
        p,
        lambda g, k: pixel_gradient.at[k, lax.rem(g, 2), g // 2],
        pixel_send,
        pixel_recv,
        lambda k: pixel_own.at[k],
    )
    shares = (2, s.ny, s.sub, TILE)

    @pl.loop(0, s.chunks)
    def _(k):
        low = middle[chunk_rows(s, k), :]
        for tile in range(s.model // TILE):
            cols = slice(tile * TILE, (tile + 1) * TILE)
            parts[k, :, :, :, cols] = dot(low, down_weight[:, cols]).reshape(shares)
        two.start(k)

    first = labels_across[0][:, 0:1]
    state[...] = jnp.zeros_like(state)
    total[...] = jnp.zeros_like(total)
    ones[...] = block_ones(s.width)

    @pl.loop(0, s.chunks)
    def _(k):
        at = chunk_rows(s, k)
        back = dot_right(hidden_low[at, :], out_weight[...])
        below = denominator[at, :]
        low = (back / below).astype(LOW)
        numerator_low[at, :] = low
        slope = -over_heads(back * attended[at, :], ones[...]) / below
        denominator_back[at, :] = slope
        query = query_feature[at, :].astype(WIDE)
        spread = slope * query
        spread_back[at, :] = spread.astype(LOW)
        leading = (labels_down[at, :] == first).astype(WIDE)
        state[...] += dot_left((query * leading).astype(LOW), low)
        total[0:1, :] += jnp.sum(spread * leading, axis=0, keepdims=True)

    write_message(s, messages.at[0], state, total[0:1, :], first)
    send_messages(p, messages, message_send, message_recv)

    @pl.loop(0, s.chunks)
    def _(k):
        two.middle(k)

    wide_middle(0)

    @pl.loop(0, s.chunks)
    def _(i):
        at = chunk_rows(s, i)
        query_back[at, :] = denominator_back[at, :] * key_sum[at, :]

        def over(j, carry):
            to = chunk_rows(s, j)
            mask = block_mask(s, labels_down, labels_across, i, j, False)
            value = query_back[at, :]
            for head in range(s.here):
                lanes = head_lanes(s.width, head)
                scores = dot_right(only(numerator_low[at, :], lanes), values[to, :])
                value = value + dot((scores * mask).astype(LOW), only(key_feature[to, :], lanes))
            query_back[at, :] = value
            return carry

        lax.fori_loop(0, i + 1, over, 0)

    wide_middle(1)

    @pl.loop(0, s.chunks)
    def _(j):
        to = chunk_rows(s, j)
        key_back[to, :] = jnp.zeros((s.chunk, s.width), WIDE)
        value_back[to, :] = jnp.zeros((s.chunk, s.width), WIDE)

        def over(i, carry):
            at = chunk_rows(s, i)
            mask = block_mask(s, labels_down, labels_across, i, j, True)
            key_value = key_back[to, :] + dot(mask.astype(LOW), spread_back[at, :])
            value_value = value_back[to, :]
            for head in range(s.here):
                lanes = head_lanes(s.width, head)
                back = dot_right(only(values[to, :], lanes), numerator_low[at, :])
                key_value = key_value + dot((back * mask).astype(LOW), only(query_feature[at, :], lanes))
                scores = dot_right(only(key_feature[to, :], lanes), query_feature[at, :])
                value_value = value_value + dot((scores * mask).astype(LOW), only(numerator_low[at, :], lanes))
            key_back[to, :] = key_value
            value_back[to, :] = value_value
            return carry

        lax.fori_loop(j, s.chunks, over, 0)

    @pl.loop(0, s.chunks)
    def _(k):
        result_own[k] = (hidden_share[k] + two.total(k)).astype(LOW).astype(WIDE)
        result_gather.start(k)

    take_messages(p, messages, message_send, message_recv)
    suffix_total, label = join_messages(p, messages, suffix_low, s.rows - 1, p.row < s.rows - 1, False)
    following = label

    @pl.loop(0, s.chunks)
    def _(k):
        at = chunk_rows(s, k)
        matching = (labels_down[at, :] == latest[0:1, 0:1]).astype(WIDE)
        later = (labels_down[at, :] == following).astype(WIDE)
        query, key = query_feature[at, :], key_feature[at, :]
        value = query_back[at, :] + matching * dot_right(numerator_low[at, :], prefix_low[...])
        low = (value * jnp.minimum(query.astype(WIDE), 1.0)).astype(LOW)
        numerator_value = value_back[at, :] + later * dot(key, suffix_low[...])
        key_value = key_back[at, :] + later * (dot_right(values[at, :], suffix_low[...]) + suffix_total)
        key_low = (key_value * jnp.minimum(key.astype(WIDE), 1.0)).astype(LOW)
        value_low = numerator_value.astype(LOW)
        narrow_low[0, at, :] = low
        narrow_low[1, at, :] = key_low
        narrow_low[2, at, :] = value_low
        two.near_sent(k)
        for tile in range(s.model // TILE):
            cols = slice(tile * TILE, (tile + 1) * TILE)
            product = (
                dot_right(low, query_weight[cols, :])
                + dot_right(key_low, key_weight[cols, :])
                + dot_right(value_low, value_weight[cols, :])
            )
            parts[k, :, :, :, cols] = product.reshape(shares)
        four.start(k)

    wide_middle(2)
    span = s.nx * s.cut
    for piece in range(s.nz):
        cols = slice(piece * span, (piece + 1) * span)
        shape = (s.nx, s.cut, s.width)
        product = dot_left(hidden_low[:, cols], attended[...].astype(LOW))
        narrow_gradient[piece, :, :, 0 : s.width] = product.reshape(shape)
        for part in range(3):
            product = dot_left(normed[:, cols], narrow_low[part])
            narrow_gradient[piece, :, :, (part + 1) * s.width : (part + 2) * s.width] = product.reshape(shape)
    for turn in range(s.nz):
        narrow.start(turn)

    @pl.loop(0, s.chunks)
    def _(k):
        four.middle(k)

    for at in range(3, s.nz):
        wide_middle(at)
    gain_heads[0] = gain_part[...]

    def result_local(k):
        return pltpu.make_async_copy(result_own.at[k], result_wide.at[k, p.c, p.y], result_sem.at[k])

    def pixel_local(k):
        return pltpu.make_async_copy(pixel_own.at[k], pixel_gradient.at[k, p.c, p.y], pixel_sem.at[k])

    def result_read(k):
        return pltpu.make_async_copy(result_wide.at[k], parts.at[k], read_sem.at[k])

    @pl.loop(0, s.chunks)
    def _(k):
        grad = four.total(k)
        unit, scale = normalise(pixel_share[k].astype(WIDE))
        gain_heads[0, 1:2, :] += jnp.sum(grad * unit, axis=0, keepdims=True)
        pixel_own[k] = gradient_share[k] + normalise_back(unit, scale, first_gain[...], grad)
        pixel_gather.start(k)
        pixel_local(k).start()
        result_local(k).start()

    wide_middle(s.nz)

    def gain_round(buffer, device, index):
        copies = []
        for step in range(1, buffer.shape[0]):
            copy = remote(
                buffer.at[0], buffer.at[step], gain_send.at[index, step], gain_recv.at[index, step], device(step)
            )
            copy.start()
            copies.append(copy)
        for copy in copies:
            copy.wait()
        value = buffer[0]
        for step in range(1, buffer.shape[0]):
            value = value + buffer[step]
        return value

    gain_x[0] = gain_round(gain_heads, p.along_heads, 0)
    gain_z[0] = gain_round(gain_x, p.along_x, 1)
    gains[...] = gain_round(gain_z, p.along_z, 2)

    for at in range(s.nz + 1, 2 * s.nz):
        wide_middle(at)
    for k in range(s.chunks):
        result_gather.forward(k)
    for k in range(s.chunks):
        pixel_gather.forward(k)
    for k in range(s.chunks):
        result_gather.finish(k)
        result_local(k).wait()
        four.near_sent(k)
        result_read(k).start()
    for k in range(s.chunks):
        result_read(k).wait()
        result[k * s.chunk : (k + 1) * s.chunk, :] = parts[k].reshape(s.chunk, s.model).astype(LOW)
    up_out[...] = up.total()
    for turn in range(s.nz):
        narrow.middle(turn, narrow_gradient[narrow.piece(turn), p.x])
    down_out[...] = down.total()
    for k in range(s.chunks):
        pixel_gather.finish(k)
        pixel_local(k).wait()
        pixel_gather.sent(k)
        result_gather.sent(k)
        two.far_sent(k)
        four.far_sent(k)
    narrow_out[...] = narrow.total()
    for job in (up, down, narrow):
        job.sent()


def vmem(count):
    return [pl.BlockSpec(memory_space=pltpu.VMEM)] * count


def dma(*shape):
    return pltpu.SemaphoreType.DMA(shape)


def on_device(
    rows,
    heads,
    pixels,
    crop_ids,
    first_gain,
    query_weight,
    key_weight,
    value_weight,
    out_weight,
    second_gain,
    up_weight,
    down_weight,
    cotangent,
):
    tokens, model = pixels.shape
    s = Sizes(rows, heads, tokens, model, query_weight.shape[1], up_weight.shape[1])
    whole = (s.chunks, 2, s.ny, s.sub, model)
    share = (s.chunks, s.sub, model)
    labels = crop_ids.astype(WIDE)
    labels_down = labels.reshape(tokens, 1)
    labels_across = labels.reshape(s.chunks, 1, s.chunk)
    shape = jax.ShapeDtypeStruct
    any_space = pl.BlockSpec(memory_space=pl.ANY)

    def reduce_sems():
        return [
            dma(s.chunks),
            dma(s.chunks),
            dma(s.ny - 1, s.chunks),
            dma(s.ny - 1, s.chunks),
        ]

    def gather_sems(count):
        return [dma(2 * s.ny - 1, count), dma(heads, count)]

    outs = [
        shape((tokens, model), LOW),
        shape((tokens, s.width), LOW),
        shape((tokens, s.width), LOW),
        shape((tokens, s.width), LOW),
        shape((tokens, s.width), WIDE),
        shape((tokens, s.width), WIDE),
        shape((tokens, s.width), WIDE),
        shape((tokens, model), LOW),
        shape(share, WIDE),
        shape(share, WIDE),
        shape(share, LOW),
        shape((8, model), WIDE),
        shape((s.width, s.width), LOW),
        shape((8, LANES), WIDE),
        shape((tokens, s.units), LOW),
        shape((2, s.nz, s.nx, s.cut, s.units), WIDE),
    ]
    (
        normed,
        query_feature,
        key_feature,
        values,
        attended,
        denominator,
        key_sum,
        hidden_low,
        hidden_share,
        gradient_share,
        pixel_share,
        gain_part,
        prefix_low,
        latest,
        middle,
        wide_gradient,
    ) = pl.pallas_call(
        functools.partial(forward_kernel, s),
        out_shape=outs,
        in_specs=vmem(12),
        out_specs=vmem(15) + [any_space],
        scratch_shapes=[
            pltpu.VMEM((heads, s.chunks, s.chunk, s.width), WIDE),
            pltpu.VMEM((heads, 1, s.width, model), WIDE),
            pltpu.VMEM((model, model), LOW),
            pltpu.VMEM((s.chunk, model), LOW),
            pltpu.VMEM(whole[1:], WIDE),
            pltpu.VMEM((tokens, model), LOW),
            pltpu.VMEM((tokens, s.units), LOW),
            pltpu.VMEM(whole, WIDE),
            pltpu.VMEM(whole, WIDE),
            pltpu.VMEM((s.chunks, s.ny, s.sub, model), WIDE),
            pltpu.VMEM((s.ny - 1,) + share, WIDE),
            pltpu.VMEM((rows, s.message, LANES), WIDE),
            pltpu.VMEM((s.width, s.width), WIDE),
            pltpu.VMEM((8, s.width), WIDE),
            pltpu.VMEM((s.width, s.width), LOW),
            pltpu.VMEM((2, s.nx, s.cut, s.units), WIDE),
            *gather_sems(1),
            *gather_sems(s.chunks),
            *gather_sems(s.chunks),
            dma(rows),
            dma(rows),
            *reduce_sems(),
            dma(2),
        ],
        compiler_params=pltpu.CompilerParams(
            collective_id=0, has_side_effects=True, vmem_limit_bytes=60 << 20
        ),
        name="forward_part",
    )(
        pixels.reshape(whole),
        labels_down,
        labels_across,
        first_gain.reshape(1, model),
        query_weight,
        key_weight,
        value_weight,
        out_weight,
        second_gain.reshape(1, model),
        up_weight,
        down_weight,
        cotangent.reshape(whole),
    )
    columns = 4 * s.width
    outs = [
        shape((tokens, model), LOW),
        shape((8, model), WIDE),
        shape((s.cut, s.units), WIDE),
        shape((s.cut, s.units), WIDE),
        shape((s.cut, columns), WIDE),
        shape(whole, WIDE),
        shape(whole, WIDE),
    ]

    def scatter_buffers(width):
        return [
            pltpu.VMEM((s.nx - 1, s.nz, s.cut, width), WIDE),
            pltpu.VMEM((s.nz - 1, s.cut, width), WIDE),
        ]

    def reduce_buffers():
        return [
            pltpu.VMEM((s.chunks, s.ny, s.sub, model), WIDE),
            pltpu.VMEM((s.ny - 1,) + share, WIDE),
        ]

    result, gains, up_out, down_out, narrow_out, pixel_gradient, unused = pl.pallas_call(
        functools.partial(backward_kernel, s),
        out_shape=outs,
        in_specs=vmem(23) + [any_space],
        out_specs=vmem(5) + [any_space] * 2,
        scratch_shapes=[
            pltpu.VMEM(whole, WIDE),
            *reduce_buffers(),
            *reduce_buffers(),
            pltpu.VMEM(share, WIDE),
            pltpu.VMEM(share, WIDE),
            pltpu.VMEM((tokens, s.width), LOW),
            pltpu.VMEM((tokens, s.width), WIDE),
            pltpu.VMEM((tokens, s.width), LOW),
            pltpu.VMEM((tokens, s.width), WIDE),
            pltpu.VMEM((tokens, s.width), WIDE),
            pltpu.VMEM((tokens, s.width), WIDE),
            pltpu.VMEM((3, tokens, s.width), LOW),
            pltpu.VMEM((s.width, s.width), LOW),
            pltpu.VMEM((s.width, s.width), WIDE),
            pltpu.VMEM((8, s.width), WIDE),
            pltpu.VMEM((s.width, s.width), LOW),
            pltpu.VMEM((rows, s.message, LANES), WIDE),
            pltpu.VMEM((s.nz, s.nx, s.cut, columns), WIDE),
            pltpu.VMEM((2, s.cut, s.units), WIDE),
            *scatter_buffers(s.units),
            *scatter_buffers(s.units),
            *scatter_buffers(columns),
            pltpu.VMEM((heads, 8, model), WIDE),
            pltpu.VMEM((s.nx, 8, model), WIDE),
            pltpu.VMEM((s.nz, 8, model), WIDE),
            dma(rows),
            dma(rows),
            *reduce_sems(),
            *reduce_sems(),
            *gather_sems(s.chunks),
            *gather_sems(s.chunks),
            dma(3, s.nx - 1, s.nz),
            dma(3, s.nx - 1, s.nz),
            dma(3, s.nz - 1),
            dma(3, s.nz - 1),
            dma(3, max(heads, s.nx, s.nz)),
            dma(3, max(heads, s.nx, s.nz)),
            dma(2),
            dma(s.chunks),
            dma(s.chunks),
            dma(s.chunks),
        ],
        compiler_params=pltpu.CompilerParams(
            collective_id=1, has_side_effects=True, vmem_limit_bytes=60 << 20
        ),
        name="backward_part",
    )(
        labels_down,
        labels_across,
        normed,
        query_feature,
        key_feature,
        values,
        attended,
        denominator,
        key_sum,
        hidden_low,
        hidden_share,
        gradient_share,
        pixel_share,
        gain_part,
        prefix_low,
        latest,
        middle,
        down_weight,
        query_weight,
        key_weight,
        value_weight,
        out_weight,
        first_gain.reshape(1, model),
        wide_gradient,
    )
    start = lax.axis_index("rows") * s.cut
    second_part, first_part = (lax.dynamic_slice(gains[i], (start,), (s.cut,)) for i in range(2))
    narrow = [narrow_out[:, i * s.width : (i + 1) * s.width] for i in range(4)]
    return (
        result,
        pixel_gradient.reshape(tokens, model),
        first_part,
        narrow[1],
        narrow[2],
        narrow[3],
        narrow[0].T,
        second_part,
        up_out,
        down_out.T,
    )


def solution(mesh):
    return jax.shard_map(
        functools.partial(on_device, mesh.shape["rows"], mesh.shape["heads"]),
        mesh=mesh,
        in_specs=(
            P("rows", None),
            P("rows"),
            P(),
            P(None, "heads"),
            P(None, "heads"),
            P(None, "heads"),
            P("heads", None),
            P(),
            P(None, "heads"),
            P("heads", None),
            P("rows", None),
        ),
        out_specs=(
            P("rows", None),
            P("rows", None),
            P("rows"),
            P("rows", "heads"),
            P("rows", "heads"),
            P("rows", "heads"),
            P("heads", "rows"),
            P("rows"),
            P("rows", "heads"),
            P("heads", "rows"),
        ),
        check_vma=False,
    )
```

```python
import functools
import math

import jax
import jax.numpy as jnp
from jax import lax
from jax.experimental import pallas as pl
from jax.experimental.pallas import tpu as pltpu
from jax.sharding import PartitionSpec as P

HEAD = 64
EPSILON = 1e-05
MESH = pl.DeviceIdType.MESH
LOW = jnp.bfloat16
WIDE = jnp.float32
LANES = 128
TILE = 256
AHEAD = 3


def dot(left, right):
    return jnp.dot(left, right, preferred_element_type=WIDE)


def dot_left(left, right):
    return lax.dot_general(left, right, (((0,), (0,)), ((), ())), preferred_element_type=WIDE)


def dot_right(left, right):
    return lax.dot_general(left, right, (((1,), (1,)), ((), ())), preferred_element_type=WIDE)


def normalise(value):
    middle = jnp.mean(value, axis=-1, keepdims=True)
    centred = value - middle
    spread = jnp.mean(centred * centred, axis=-1, keepdims=True)
    scale = lax.rsqrt(spread + EPSILON)
    return centred * scale, scale


def normalise_back(unit, scale, gain, grad):
    scaled = grad * gain
    along = jnp.mean(scaled * unit, axis=-1, keepdims=True)
    return scale * (scaled - jnp.mean(scaled, axis=-1, keepdims=True) - unit * along)


class Sizes:
    def __init__(self, rows, heads, tokens, model, width, units):
        self.rows, self.heads = rows, heads
        self.ny = heads // 2
        self.nx = self.ny if rows % self.ny == 0 else 1
        self.nz = rows // self.nx
        self.tokens, self.model, self.width, self.units = tokens, model, width, units
        self.chunk = min(TILE, tokens)
        self.chunks = tokens // self.chunk
        self.sub = self.chunk // heads
        self.here = width // HEAD
        self.pairs = width // LANES
        self.tiles = (self.pairs + 1) // 2
        self.message = self.tiles * LANES + 8
        self.cut = model // rows


class Place:
    def __init__(self, sizes):
        s = self.s = sizes
        self.row = lax.axis_index("rows")
        self.head = lax.axis_index("heads")
        self.y, self.c = self.head // 2, lax.rem(self.head, 2)
        self.x, self.z = lax.rem(self.row, s.nx), self.row // s.nx

    def other(self):
        return (self.row, self.y * 2 + 1 - self.c)

    def group(self, step):
        return lax.rem(self.y + self.s.ny - step, self.s.ny) * 2 + self.c

    def along_y(self, step):
        return (self.row, lax.rem(self.y + step, self.s.ny) * 2 + self.c)

    def along_x(self, step):
        return (self.z * self.s.nx + lax.rem(self.x + step, self.s.nx), self.head)

    def along_z(self, step):
        return (lax.rem(self.z + step, self.s.nz) * self.s.nx + self.x, self.head)

    def along_rows(self, step):
        return (lax.rem(self.row + step, self.s.rows), self.head)

    def along_heads(self, step):
        return (self.row, lax.rem(self.head + step, self.s.heads))

    def meet(self):
        barrier = pltpu.get_barrier_semaphore()
        for step in range(1, self.s.heads):
            pl.semaphore_signal(barrier, inc=1, device_id=self.along_heads(step), device_id_type=MESH)
        for step in range(1, self.s.rows):
            pl.semaphore_signal(barrier, inc=1, device_id=self.along_rows(step), device_id_type=MESH)
        pl.semaphore_wait(barrier, self.s.heads + self.s.rows - 2)


def remote(source, target, send, receive, device):
    return pltpu.make_async_remote_copy(
        src_ref=source, dst_ref=target, send_sem=send, recv_sem=receive, device_id=device, device_id_type=MESH
    )


class Gather:
    def __init__(self, place, view, send, receive, own=None):
        self.p, self.view, self.send, self.receive = place, view, send, receive
        self.own = own

    def copy(self, group, k, slot, device):
        source = self.view(group, k)
        return remote(source, self.view(group, k), self.send.at[slot, k], self.receive.at[group, k], device)

    def own_copy(self, k, slot, device):
        group = self.p.head
        source = self.view(group, k) if self.own is None else self.own(k)
        return remote(source, self.view(group, k), self.send.at[slot, k], self.receive.at[group, k], device)

    def start(self, k):
        for step in range(1, self.p.s.ny):
            self.own_copy(k, step, self.p.along_y(step)).start()
        self.own_copy(k, 0, self.p.other()).start()

    def forward(self, k):
        ny = self.p.s.ny
        for step in range(1, ny):
            group = self.p.group(step)
            self.copy(group, k, 0, self.p.along_y(step)).wait_recv()
            self.copy(group, k, ny - 1 + step, self.p.other()).start()

    def finish(self, k):
        for step in range(self.p.s.ny):
            own = self.p.group(step)
            group = own + 1 - 2 * self.p.c
            self.copy(group, k, 0, self.p.other()).wait_recv()

    def sent(self, k):
        ny = self.p.s.ny
        for step in range(ny):
            self.own_copy(k, step, self.p.other()).wait_send()
        for step in range(1, ny):
            self.copy(self.p.group(step), k, ny - 1 + step, self.p.other()).wait_send()


class Reduce:
    def __init__(self, place, parts, near, far, sems):
        self.p, self.parts, self.near, self.far = place, parts, near, far
        self.near_send, self.near_recv, self.far_send, self.far_recv = sems

    def near_copy(self, k):
        return remote(
            self.parts.at[k, 1 - self.p.c],
            self.near.at[k],
            self.near_send.at[k],
            self.near_recv.at[k],
            self.p.other(),
        )

    def far_copy(self, k, step):
        share = lax.rem(self.p.y + step, self.p.s.ny)
        return remote(
            self.near.at[k, share],
            self.far.at[step - 1, k],
            self.far_send.at[step - 1, k],
            self.far_recv.at[step - 1, k],
            self.p.along_y(step),
        )

    def start(self, k):
        self.near_copy(k).start()

    def middle(self, k):
        self.near_copy(k).wait_recv()
        for step in range(self.p.s.ny):
            share = lax.rem(self.p.y + self.p.s.ny - 1 - step, self.p.s.ny)
            self.near[k, share] = self.near[k, share] + self.parts[k, self.p.c, share]
        for step in range(1, self.p.s.ny):
            self.far_copy(k, step).start()

    def total(self, k):
        value = self.near[k, self.p.y]
        for step in range(1, self.p.s.ny):
            self.far_copy(k, step).wait_recv()
            value = value + self.far[step - 1, k]
        return value

    def near_sent(self, k):
        self.near_copy(k).wait_send()

    def far_sent(self, k):
        for step in range(1, self.p.s.ny):
            self.far_copy(k, step).wait_send()


def iota(shape, axis):
    return lax.broadcasted_iota(jnp.int32, shape, axis)


def head_lanes(width, head):
    lanes = iota((1, width), 1) // HEAD
    return (lanes == head).astype(WIDE)


def only(value, lanes):
    return (value.astype(WIDE) * lanes).astype(LOW)


def block_ones(width):
    return (iota((width, width), 0) // HEAD == iota((width, width), 1) // HEAD).astype(WIDE).astype(LOW)


def over_heads(product, ones):
    high = product.astype(LOW)
    rest = (product - high.astype(WIDE)).astype(LOW)
    return dot(high, ones) + dot(rest, ones)


def same_head():
    return iota((LANES, LANES), 0) // HEAD == iota((LANES, LANES), 1) // HEAD


def write_message(s, message, state, total, label):
    same = same_head()
    for tile in range(s.tiles):
        first = 2 * tile * LANES
        block = jnp.where(same, state[first : first + LANES, first : first + LANES], 0.0)
        if 2 * tile + 1 < s.pairs:
            second = first + LANES
            more = jnp.where(same, state[second : second + LANES, second : second + LANES], 0.0)
            block = block + pltpu.roll(more, HEAD, 1)
        message[tile * LANES : (tile + 1) * LANES, :] = block
    at = iota((8, LANES), 0)
    tail = jnp.where(at == s.pairs, label, 0.0)
    for pair in range(s.pairs):
        tail = tail + jnp.where(at == pair, total[:, pair * LANES : (pair + 1) * LANES], 0.0)
    message[s.tiles * LANES :, :] = tail


def join_messages(place, messages, state_low, first, have_first, earlier):
    s = place.s
    tail_at = s.tiles * LANES
    label = jnp.where(have_first, messages[first, tail_at + s.pairs : tail_at + s.pairs + 1, :], -1.0)

    def one(step, carry):
        block, tail = carry
        counts = (place.row - step >= 0) if earlier else (place.row - step < 0)
        here = messages[step, tail_at + s.pairs : tail_at + s.pairs + 1, :]
        weight = jnp.where(counts, (here == label).astype(WIDE), 0.0)
        return (
            block + messages[step, 0:tail_at, :] * weight,
            tail + messages[step, tail_at : tail_at + 8, :] * weight,
        )

    start = (jnp.zeros((tail_at, LANES), WIDE), jnp.zeros((8, LANES), WIDE))
    block, tail = lax.fori_loop(1, s.rows, one, start)
    same = same_head()
    state_low[...] = jnp.zeros_like(state_low)
    for tile in range(s.tiles):
        part = block[tile * LANES : (tile + 1) * LANES]
        first_at = 2 * tile * LANES
        state_low[first_at : first_at + LANES, first_at : first_at + LANES] = jnp.where(same, part, 0.0).astype(LOW)
        if 2 * tile + 1 < s.pairs:
            at = first_at + LANES
            more = pltpu.roll(jnp.where(same, 0.0, part), HEAD, 1)
            state_low[at : at + LANES, at : at + LANES] = more.astype(LOW)
    total = jnp.concatenate([tail[pair : pair + 1] for pair in range(s.pairs)], axis=1)
    return total, label[:, 0:1]


def send_messages(place, messages, send, receive):
    for step in range(1, place.s.rows):
        remote(
            messages.at[0], messages.at[step], send.at[step], receive.at[step], place.along_rows(step)
        ).start()


def take_messages(place, messages, send, receive):
    for step in range(1, place.s.rows):
        copy = remote(messages.at[0], messages.at[step], send.at[step], receive.at[step], place.along_rows(step))
        copy.wait()


def block_mask(s, labels_down, labels_across, i, j, turned):
    shape = (s.chunk, s.chunk)
    down, across = iota(shape, 0), iota(shape, 1)
    if turned:
        ordered = (i * s.chunk + across) >= (j * s.chunk + down)
        equal = labels_down[chunk_rows(s, j), :] == labels_across[i]
    else:
        ordered = (i * s.chunk + down) >= (j * s.chunk + across)
        equal = labels_down[chunk_rows(s, i), :] == labels_across[j]
    return jnp.where(ordered & equal, 1.0, 0.0)


def chunk_rows(s, k):
    return pl.ds(pl.multiple_of(k * s.chunk, s.chunk), s.chunk)


def forward_kernel(
    s,
    pixels,
    labels_down,
    labels_across,
    first_gain,
    query_weight,
    key_weight,
    value_weight,
    out_weight,
    second_gain,
    up_weight,
    down_weight,
    cotangent,
    normed,
    query_feature,
    key_feature,
    values,
    attended,
    denominator,
    key_sum,
    hidden_low,
    hidden_share,
    gradient_share,
    pixel_share,
    gain_part,
    prefix_low,
    latest,
    middle,
    wide_gradient,
    gathered,
    weight_wide,
    weight_full,
    joined,
    hidden,
    normed_again,
    upward_low,
    low_wide,
    parts,
    near,
    far,
    messages,
    state,
    total,
    ones,
    staging,
    weight_send,
    weight_recv,
    att_send,
    att_recv,
    low_send,
    low_recv,
    message_send,
    message_recv,
    near_send,
    near_recv,
    far_send,
    far_recv,
    staging_sem,
):
    p = Place(s)
    weight_wide[p.head, 0] = out_weight[...].astype(WIDE)
    p.meet()
    weights = Gather(p, lambda g, k: weight_wide.at[g, k], weight_send, weight_recv)
    weights.start(0)

    last = labels_across[s.chunks - 1][:, s.chunk - 1 : s.chunk]
    state[...] = jnp.zeros_like(state)
    total[...] = jnp.zeros_like(total)
    ones[...] = block_ones(s.width)

    @pl.loop(0, s.chunks)
    def _(k):
        at = chunk_rows(s, k)
        unit, scale = normalise(pixels[k].reshape(s.chunk, s.model).astype(WIDE))
        low = (unit * first_gain[...]).astype(LOW)
        normed[at, :] = low
        for weight, out in ((query_weight, query_feature), (key_weight, key_feature)):
            raw = dot(low, weight[...])
            out[at, :] = jnp.where(raw > 0, raw + 1.0, jnp.exp(jnp.minimum(raw, 0.0))).astype(LOW)
        values[at, :] = dot(low, value_weight[...]).astype(LOW)
        ending = (labels_down[at, :] == last).astype(WIDE)
        kept = key_feature[at, :].astype(WIDE) * ending
        state[...] += dot_left(kept.astype(LOW), values[at, :])
        total[0:1, :] += jnp.sum(kept, axis=0, keepdims=True)

    write_message(s, messages.at[0], state, total[0:1, :], last)
    send_messages(p, messages, message_send, message_recv)

    @pl.loop(0, s.chunks)
    def _(i):
        at = chunk_rows(s, i)
        attended[at, :] = jnp.zeros((s.chunk, s.width), WIDE)
        key_sum[at, :] = jnp.zeros((s.chunk, s.width), WIDE)

        def over(j, carry):
            to = chunk_rows(s, j)
            mask = block_mask(s, labels_down, labels_across, i, j, False)
            key_sum[at, :] += dot(mask.astype(LOW), key_feature[to, :])
            numerator = attended[at, :]
            for head in range(s.here):
                lanes = head_lanes(s.width, head)
                scores = dot_right(only(query_feature[at, :], lanes), key_feature[to, :])
                numerator = numerator + dot((scores * mask).astype(LOW), only(values[to, :], lanes))
            attended[at, :] = numerator
            return carry

        lax.fori_loop(0, i + 1, over, 0)

    take_messages(p, messages, message_send, message_recv)
    prefix_total, label = join_messages(p, messages, prefix_low, 1, p.row > 0, True)
    latest[...] = jnp.broadcast_to(label, latest.shape)

    attention = Gather(p, lambda g, k: gathered.at[g, k], att_send, att_recv)

    @pl.loop(0, s.chunks)
    def _(i):
        at = chunk_rows(s, i)
        matching = (labels_down[at, :] == latest[0:1, 0:1]).astype(WIDE)
        query = query_feature[at, :].astype(WIDE)
        numerator = attended[at, :] + dot((query * matching).astype(LOW), prefix_low[...])
        sums = key_sum[at, :] + matching * prefix_total
        key_sum[at, :] = sums
        below = over_heads(query * sums, ones[...])
        denominator[at, :] = below
        value = numerator / below
        attended[at, :] = value
        gathered[p.head, i] = value.astype(LOW).astype(WIDE)
        attention.start(i)

    weights.forward(0)
    attention.forward(0)
    weights.finish(0)
    weights.sent(0)
    for group in range(s.heads):
        weight_full[group * s.width : (group + 1) * s.width, :] = weight_wide[group, 0].astype(LOW)

    hidden_gather = Gather(p, lambda g, k: low_wide.at[k, lax.rem(g, 2), g // 2], low_send, low_recv)
    reduced = Reduce(p, parts, near, far, (near_send, near_recv, far_send, far_recv))
    gain_part[...] = jnp.zeros_like(gain_part)

    def feed_forward(k):
        at = chunk_rows(s, k)
        attention.finish(k)
        for group in range(s.heads):
            joined[:, group * s.width : (group + 1) * s.width] = gathered[group, k].astype(LOW)
        shares = (2, s.ny, s.sub, TILE)
        for tile in range(s.model // TILE):
            cols = slice(tile * TILE, (tile + 1) * TILE)
            product = dot(joined[...], weight_full[:, cols])
            hidden[:, :, :, cols] = product.reshape(shares) + pixels[k, :, :, :, cols].astype(WIDE)
        hidden_share[k] = hidden[p.c, p.y]
        unit, scale = normalise(hidden[...].reshape(s.chunk, s.model))
        normed_again[at, :] = (unit * second_gain[...]).astype(LOW)

        @pl.when(k + 1 < s.chunks)
        def _():
            attention.forward(k + 1)

        low = normed_again[at, :]
        back = cotangent[k].reshape(s.chunk, s.model)
        for tile in range(s.units // TILE):
            cols = slice(tile * TILE, (tile + 1) * TILE)
            upward = dot(low, up_weight[:, cols])
            middle_back = dot_right(back, down_weight[cols, :])
            root = math.sqrt(2.0 / math.pi)
            square = upward * upward
            bent = jnp.tanh(root * upward * (1.0 + 0.044715 * square))
            half = 0.5 + 0.5 * bent
            slope = half + 0.5 * upward * (1.0 - bent * bent) * (root * (1.0 + 3.0 * 0.044715 * square))
            middle[at, cols] = (upward * half).astype(LOW)
            upward_low[at, cols] = (middle_back * slope).astype(LOW)
        low = upward_low[at, :]
        for tile in range(s.model // TILE):
            cols = slice(tile * TILE, (tile + 1) * TILE)
            parts[k, :, :, :, cols] = dot_right(low, up_weight[cols, :]).reshape(shares)
        reduced.start(k)

    def second_norm_back(k):
        grad = reduced.total(k)
        unit, scale = normalise(hidden_share[k])
        gain_part[0:1, :] += jnp.sum(grad * unit, axis=0, keepdims=True)
        part = normalise_back(unit, scale, second_gain[...], grad)
        value = cotangent[k, p.c, p.y].astype(WIDE) + part
        gradient_share[k] = value
        low_wide[k, p.c, p.y] = value.astype(LOW).astype(WIDE)
        hidden_gather.start(k)

    def staged(piece, job):
        return pltpu.make_async_copy(staging.at[job], wide_gradient.at[job, piece], staging_sem.at[job])

    def outer(job, left, right):
        for piece in range(s.nz):
            block = left(slice(piece * s.model // s.nz, (piece + 1) * s.model // s.nz))
            if piece > 0:
                staged(piece - 1, job).wait()
            for tile in range(s.units // TILE):
                cols = slice(tile * TILE, (tile + 1) * TILE)
                staging[job, :, :, cols] = dot_left(block, right[:, cols]).reshape(s.nx, s.cut, TILE)
            staged(piece, job).start()

    @pl.loop(0, s.chunks + 3)
    def _(k):
        @pl.when(k < s.chunks)
        def _():
            feed_forward(k)

        @pl.when((k >= 1) & (k <= s.chunks))
        def _():
            reduced.middle(k - 1)

        @pl.when(k == s.chunks)
        def _():
            outer(0, lambda cols: normed_again[:, cols], upward_low)

        @pl.when((k >= 2) & (k <= s.chunks + 1))
        def _():
            second_norm_back(k - 2)

        @pl.when(k == s.chunks + 1)
        def _():
            outer(1, lambda cols: cotangent_rows(s, cotangent, cols), middle)

        @pl.when((k >= 3) & (k <= s.chunks + 2))
        def _():
            hidden_gather.forward(k - 3)

    for k in range(s.chunks):
        pixel_share[k] = pixels[k, p.c, p.y]
        hidden_gather.finish(k)
        hidden_low[k * s.chunk : (k + 1) * s.chunk, :] = low_wide[k].reshape(s.chunk, s.model).astype(LOW)
    for job in range(2):
        staged(s.nz - 1, job).wait()
    for k in range(s.chunks):
        attention.sent(k)
        hidden_gather.sent(k)
        reduced.near_sent(k)
        reduced.far_sent(k)


def cotangent_rows(s, cotangent, cols):
    return cotangent[:, :, :, :, cols].reshape(s.tokens, cols.stop - cols.start)


class Scatter:
    def __init__(self, place, source, near, far, sems):
        self.p, self.source, self.near, self.far = place, source, near, far
        self.near_send, self.near_recv, self.far_send, self.far_recv = sems

    def piece(self, turn):
        return lax.rem(self.p.z + turn + 1, self.p.s.nz)

    def near_copy(self, turn, step):
        to = lax.rem(self.p.x + step, self.p.s.nx)
        return remote(
            self.source.at[self.piece(turn), to],
            self.near.at[step - 1, turn],
            self.near_send.at[step - 1, turn],
            self.near_recv.at[step - 1, turn],
            self.p.along_x(step),
        )

    def far_copy(self, turn):
        return remote(
            self.near.at[0, turn],
            self.far.at[turn],
            self.far_send.at[turn],
            self.far_recv.at[turn],
            self.p.along_z(turn + 1),
        )

    def start(self, turn):
        for step in range(1, self.p.s.nx):
            self.near_copy(turn, step).start()

    def middle(self, turn, own):
        value = own
        for step in range(1, self.p.s.nx):
            self.near_copy(turn, step).wait_recv()
            value = value + self.near[step - 1, turn]
        self.near[0, turn] = value
        if turn < self.p.s.nz - 1:
            self.far_copy(turn).start()

    def total(self):
        value = self.near[0, self.p.s.nz - 1]
        for turn in range(self.p.s.nz - 1):
            self.far_copy(turn).wait_recv()
            value = value + self.far[turn]
        return value

    def sent(self):
        for turn in range(self.p.s.nz):
            for step in range(1, self.p.s.nx):
                self.near_copy(turn, step).wait_send()
        for turn in range(self.p.s.nz - 1):
            self.far_copy(turn).wait_send()


def backward_kernel(
    s,
    labels_down,
    labels_across,
    normed,
    query_feature,
    key_feature,
    values,
    attended,
    denominator,
    key_sum,
    hidden_low,
    hidden_share,
    gradient_share,
    pixel_share,
    gain_part,
    prefix_low,
    latest,
    middle,
    down_weight,
    query_weight,
    key_weight,
    value_weight,
    out_weight,
    first_gain,
    wide_gradient,
    result,
    gains,
    up_out,
    down_out,
    narrow_out,
    pixel_gradient,
    result_wide,
    parts,
    near_two,
    far_two,
    near_four,
    far_four,
    result_own,
    pixel_own,
    numerator_low,
    denominator_back,
    spread_back,
    query_back,
    key_back,
    value_back,
    narrow_low,
    suffix_low,
    state,
    total,
    ones,
    messages,
    narrow_gradient,
    own_wide,
    near_up,
    far_up,
    near_down,
    far_down,
    near_narrow,
    far_narrow,
    gain_heads,
    gain_x,
    gain_z,
    message_send,
    message_recv,
    two_near_send,
    two_near_recv,
    two_far_send,
    two_far_recv,
    four_near_send,
    four_near_recv,
    four_far_send,
    four_far_recv,
    result_send,
    result_recv,
    pixel_send,
    pixel_recv,
    scatter_near_send,
    scatter_near_recv,
    scatter_far_send,
    scatter_far_recv,
    gain_send,
    gain_recv,
    own_sem,
    result_sem,
    pixel_sem,
    read_sem,
):
    p = Place(s)
    p.meet()

    def scatter(job, source, near, far):
        sems = (
            scatter_near_send.at[job],
            scatter_near_recv.at[job],
            scatter_far_send.at[job],
            scatter_far_recv.at[job],
        )
        return Scatter(p, source, near, far, sems)

    up = scatter(0, wide_gradient.at[0], near_up, far_up)
    down = scatter(1, wide_gradient.at[1], near_down, far_down)
    narrow = scatter(2, narrow_gradient, near_narrow, far_narrow)
    jobs = (up, down, narrow)
    wide = 2 * s.nz
    flight = {"next": 0, "ready": wide}

    def push(limit):
        while flight["next"] <= limit and flight["next"] < flight["ready"]:
            at = flight["next"]
            jobs[at // s.nz].start(at % s.nz)
            flight["next"] = at + 1

    def own_load(at):
        job, turn = at // s.nz, at % s.nz
        source = wide_gradient.at[job, jobs[job].piece(turn), p.x]
        return pltpu.make_async_copy(source, own_wide.at[at % 2], own_sem.at[at % 2])

    def take(at):
        job, turn = at // s.nz, at % s.nz
        if at < wide:
            own_load(at).wait()
            jobs[job].middle(turn, own_wide[at % 2])
        else:
            narrow.middle(turn, narrow_gradient[narrow.piece(turn), p.x])
        if at + 2 < wide:
            own_load(at + 2).start()
        push(at + AHEAD)

    push(0)
    own_load(0).start()
    own_load(1).start()
    two = Reduce(p, parts, near_two, far_two, (two_near_send, two_near_recv, two_far_send, two_far_recv))
    four = Reduce(p, parts, near_four, far_four, (four_near_send, four_near_recv, four_far_send, four_far_recv))
    result_gather = Gather(
        p,
        lambda g, k: result_wide.at[k, lax.rem(g, 2), g // 2],
        result_send,
        result_recv,
        lambda k: result_own.at[k],
    )
    pixel_gather = Gather(
        p,
        lambda g, k: pixel_gradient.at[k, lax.rem(g, 2), g // 2],
        pixel_send,
        pixel_recv,
        lambda k: pixel_own.at[k],
    )
    shares = (2, s.ny, s.sub, TILE)

    first = labels_across[0][:, 0:1]
    state[...] = jnp.zeros_like(state)
    total[...] = jnp.zeros_like(total)
    ones[...] = block_ones(s.width)

    @pl.loop(0, s.chunks)
    def _(k):
        at = chunk_rows(s, k)
        back = dot_right(hidden_low[at, :], out_weight[...])
        below = denominator[at, :]
        low = (back / below).astype(LOW)
        numerator_low[at, :] = low
        slope = -over_heads(back * attended[at, :], ones[...]) / below
        denominator_back[at, :] = slope
        query = query_feature[at, :].astype(WIDE)
        spread = slope * query
        spread_back[at, :] = spread.astype(LOW)
        leading = (labels_down[at, :] == first).astype(WIDE)
        state[...] += dot_left((query * leading).astype(LOW), low)
        total[0:1, :] += jnp.sum(spread * leading, axis=0, keepdims=True)

    write_message(s, messages.at[0], state, total[0:1, :], first)
    send_messages(p, messages, message_send, message_recv)
    push(AHEAD - 1)

    @pl.loop(0, s.chunks)
    def _(k):
        low = middle[chunk_rows(s, k), :]
        for tile in range(s.model // TILE):
            cols = slice(tile * TILE, (tile + 1) * TILE)
            parts[k, :, :, :, cols] = dot(low, down_weight[:, cols]).reshape(shares)
        two.start(k)

    @pl.loop(0, s.chunks)
    def _(k):
        two.middle(k)

    take(0)

    @pl.loop(0, s.chunks)
    def _(i):
        at = chunk_rows(s, i)
        query_back[at, :] = denominator_back[at, :] * key_sum[at, :]

        def over(j, carry):
            to = chunk_rows(s, j)
            mask = block_mask(s, labels_down, labels_across, i, j, False)
            value = query_back[at, :]
            for head in range(s.here):
                lanes = head_lanes(s.width, head)
                scores = dot_right(only(numerator_low[at, :], lanes), values[to, :])
                value = value + dot((scores * mask).astype(LOW), only(key_feature[to, :], lanes))
            query_back[at, :] = value
            return carry

        lax.fori_loop(0, i + 1, over, 0)

    take(1)

    @pl.loop(0, s.chunks)
    def _(j):
        to = chunk_rows(s, j)
        key_back[to, :] = jnp.zeros((s.chunk, s.width), WIDE)
        value_back[to, :] = jnp.zeros((s.chunk, s.width), WIDE)

        def over(i, carry):
            at = chunk_rows(s, i)
            mask = block_mask(s, labels_down, labels_across, i, j, True)
            key_value = key_back[to, :] + dot(mask.astype(LOW), spread_back[at, :])
            value_value = value_back[to, :]
            for head in range(s.here):
                lanes = head_lanes(s.width, head)
                back = dot_right(only(values[to, :], lanes), numerator_low[at, :])
                key_value = key_value + dot((back * mask).astype(LOW), only(query_feature[at, :], lanes))
                scores = dot_right(only(key_feature[to, :], lanes), query_feature[at, :])
                value_value = value_value + dot((scores * mask).astype(LOW), only(numerator_low[at, :], lanes))
            key_back[to, :] = key_value
            value_back[to, :] = value_value
            return carry

        lax.fori_loop(j, s.chunks, over, 0)

    @pl.loop(0, s.chunks)
    def _(k):
        result_own[k] = (hidden_share[k] + two.total(k)).astype(LOW).astype(WIDE)
        result_gather.start(k)

    take_messages(p, messages, message_send, message_recv)
    suffix_total, label = join_messages(p, messages, suffix_low, s.rows - 1, p.row < s.rows - 1, False)
    following = label

    @pl.loop(0, s.chunks)
    def _(k):
        at = chunk_rows(s, k)
        matching = (labels_down[at, :] == latest[0:1, 0:1]).astype(WIDE)
        later = (labels_down[at, :] == following).astype(WIDE)
        query, key = query_feature[at, :], key_feature[at, :]
        value = query_back[at, :] + matching * dot_right(numerator_low[at, :], prefix_low[...])
        low = (value * jnp.minimum(query.astype(WIDE), 1.0)).astype(LOW)
        numerator_value = value_back[at, :] + later * dot(key, suffix_low[...])
        key_value = key_back[at, :] + later * (dot_right(values[at, :], suffix_low[...]) + suffix_total)
        key_low = (key_value * jnp.minimum(key.astype(WIDE), 1.0)).astype(LOW)
        value_low = numerator_value.astype(LOW)
        narrow_low[0, at, :] = low
        narrow_low[1, at, :] = key_low
        narrow_low[2, at, :] = value_low
        two.near_sent(k)
        for tile in range(s.model // TILE):
            cols = slice(tile * TILE, (tile + 1) * TILE)
            product = (
                dot_right(low, query_weight[cols, :])
                + dot_right(key_low, key_weight[cols, :])
                + dot_right(value_low, value_weight[cols, :])
            )
            parts[k, :, :, :, cols] = product.reshape(shares)
        four.start(k)


    @pl.loop(0, s.chunks)
    def _(k):
        four.middle(k)

    take(2)
    span = s.nx * s.cut
    for piece in range(s.nz):
        cols = slice(piece * span, (piece + 1) * span)
        shape = (s.nx, s.cut, s.width)
        product = dot_left(hidden_low[:, cols], attended[...].astype(LOW))
        narrow_gradient[piece, :, :, 0 : s.width] = product.reshape(shape)
        for part in range(3):
            product = dot_left(normed[:, cols], narrow_low[part])
            narrow_gradient[piece, :, :, (part + 1) * s.width : (part + 2) * s.width] = product.reshape(shape)
    flight["ready"] = 3 * s.nz
    rest = list(range(3, 3 * s.nz))

    def take_some(count):
        for at in rest[:count]:
            take(at)
        del rest[:count]

    def take_until_left(count):
        take_some(max(0, len(rest) - count))

    take_until_left(7)
    gain_heads[0] = gain_part[...]

    def result_local(k):
        return pltpu.make_async_copy(result_own.at[k], result_wide.at[k, p.c, p.y], result_sem.at[k])

    def pixel_local(k):
        return pltpu.make_async_copy(pixel_own.at[k], pixel_gradient.at[k, p.c, p.y], pixel_sem.at[k])

    def result_read(k):
        return pltpu.make_async_copy(result_wide.at[k], parts.at[k], read_sem.at[k])

    @pl.loop(0, s.chunks)
    def _(k):
        grad = four.total(k)
        unit, scale = normalise(pixel_share[k].astype(WIDE))
        gain_heads[0, 1:2, :] += jnp.sum(grad * unit, axis=0, keepdims=True)
        pixel_own[k] = gradient_share[k] + normalise_back(unit, scale, first_gain[...], grad)
        pixel_gather.start(k)
        pixel_local(k).start()
        result_local(k).start()

    def gain_copies(index, buffer, device):
        return [
            remote(buffer.at[0], buffer.at[step], gain_send.at[index, step], gain_recv.at[index, step], device(step))
            for step in range(1, buffer.shape[0])
        ]

    def gain_start(*what):
        for copy in gain_copies(*what):
            copy.start()

    def gain_total(*what):
        for copy in gain_copies(*what):
            copy.wait()
        value = what[1][0]
        for step in range(1, what[1].shape[0]):
            value = value + what[1][step]
        return value

    rounds = (
        (0, gain_heads, p.along_heads),
        (1, gain_x, p.along_x),
        (2, gain_z, p.along_z),
    )
    gain_start(*rounds[0])
    take_until_left(5)
    for k in range(s.chunks):
        result_gather.forward(k)
    gain_x[0] = gain_total(*rounds[0])
    gain_start(*rounds[1])
    take_until_left(4)
    for k in range(s.chunks):
        pixel_gather.forward(k)
    take_until_left(3)
    gain_z[0] = gain_total(*rounds[1])
    gain_start(*rounds[2])
    for k in range(s.chunks):
        result_gather.finish(k)
        result_local(k).wait()
        four.near_sent(k)
        result_read(k).start()
    for k in range(s.chunks):
        result_read(k).wait()
        result[k * s.chunk : (k + 1) * s.chunk, :] = parts[k].reshape(s.chunk, s.model).astype(LOW)
    take_until_left(2)
    up_out[...] = up.total()
    gains[...] = gain_total(*rounds[2])
    take_until_left(1)
    for k in range(s.chunks):
        pixel_gather.finish(k)
        pixel_local(k).wait()
        pixel_gather.sent(k)
        result_gather.sent(k)
        two.far_sent(k)
        four.far_sent(k)
    take_until_left(0)
    down_out[...] = down.total()
    narrow_out[...] = narrow.total()
    for job in jobs:
        job.sent()


def vmem(count):
    return [pl.BlockSpec(memory_space=pltpu.VMEM)] * count


def dma(*shape):
    return pltpu.SemaphoreType.DMA(shape)


def on_device(
    rows,
    heads,
    pixels,
    crop_ids,
    first_gain,
    query_weight,
    key_weight,
    value_weight,
    out_weight,
    second_gain,
    up_weight,
    down_weight,
    cotangent,
):
    tokens, model = pixels.shape
    s = Sizes(rows, heads, tokens, model, query_weight.shape[1], up_weight.shape[1])
    whole = (s.chunks, 2, s.ny, s.sub, model)
    share = (s.chunks, s.sub, model)
    labels = crop_ids.astype(WIDE)
    labels_down = labels.reshape(tokens, 1)
    labels_across = labels.reshape(s.chunks, 1, s.chunk)
    shape = jax.ShapeDtypeStruct
    any_space = pl.BlockSpec(memory_space=pl.ANY)

    def reduce_sems():
        return [
            dma(s.chunks),
            dma(s.chunks),
            dma(s.ny - 1, s.chunks),
            dma(s.ny - 1, s.chunks),
        ]

    def gather_sems(count):
        return [dma(2 * s.ny - 1, count), dma(heads, count)]

    outs = [
        shape((tokens, model), LOW),
        shape((tokens, s.width), LOW),
        shape((tokens, s.width), LOW),
        shape((tokens, s.width), LOW),
        shape((tokens, s.width), WIDE),
        shape((tokens, s.width), WIDE),
        shape((tokens, s.width), WIDE),
        shape((tokens, model), LOW),
        shape(share, WIDE),
        shape(share, WIDE),
        shape(share, LOW),
        shape((8, model), WIDE),
        shape((s.width, s.width), LOW),
        shape((8, LANES), WIDE),
        shape((tokens, s.units), LOW),
        shape((2, s.nz, s.nx, s.cut, s.units), WIDE),
    ]
    (
        normed,
        query_feature,
        key_feature,
        values,
        attended,
        denominator,
        key_sum,
        hidden_low,
        hidden_share,
        gradient_share,
        pixel_share,
        gain_part,
        prefix_low,
        latest,
        middle,
        wide_gradient,
    ) = pl.pallas_call(
        functools.partial(forward_kernel, s),
        out_shape=outs,
        in_specs=vmem(12),
        out_specs=vmem(15) + [any_space],
        scratch_shapes=[
            pltpu.VMEM((heads, s.chunks, s.chunk, s.width), WIDE),
            pltpu.VMEM((heads, 1, s.width, model), WIDE),
            pltpu.VMEM((model, model), LOW),
            pltpu.VMEM((s.chunk, model), LOW),
            pltpu.VMEM(whole[1:], WIDE),
            pltpu.VMEM((tokens, model), LOW),
            pltpu.VMEM((tokens, s.units), LOW),
            pltpu.VMEM(whole, WIDE),
            pltpu.VMEM(whole, WIDE),
            pltpu.VMEM((s.chunks, s.ny, s.sub, model), WIDE),
            pltpu.VMEM((s.ny - 1,) + share, WIDE),
            pltpu.VMEM((rows, s.message, LANES), WIDE),
            pltpu.VMEM((s.width, s.width), WIDE),
            pltpu.VMEM((8, s.width), WIDE),
            pltpu.VMEM((s.width, s.width), LOW),
            pltpu.VMEM((2, s.nx, s.cut, s.units), WIDE),
            *gather_sems(1),
            *gather_sems(s.chunks),
            *gather_sems(s.chunks),
            dma(rows),
            dma(rows),
            *reduce_sems(),
            dma(2),
        ],
        compiler_params=pltpu.CompilerParams(
            collective_id=0, has_side_effects=True, vmem_limit_bytes=60 << 20
        ),
        name="forward_part",
    )(
        pixels.reshape(whole),
        labels_down,
        labels_across,
        first_gain.reshape(1, model),
        query_weight,
        key_weight,
        value_weight,
        out_weight,
        second_gain.reshape(1, model),
        up_weight,
        down_weight,
        cotangent.reshape(whole),
    )
    columns = 4 * s.width
    outs = [
        shape((tokens, model), LOW),
        shape((8, model), WIDE),
        shape((s.cut, s.units), WIDE),
        shape((s.cut, s.units), WIDE),
        shape((s.cut, columns), WIDE),
        shape(whole, WIDE),
        shape(whole, WIDE),
    ]

    def scatter_buffers(width):
        return [
            pltpu.VMEM((s.nx - 1, s.nz, s.cut, width), WIDE),
            pltpu.VMEM((s.nz - 1, s.cut, width), WIDE),
        ]

    def reduce_buffers():
        return [
            pltpu.VMEM((s.chunks, s.ny, s.sub, model), WIDE),
            pltpu.VMEM((s.ny - 1,) + share, WIDE),
        ]

    result, gains, up_out, down_out, narrow_out, pixel_gradient, unused = pl.pallas_call(
        functools.partial(backward_kernel, s),
        out_shape=outs,
        in_specs=vmem(23) + [any_space],
        out_specs=vmem(5) + [any_space] * 2,
        scratch_shapes=[
            pltpu.VMEM(whole, WIDE),
            *reduce_buffers(),
            *reduce_buffers(),
            pltpu.VMEM(share, WIDE),
            pltpu.VMEM(share, WIDE),
            pltpu.VMEM((tokens, s.width), LOW),
            pltpu.VMEM((tokens, s.width), WIDE),
            pltpu.VMEM((tokens, s.width), LOW),
            pltpu.VMEM((tokens, s.width), WIDE),
            pltpu.VMEM((tokens, s.width), WIDE),
            pltpu.VMEM((tokens, s.width), WIDE),
            pltpu.VMEM((3, tokens, s.width), LOW),
            pltpu.VMEM((s.width, s.width), LOW),
            pltpu.VMEM((s.width, s.width), WIDE),
            pltpu.VMEM((8, s.width), WIDE),
            pltpu.VMEM((s.width, s.width), LOW),
            pltpu.VMEM((rows, s.message, LANES), WIDE),
            pltpu.VMEM((s.nz, s.nx, s.cut, columns), WIDE),
            pltpu.VMEM((2, s.cut, s.units), WIDE),
            *scatter_buffers(s.units),
            *scatter_buffers(s.units),
            *scatter_buffers(columns),
            pltpu.VMEM((heads, 8, model), WIDE),
            pltpu.VMEM((s.nx, 8, model), WIDE),
            pltpu.VMEM((s.nz, 8, model), WIDE),
            dma(rows),
            dma(rows),
            *reduce_sems(),
            *reduce_sems(),
            *gather_sems(s.chunks),
            *gather_sems(s.chunks),
            dma(3, s.nx - 1, s.nz),
            dma(3, s.nx - 1, s.nz),
            dma(3, s.nz - 1),
            dma(3, s.nz - 1),
            dma(3, max(heads, s.nx, s.nz)),
            dma(3, max(heads, s.nx, s.nz)),
            dma(2),
            dma(s.chunks),
            dma(s.chunks),
            dma(s.chunks),
        ],
        compiler_params=pltpu.CompilerParams(
            collective_id=1, has_side_effects=True, vmem_limit_bytes=60 << 20
        ),
        name="backward_part",
    )(
        labels_down,
        labels_across,
        normed,
        query_feature,
        key_feature,
        values,
        attended,
        denominator,
        key_sum,
        hidden_low,
        hidden_share,
        gradient_share,
        pixel_share,
        gain_part,
        prefix_low,
        latest,
        middle,
        down_weight,
        query_weight,
        key_weight,
        value_weight,
        out_weight,
        first_gain.reshape(1, model),
        wide_gradient,
    )
    start = lax.axis_index("rows") * s.cut
    second_part, first_part = (lax.dynamic_slice(gains[i], (start,), (s.cut,)) for i in range(2))
    narrow = [narrow_out[:, i * s.width : (i + 1) * s.width] for i in range(4)]
    return (
        result,
        pixel_gradient.reshape(tokens, model),
        first_part,
        narrow[1],
        narrow[2],
        narrow[3],
        narrow[0].T,
        second_part,
        up_out,
        down_out.T,
    )


def solution(mesh):
    return jax.shard_map(
        functools.partial(on_device, mesh.shape["rows"], mesh.shape["heads"]),
        mesh=mesh,
        in_specs=(
            P("rows", None),
            P("rows"),
            P(),
            P(None, "heads"),
            P(None, "heads"),
            P(None, "heads"),
            P("heads", None),
            P(),
            P(None, "heads"),
            P("heads", None),
            P("rows", None),
        ),
        out_specs=(
            P("rows", None),
            P("rows", None),
            P("rows"),
            P("rows", "heads"),
            P("rows", "heads"),
            P("rows", "heads"),
            P("heads", "rows"),
            P("rows"),
            P("rows", "heads"),
            P("heads", "rows"),
        ),
        check_vma=False,
    )
```

```python
import functools
import math

import jax
import jax.numpy as jnp
from jax import lax
from jax.experimental import pallas as pl
from jax.experimental.pallas import tpu as pltpu
from jax.sharding import PartitionSpec as P

HEAD = 64
EPSILON = 1e-05
MESH = pl.DeviceIdType.MESH
LOW = jnp.bfloat16
WIDE = jnp.float32
LANES = 128
TILE = 256
AHEAD = 2
FIRST = 4


def dot(left, right):
    return jnp.dot(left, right, preferred_element_type=WIDE)


def dot_left(left, right):
    return lax.dot_general(left, right, (((0,), (0,)), ((), ())), preferred_element_type=WIDE)


def dot_right(left, right):
    return lax.dot_general(left, right, (((1,), (1,)), ((), ())), preferred_element_type=WIDE)


def normalise(value):
    middle = jnp.mean(value, axis=-1, keepdims=True)
    centred = value - middle
    spread = jnp.mean(centred * centred, axis=-1, keepdims=True)
    scale = lax.rsqrt(spread + EPSILON)
    return centred * scale, scale


def normalise_back(unit, scale, gain, grad):
    scaled = grad * gain
    along = jnp.mean(scaled * unit, axis=-1, keepdims=True)
    return scale * (scaled - jnp.mean(scaled, axis=-1, keepdims=True) - unit * along)


class Sizes:
    def __init__(self, rows, heads, tokens, model, width, units):
        self.rows, self.heads = rows, heads
        self.ny = heads // 2
        self.nx = self.ny if rows % self.ny == 0 else 1
        self.nz = rows // self.nx
        self.tokens, self.model, self.width, self.units = tokens, model, width, units
        self.chunk = min(TILE, tokens)
        self.chunks = tokens // self.chunk
        self.sub = self.chunk // heads
        self.here = width // HEAD
        self.pairs = width // LANES
        self.tiles = (self.pairs + 1) // 2
        self.message = self.tiles * LANES + 8
        self.cut = model // rows
        self.first = units // LANES * FIRST // 8 * LANES
        self.step = TILE if self.first % TILE == 0 and units % TILE == 0 else LANES
        self.wide = 2 * units - self.first
        self.narrow = 4 * width
        self.split = round((self.wide + self.narrow) / (4 * LANES)) * LANES


class Place:
    def __init__(self, sizes):
        s = self.s = sizes
        self.row = lax.axis_index("rows")
        self.head = lax.axis_index("heads")
        self.y, self.c = self.head // 2, lax.rem(self.head, 2)
        self.x, self.z = lax.rem(self.row, s.nx), self.row // s.nx

    def other(self):
        return (self.row, self.y * 2 + 1 - self.c)

    def group(self, step):
        return lax.rem(self.y + self.s.ny - step, self.s.ny) * 2 + self.c

    def along_y(self, step):
        return (self.row, lax.rem(self.y + step, self.s.ny) * 2 + self.c)

    def along_x(self, step):
        return (self.z * self.s.nx + lax.rem(self.x + step, self.s.nx), self.head)

    def along_z(self, step):
        return (lax.rem(self.z + step, self.s.nz) * self.s.nx + self.x, self.head)

    def along_rows(self, step):
        return (lax.rem(self.row + step, self.s.rows), self.head)

    def along_heads(self, step):
        return (self.row, lax.rem(self.head + step, self.s.heads))

    def meet(self):
        barrier = pltpu.get_barrier_semaphore()
        for step in range(1, self.s.heads):
            pl.semaphore_signal(barrier, inc=1, device_id=self.along_heads(step), device_id_type=MESH)
        for step in range(1, self.s.rows):
            pl.semaphore_signal(barrier, inc=1, device_id=self.along_rows(step), device_id_type=MESH)
        pl.semaphore_wait(barrier, self.s.heads + self.s.rows - 2)


def remote(source, target, send, receive, device):
    return pltpu.make_async_remote_copy(
        src_ref=source, dst_ref=target, send_sem=send, recv_sem=receive, device_id=device, device_id_type=MESH
    )


class Gather:
    def __init__(self, place, view, send, receive, own=None):
        self.p, self.view, self.send, self.receive = place, view, send, receive
        self.own = own

    def copy(self, group, k, slot, device):
        source = self.view(group, k)
        return remote(source, self.view(group, k), self.send.at[slot, k], self.receive.at[group, k], device)

    def own_copy(self, k, slot, device):
        group = self.p.head
        source = self.view(group, k) if self.own is None else self.own(k)
        return remote(source, self.view(group, k), self.send.at[slot, k], self.receive.at[group, k], device)

    def start(self, k):
        for step in range(1, self.p.s.ny):
            self.own_copy(k, step, self.p.along_y(step)).start()
        self.own_copy(k, 0, self.p.other()).start()

    def forward(self, k):
        ny = self.p.s.ny
        for step in range(1, ny):
            group = self.p.group(step)
            self.copy(group, k, 0, self.p.along_y(step)).wait_recv()
            self.copy(group, k, ny - 1 + step, self.p.other()).start()

    def finish(self, k):
        for step in range(self.p.s.ny):
            own = self.p.group(step)
            group = own + 1 - 2 * self.p.c
            self.copy(group, k, 0, self.p.other()).wait_recv()

    def sent(self, k):
        ny = self.p.s.ny
        for step in range(ny):
            self.own_copy(k, step, self.p.other()).wait_send()
        for step in range(1, ny):
            self.copy(self.p.group(step), k, ny - 1 + step, self.p.other()).wait_send()


class WeightGather:
    halves = 2

    def __init__(self, place, rows, sems):
        self.p, self.rows = place, rows
        self.y_send, self.y_recv, self.x_send, self.x_recv, self.c_send, self.c_recv = sems
        self.size = place.s.width // (place.s.nx * self.halves)

    def share(self, group, x, half):
        start = (group * self.p.s.nx + x) * (self.size * self.halves) + half * self.size
        return self.rows.at[pl.ds(pl.multiple_of(start, self.size), self.size)]

    def slice(self, group):
        width = self.p.s.width
        return self.rows.at[pl.ds(pl.multiple_of(group * width, width), width)]

    def y_copy(self, step, half, group):
        ref = self.share(group, self.p.x, half)
        at = (step - 1, half)
        return remote(ref, ref, self.y_send.at[at], self.y_recv.at[at], self.p.along_y(step))

    def x_copy(self, step, side, half, x):
        ref = self.share(self.p.group(step), x, half)
        at = (step - 1, side - 1, half)
        return remote(ref, ref, self.x_send.at[at], self.x_recv.at[at], self.p.along_x(side))

    def c_copy(self, step, group):
        ref = self.slice(group)
        return remote(ref, ref, self.c_send.at[step], self.c_recv.at[step], self.p.other())

    def start(self):
        for half in range(self.halves):
            for step in range(1, self.p.s.ny):
                self.y_copy(step, half, self.p.head).start()
        self.c_copy(0, self.p.head).start()

    def pass_x(self, half):
        for step in range(1, self.p.s.ny):
            self.y_copy(step, half, self.p.group(step)).wait_recv()
            for side in range(1, self.p.s.nx):
                self.x_copy(step, side, half, self.p.x).start()

    def pass_core(self):
        nx = self.p.s.nx
        for step in range(1, self.p.s.ny):
            for half in range(self.halves):
                for side in range(1, nx):
                    self.x_copy(step, side, half, lax.rem(self.p.x + nx - side, nx)).wait_recv()
            self.c_copy(step, self.p.group(step)).start()

    def finish(self):
        for step in range(self.p.s.ny):
            self.c_copy(step, self.p.group(step) + 1 - 2 * self.p.c).wait_recv()

    def sent(self):
        for step in range(self.p.s.ny):
            self.c_copy(step, self.p.group(step)).wait_send()
            if step == 0:
                continue
            for half in range(self.halves):
                self.y_copy(step, half, self.p.head).wait_send()
                for side in range(1, self.p.s.nx):
                    self.x_copy(step, side, half, self.p.x).wait_send()


class Reduce:
    def __init__(self, place, parts, near, far, sems):
        self.p, self.parts, self.near, self.far = place, parts, near, far
        self.near_send, self.near_recv, self.far_send, self.far_recv = sems

    def near_copy(self, k):
        return remote(
            self.parts.at[k, 1 - self.p.c],
            self.near.at[k],
            self.near_send.at[k],
            self.near_recv.at[k],
            self.p.other(),
        )

    def far_copy(self, k, step):
        share = lax.rem(self.p.y + step, self.p.s.ny)
        return remote(
            self.near.at[k, share],
            self.far.at[step - 1, k],
            self.far_send.at[step - 1, k],
            self.far_recv.at[step - 1, k],
            self.p.along_y(step),
        )

    def start(self, k):
        self.near_copy(k).start()

    def join(self, k):
        self.near_copy(k).wait_recv()
        self.near[k] = self.near[k] + self.parts[k, self.p.c]

    def spread(self, k):
        for step in range(1, self.p.s.ny):
            self.far_copy(k, step).start()

    def middle(self, k):
        self.join(k)
        self.spread(k)

    def total(self, k, own=None):
        value = self.near[k, self.p.y] if own is None else own
        for step in range(1, self.p.s.ny):
            self.far_copy(k, step).wait_recv()
            value = value + self.far[step - 1, k]
        return value

    def near_sent(self, k):
        self.near_copy(k).wait_send()

    def far_sent(self, k):
        for step in range(1, self.p.s.ny):
            self.far_copy(k, step).wait_send()


def flipped(value, mask):
    bit = 0
    out = value
    while mask >> bit:
        if (mask >> bit) & 1:
            out = out + (1 - 2 * lax.rem(value // (1 << bit), 2)) * (1 << bit)
        bit += 1
    return out


def low_zeros(mask, count):
    return count if mask == 0 else (mask & -mask).bit_length() - 1


class Halving:
    def __init__(self, place, source, near, far, sems, pairs=None, pair_sems=None):
        self.p, self.source, self.near, self.far = place, source, near, far
        self.near_send, self.near_recv, self.far_send, self.far_recv = sems
        self.pairs, self.pair_sems = pairs, pair_sems
        self.bits = place.s.nz.bit_length() - 1
        self.first_bit = 0 if pairs is None else 1
        self.order = list(reversed(range(0, place.s.nz, 1 << self.first_bit)))
        self.odd = [m for m in reversed(range(place.s.nz)) if m % 2]

    def piece(self, m):
        return flipped(self.p.z, m)

    def to_z(self, bit):
        return (flipped(self.p.z, 1 << bit) * self.p.s.nx + self.p.x, self.p.head)

    def at(self, m):
        return m >> self.first_bit

    def pair_copy(self, m):
        send, receive = self.pair_sems
        return remote(
            self.source(self.piece(m)), self.pairs.at[m >> 1], send.at[m >> 1], receive.at[m >> 1], self.to_z(0)
        )

    def join_pair(self, m, own):
        self.pair_copy(m + 1).wait_recv()
        self.pairs[m >> 1] = self.pairs[m >> 1] + own

    def near_copy(self, m, step):
        to = lax.rem(self.p.x + step, self.p.s.nx)
        source = self.source(self.piece(m)) if self.pairs is None else self.pairs.at[m >> 1]
        at = (step - 1, self.at(m))
        return remote(
            source.at[to], self.near.at[at], self.near_send.at[at], self.near_recv.at[at], self.p.along_x(step)
        )

    def start(self, m):
        for step in range(1, self.p.s.nx):
            self.near_copy(m, step).start()

    def join(self, m, own=None):
        value = self.pairs[m >> 1, self.p.x] if own is None else own
        for step in range(1, self.p.s.nx):
            self.near_copy(m, step).wait_recv()
            value = value + self.near[step - 1, self.at(m)]
        self.near[0, self.at(m)] = value

    def far_copy(self, m, bit):
        nz = self.p.s.nz
        slot = (nz >> self.first_bit) - (nz >> bit) + (m >> (bit + 1))
        return slot, remote(
            self.near.at[0, self.at(m)], self.far.at[slot], self.far_send.at[slot], self.far_recv.at[slot], self.to_z(bit)
        )

    def settle(self, m):
        for bit in range(self.first_bit, self.bits):
            slot, copy = self.far_copy(m, bit)
            if (m >> bit) & 1:
                copy.start()
                return
            copy.wait_recv()
            self.near[0, self.at(m)] = self.near[0, self.at(m)] + self.far[slot]

    def total(self):
        return self.near[0, 0]

    def sent(self):
        if self.pairs is not None:
            for m in self.odd:
                self.pair_copy(m).wait_send()
        for m in self.order:
            for step in range(1, self.p.s.nx):
                self.near_copy(m, step).wait_send()
            if m:
                self.far_copy(m, low_zeros(m, self.bits))[1].wait_send()


def iota(shape, axis):
    return lax.broadcasted_iota(jnp.int32, shape, axis)


def head_lanes(width, head):
    lanes = iota((1, width), 1) // HEAD
    return (lanes == head).astype(WIDE)


def only(value, lanes):
    return (value.astype(WIDE) * lanes).astype(LOW)


def block_ones(width):
    return (iota((width, width), 0) // HEAD == iota((width, width), 1) // HEAD).astype(WIDE).astype(LOW)


def over_heads(product, ones):
    high = product.astype(LOW)
    rest = (product - high.astype(WIDE)).astype(LOW)
    return dot(high, ones) + dot(rest, ones)


def same_head():
    return iota((LANES, LANES), 0) // HEAD == iota((LANES, LANES), 1) // HEAD


def write_message(s, message, state, total, label):
    same = same_head()
    for tile in range(s.tiles):
        first = 2 * tile * LANES
        block = jnp.where(same, state[first : first + LANES, first : first + LANES], 0.0)
        if 2 * tile + 1 < s.pairs:
            second = first + LANES
            more = jnp.where(same, state[second : second + LANES, second : second + LANES], 0.0)
            block = block + pltpu.roll(more, HEAD, 1)
        message[tile * LANES : (tile + 1) * LANES, :] = block
    at = iota((8, LANES), 0)
    tail = jnp.where(at == s.pairs, label, 0.0)
    for pair in range(s.pairs):
        tail = tail + jnp.where(at == pair, total[:, pair * LANES : (pair + 1) * LANES], 0.0)
    message[s.tiles * LANES :, :] = tail


def join_messages(place, messages, state_low, first, have_first, earlier):
    s = place.s
    tail_at = s.tiles * LANES
    label = jnp.where(have_first, messages[first, tail_at + s.pairs : tail_at + s.pairs + 1, :], -1.0)

    def one(step, carry):
        block, tail = carry
        counts = (place.row - step >= 0) if earlier else (place.row - step < 0)
        here = messages[step, tail_at + s.pairs : tail_at + s.pairs + 1, :]
        weight = jnp.where(counts, (here == label).astype(WIDE), 0.0)
        return (
            block + messages[step, 0:tail_at, :] * weight,
            tail + messages[step, tail_at : tail_at + 8, :] * weight,
        )

    start = (jnp.zeros((tail_at, LANES), WIDE), jnp.zeros((8, LANES), WIDE))
    block, tail = lax.fori_loop(1, s.rows, one, start)
    same = same_head()
    state_low[...] = jnp.zeros_like(state_low)
    for tile in range(s.tiles):
        part = block[tile * LANES : (tile + 1) * LANES]
        first_at = 2 * tile * LANES
        state_low[first_at : first_at + LANES, first_at : first_at + LANES] = jnp.where(same, part, 0.0).astype(LOW)
        if 2 * tile + 1 < s.pairs:
            at = first_at + LANES
            more = pltpu.roll(jnp.where(same, 0.0, part), HEAD, 1)
            state_low[at : at + LANES, at : at + LANES] = more.astype(LOW)
    total = jnp.concatenate([tail[pair : pair + 1] for pair in range(s.pairs)], axis=1)
    return total, label[:, 0:1]


def send_messages(place, messages, send, receive):
    for step in range(1, place.s.rows):
        remote(
            messages.at[0], messages.at[step], send.at[step], receive.at[step], place.along_rows(step)
        ).start()


def take_messages(place, messages, send, receive):
    for step in range(1, place.s.rows):
        copy = remote(messages.at[0], messages.at[step], send.at[step], receive.at[step], place.along_rows(step))
        copy.wait()


def spread_labels(s, crop_ids, labels_across, labels_down):
    for k in range(s.chunks):
        labels = crop_ids[k].astype(WIDE)
        labels_across[k] = labels
        labels_down[k * s.chunk : (k + 1) * s.chunk, :] = jnp.broadcast_to(labels, (LANES, s.chunk)).T


def block_mask(s, labels_down, labels_across, i, j, turned):
    shape = (s.chunk, s.chunk)
    down, across = iota(shape, 0), iota(shape, 1)
    if turned:
        ordered = (i * s.chunk + across) >= (j * s.chunk + down)
        equal = labels_down[chunk_rows(s, j), 0:1] == labels_across[i]
    else:
        ordered = (i * s.chunk + down) >= (j * s.chunk + across)
        equal = labels_down[chunk_rows(s, i), 0:1] == labels_across[j]
    return jnp.where(ordered & equal, 1.0, 0.0)


def chunk_rows(s, k):
    return pl.ds(pl.multiple_of(k * s.chunk, s.chunk), s.chunk)


def forward_kernel(
    s,
    pixels,
    crop_ids,
    first_gain,
    query_weight,
    key_weight,
    value_weight,
    out_weight,
    second_gain,
    up_source,
    down_source,
    cotangent_source,
    hidden_low,
    hidden_share,
    gradient_share,
    pixel_share,
    gain_part,
    prefix_low,
    latest,
    near_two,
    first_out,
    normed_out,
    query_out,
    key_out,
    values_out,
    attended_out,
    denominator_out,
    key_sum_out,
    wide_gradient,
    normed,
    query_feature,
    key_feature,
    values,
    attended,
    denominator,
    key_sum,
    up_weight,
    down_weight,
    cotangent,
    labels_across,
    labels_down,
    gathered,
    wide_rows,
    weight_full,
    joined,
    hidden,
    normed_again,
    upward_low,
    middle,
    parts,
    near,
    far,
    messages,
    state,
    total,
    ones,
    staging,
    first_gradient,
    first_near,
    first_far,
    load_sem,
    save_sem,
    staging_sem,
    weight_y_send,
    weight_y_recv,
    weight_x_send,
    weight_x_recv,
    weight_c_send,
    weight_c_recv,
    att_send,
    att_recv,
    low_send,
    low_recv,
    message_send,
    message_recv,
    near_send,
    near_recv,
    far_send,
    far_recv,
    two_send,
    two_recv,
    first_near_send,
    first_near_recv,
    first_far_send,
    first_far_recv,
):
    p = Place(s)
    loads = [
        pltpu.make_async_copy(source, target, load_sem.at[i])
        for i, (source, target) in enumerate(
            ((up_source, up_weight), (down_source, down_weight), (cotangent_source, cotangent))
        )
    ]
    saves = [
        pltpu.make_async_copy(source, target, save_sem.at[i])
        for i, (source, target) in enumerate(
            (
                (normed, normed_out),
                (query_feature, query_out),
                (key_feature, key_out),
                (values, values_out),
                (attended, attended_out),
                (denominator, denominator_out),
                (key_sum, key_sum_out),
            )
        )
    ]
    own_rows = pl.ds(pl.multiple_of(p.head * s.width, s.width), s.width)
    wide_rows[own_rows, :] = out_weight[...].astype(WIDE)
    p.meet()
    weights = WeightGather(
        p, wide_rows, (weight_y_send, weight_y_recv, weight_x_send, weight_x_recv, weight_c_send, weight_c_recv)
    )
    weights.start()
    for load in loads:
        load.start()

    spread_labels(s, crop_ids, labels_across, labels_down)
    last = labels_across[s.chunks - 1][:, s.chunk - 1 : s.chunk]
    state[...] = jnp.zeros_like(state)
    total[...] = jnp.zeros_like(total)
    ones[...] = block_ones(s.width)

    @pl.loop(0, s.chunks)
    def _(k):
        at = chunk_rows(s, k)
        unit, scale = normalise(pixels[k].reshape(s.chunk, s.model).astype(WIDE))
        low = (unit * first_gain[...]).astype(LOW)
        normed[at, :] = low
        for weight, out in ((query_weight, query_feature), (key_weight, key_feature)):
            raw = dot(low, weight[...])
            out[at, :] = jnp.where(raw > 0, raw + 1.0, jnp.exp(jnp.minimum(raw, 0.0))).astype(LOW)
        values[at, :] = dot(low, value_weight[...]).astype(LOW)
        ending = (labels_down[at, 0:1] == last).astype(WIDE)
        kept = key_feature[at, :].astype(WIDE) * ending
        state[...] += dot_left(kept.astype(LOW), values[at, :])
        total[0:1, :] += jnp.sum(kept, axis=0, keepdims=True)

    write_message(s, messages.at[0], state, total[0:1, :], last)
    send_messages(p, messages, message_send, message_recv)
    for save in saves[:4]:
        save.start()
    weights.pass_x(0)

    @pl.loop(0, s.chunks)
    def _(i):
        at = chunk_rows(s, i)
        attended[at, :] = jnp.zeros((s.chunk, s.width), WIDE)
        key_sum[at, :] = jnp.zeros((s.chunk, s.width), WIDE)

        def over(j, carry):
            to = chunk_rows(s, j)
            mask = block_mask(s, labels_down, labels_across, i, j, False)
            key_sum[at, :] += dot(mask.astype(LOW), key_feature[to, :])
            numerator = attended[at, :]
            for head in range(s.here):
                lanes = head_lanes(s.width, head)
                scores = dot_right(only(query_feature[at, :], lanes), key_feature[to, :])
                numerator = numerator + dot((scores * mask).astype(LOW), only(values[to, :], lanes))
            attended[at, :] = numerator
            return carry

        lax.fori_loop(0, i + 1, over, 0)

    weights.pass_x(1)
    take_messages(p, messages, message_send, message_recv)
    prefix_total, label = join_messages(p, messages, prefix_low, 1, p.row > 0, True)
    latest[...] = jnp.broadcast_to(label, latest.shape)

    attention = Gather(p, lambda g, k: gathered.at[g, k], att_send, att_recv)

    @pl.loop(0, s.chunks)
    def _(i):
        at = chunk_rows(s, i)
        matching = (labels_down[at, 0:1] == latest[0:1, 0:1]).astype(WIDE)
        query = query_feature[at, :].astype(WIDE)
        numerator = attended[at, :] + dot((query * matching).astype(LOW), prefix_low[...])
        sums = key_sum[at, :] + matching * prefix_total
        key_sum[at, :] = sums
        below = over_heads(query * sums, ones[...])
        denominator[at, :] = below
        value = numerator / below
        attended[at, :] = value
        gathered[p.head, i] = value.astype(LOW).astype(WIDE)
        attention.start(i)

    for save in saves[4:]:
        save.start()
    weights.pass_core()
    weights.finish()
    for group in range(s.heads):
        rows = slice(group * s.width, (group + 1) * s.width)
        weight_full[rows, :] = wide_rows[rows, :].astype(LOW)
    weights.sent()
    attention.forward(0)
    for load in loads:
        load.wait()

    def low_rows(g, k):
        start = k * s.chunk + (lax.rem(g, 2) * s.ny + g // 2) * s.sub
        return pl.ds(pl.multiple_of(start, s.sub), s.sub)

    hidden_gather = Gather(p, lambda g, k: wide_rows.at[low_rows(g, k)], low_send, low_recv)
    reduced = Reduce(p, parts, near, far, (near_send, near_recv, far_send, far_recv))
    two = Reduce(p, parts, near_two, None, (two_send, two_recv, None, None))
    first = Halving(
        p,
        lambda piece: first_gradient.at[piece],
        first_near,
        first_far,
        (first_near_send, first_near_recv, first_far_send, first_far_recv),
    )
    order = first.order
    gain_part[...] = jnp.zeros_like(gain_part)
    shares = (2, s.ny, s.sub, TILE)

    def feed_forward(k):
        at = chunk_rows(s, k)
        attention.finish(k)
        for group in range(s.heads):
            joined[:, group * s.width : (group + 1) * s.width] = gathered[group, k].astype(LOW)
        for tile in range(s.model // TILE):
            cols = slice(tile * TILE, (tile + 1) * TILE)
            product = dot(joined[...], weight_full[:, cols])
            hidden[:, :, :, cols] = product.reshape(shares) + pixels[k, :, :, :, cols].astype(WIDE)
        hidden_share[k] = hidden[p.c, p.y]
        unit, scale = normalise(hidden[...].reshape(s.chunk, s.model))
        normed_again[at, :] = (unit * second_gain[...]).astype(LOW)

        @pl.when(k + 1 < s.chunks)
        def _():
            attention.forward(k + 1)

        low = normed_again[at, :]
        back = cotangent[k].reshape(s.chunk, s.model)
        for tile in range(s.units // TILE):
            cols = slice(tile * TILE, (tile + 1) * TILE)
            upward = dot(low, up_weight[:, cols])
            middle_back = dot_right(back, down_weight[cols, :])
            root = math.sqrt(2.0 / math.pi)
            square = upward * upward
            bent = jnp.tanh(root * upward * (1.0 + 0.044715 * square))
            half = 0.5 + 0.5 * bent
            slope = half + 0.5 * upward * (1.0 - bent * bent) * (root * (1.0 + 3.0 * 0.044715 * square))
            middle[at, cols] = (upward * half).astype(LOW)
            upward_low[at, cols] = (middle_back * slope).astype(LOW)
        low = upward_low[at, :]
        for tile in range(s.model // TILE):
            cols = slice(tile * TILE, (tile + 1) * TILE)
            parts[k, :, :, :, cols] = dot_right(low, up_weight[cols, :]).reshape(shares)
        reduced.start(k)

    def second_norm_back(k):
        grad = reduced.total(k)
        unit, scale = normalise(hidden_share[k])
        gain_part[0:1, :] += jnp.sum(grad * unit, axis=0, keepdims=True)
        part = normalise_back(unit, scale, second_gain[...], grad)
        value = cotangent[k, p.c, p.y].astype(WIDE) + part
        gradient_share[k] = value
        wide_rows[low_rows(p.head, k), :] = value.astype(LOW).astype(WIDE)
        hidden_gather.start(k)

    span = s.nx * s.cut

    def span_of(turn):
        return pl.ds(pl.multiple_of(first.piece(order[turn]) * span, span), span)

    def first_outer(turn):
        block = normed_again[:, span_of(turn)]
        target = first_gradient.at[first.piece(order[turn])]
        for at in range(0, s.first, s.step):
            cols = slice(at, at + s.step)
            target[:, :, cols] = dot_left(block, upward_low[:, cols]).reshape(s.nx, s.cut, s.step)
        first.start(order[turn])

    def first_join(turn):
        first.join(order[turn], first_gradient[first.piece(order[turn]), p.x])
        if order[turn] % 2:
            first.settle(order[turn])

    def staged(turn):
        slot = turn % 2
        return pltpu.make_async_copy(staging.at[slot], wide_gradient.at[first.piece(order[turn])], staging_sem.at[slot])

    def rest_outer(turn):
        if turn >= 2:
            staged(turn - 2).wait()
        target = staging.at[turn % 2]
        block = normed_again[:, span_of(turn)]
        for at in range(s.first, s.units, s.step):
            cols = slice(at - s.first, at - s.first + s.step)
            value = dot_left(block, upward_low[:, at : at + s.step])
            target[:, :, cols] = value.reshape(s.nx, s.cut, s.step)
        block = cotangent[:, :, :, :, span_of(turn)].reshape(s.tokens, span)
        for at in range(0, s.units, TILE):
            cols = slice(s.units - s.first + at, s.units - s.first + at + TILE)
            value = dot_left(block, middle[:, at : at + TILE])
            target[:, :, cols] = value.reshape(s.nx, s.cut, TILE)
        staged(turn).start()

    @pl.loop(0, s.chunks)
    def _(k):
        feed_forward(k)

        @pl.when(k >= 1)
        def _():
            reduced.middle(k - 1)

    end = s.chunks
    first_outer(0)
    reduced.middle(end - 1)
    for turn in range(1, s.nz):
        first_outer(turn)
    for k in range(end - 2):
        second_norm_back(k)
    rest_outer(0)
    for k in range(end - 2, end):
        second_norm_back(k)
        first_join(k - end + 2)
        rest_outer(k - end + 3)
    for turn in range(3, s.nz):
        rest_outer(turn)

    @pl.loop(0, s.chunks)
    def _(k):
        reduced.near_sent(k)
        low = middle[chunk_rows(s, k), :]
        for tile in range(s.model // TILE):
            cols = slice(tile * TILE, (tile + 1) * TILE)
            parts[k, :, :, :, cols] = dot(low, down_weight[:, cols]).reshape(shares)
        two.start(k)

    for turn in range(2, s.nz):
        first_join(turn)
        if order[turn] % 2:
            first.settle(order[turn] + 1)
    for k in range(s.chunks):
        two.join(k)
        pixel_share[k] = pixels[k, p.c, p.y]
    for k in range(end - 2):
        hidden_gather.forward(k)
    first.settle(0)
    for k in range(end - 2, end):
        hidden_gather.forward(k)

    for k in range(s.chunks):
        hidden_gather.finish(k)
        rows = slice(k * s.chunk, (k + 1) * s.chunk)
        hidden_low[rows, :] = wide_rows[rows, :].astype(LOW)
    first_out[...] = first.total()
    first.sent()
    for turn in range(max(0, s.nz - 2), s.nz):
        staged(turn).wait()
    for k in range(s.chunks):
        attention.sent(k)
        hidden_gather.sent(k)
        reduced.far_sent(k)
        two.near_sent(k)
    for save in saves:
        save.wait()


def backward_kernel(
    s,
    crop_ids,
    query_feature,
    key_feature,
    values,
    attended,
    denominator,
    key_sum,
    hidden_low,
    gain_part,
    prefix_low,
    latest,
    query_weight,
    key_weight,
    value_weight,
    out_weight,
    first_gain,
    near_two,
    normed_source,
    hidden_source,
    gradient_source,
    pixel_source,
    wide_gradient,
    gains,
    wide_out,
    narrow_out,
    pixel_out,
    result_out,
    normed,
    hidden_share,
    gradient_share,
    pixel_share,
    two_own,
    labels_across,
    labels_down,
    parts,
    far_two,
    near_four,
    far_four,
    result_wide,
    result_low,
    pixel_gradient,
    numerator_low,
    denominator_back,
    spread_back,
    query_back,
    key_back,
    value_back,
    narrow_low,
    suffix_low,
    state,
    total,
    ones,
    messages,
    narrow_gradient,
    own_wide,
    own_pairs,
    near_wide,
    far_wide,
    near_split,
    far_split,
    pairs_split,
    near_narrow,
    far_narrow,
    gain_heads,
    gain_x,
    gain_z,
    load_sem,
    message_send,
    message_recv,
    two_far_send,
    two_far_recv,
    four_near_send,
    four_near_recv,
    four_far_send,
    four_far_recv,
    result_send,
    result_recv,
    pixel_send,
    pixel_recv,
    wide_near_send,
    wide_near_recv,
    wide_far_send,
    wide_far_recv,
    split_near_send,
    split_near_recv,
    split_far_send,
    split_far_recv,
    split_send,
    split_recv,
    narrow_near_send,
    narrow_near_recv,
    narrow_far_send,
    narrow_far_recv,
    gain_send,
    gain_recv,
    own_sem,
    pairs_sem,
    result_sem,
    pixel_sem,
):
    p = Place(s)
    p.meet()
    two = Reduce(p, None, near_two, far_two, (None, None, two_far_send, two_far_recv))
    four = Reduce(p, parts, near_four, far_four, (four_near_send, four_near_recv, four_far_send, four_far_recv))
    wide = Halving(
        p,
        lambda piece: wide_gradient.at[piece, :, :, s.split :],
        near_wide,
        far_wide,
        (wide_near_send, wide_near_recv, wide_far_send, wide_far_recv),
    )
    split = Halving(
        p,
        lambda piece: wide_gradient.at[piece, :, :, 0 : s.split],
        near_split,
        far_split,
        (split_near_send, split_near_recv, split_far_send, split_far_recv),
        pairs_split,
        (split_send, split_recv),
    )
    sides = (slice(0, s.narrow // 2), slice(s.narrow // 2, s.narrow))

    def narrow_job(i):
        sems = (narrow_near_send.at[i], narrow_near_recv.at[i], narrow_far_send.at[i], narrow_far_recv.at[i])
        return Halving(
            p, lambda piece: narrow_gradient.at[piece, :, :, sides[i]], near_narrow.at[i], far_narrow.at[i], sems
        )

    narrow = (narrow_job(0), narrow_job(1))
    jobs = (wide, split) + narrow
    steps = [(job, m) for job in jobs for m in job.order]
    flight = {"next": 0, "ready": s.nz, "taken": 0}
    pending = []

    def settle_ready(at):
        for entry in list(pending):
            if entry[0] <= at:
                entry[1].settle(entry[2])
                pending.remove(entry)

    def push(limit):
        while flight["next"] <= limit and flight["next"] < flight["ready"]:
            job, m = steps[flight["next"]]
            job.start(m)
            flight["next"] += 1

    def own_load(turn):
        source = wide_gradient.at[wide.piece(wide.order[turn]), p.x, :, s.split :]
        return pltpu.make_async_copy(source, own_wide.at[turn % 2], own_sem.at[turn % 2])

    def pairs_load(m):
        source = wide_gradient.at[split.piece(m), :, :, 0 : s.split]
        return pltpu.make_async_copy(source, own_pairs.at[m >> 1], pairs_sem.at[m >> 1])

    def take():
        at = flight["taken"]
        flight["taken"] = at + 1
        job, m = steps[at]
        if job is wide:
            own_load(at).wait()
            wide.join(m, own_wide[at % 2])
            if at + 2 < s.nz:
                own_load(at + 2).start()
        elif job is split:
            split.join(m)
        else:
            job.join(m, narrow_gradient[job.piece(m), p.x, :, sides[narrow.index(job)]])
        push(at + AHEAD)
        if (m >> job.first_bit) & 1:
            job.settle(m)
        else:
            pending.append((at + 1 if m else at + 2, job, m))
        settle_ready(at)

    for m in split.odd:
        split.pair_copy(m).start()
    push(0)
    for k in range(s.chunks):
        two.spread(k)
    loads = [
        pltpu.make_async_copy(source, target, load_sem.at[i])
        for i, (source, target) in enumerate(
            (
                (near_two.at[:, p.y], two_own),
                (hidden_source, hidden_share),
                (gradient_source, gradient_share),
                (pixel_source, pixel_share),
                (normed_source, normed),
            )
        )
    ]
    for load in loads:
        load.start()
    own_load(0).start()
    own_load(1).start()
    for m in split.order:
        pairs_load(m).start()
    result_gather = Gather(p, lambda g, k: result_wide.at[k, lax.rem(g, 2), g // 2], result_send, result_recv)
    pixel_gather = Gather(p, lambda g, k: pixel_gradient.at[k, lax.rem(g, 2), g // 2], pixel_send, pixel_recv)
    shares = (2, s.ny, s.sub, TILE)
    spread_labels(s, crop_ids, labels_across, labels_down)
    first = labels_across[0][:, 0:1]
    state[...] = jnp.zeros_like(state)
    total[...] = jnp.zeros_like(total)
    ones[...] = block_ones(s.width)

    @pl.loop(0, s.chunks)
    def _(k):
        at = chunk_rows(s, k)
        back = dot_right(hidden_low[at, :], out_weight[...])
        below = denominator[at, :]
        low = (back / below).astype(LOW)
        numerator_low[at, :] = low
        slope = -over_heads(back * attended[at, :], ones[...]) / below
        denominator_back[at, :] = slope
        query = query_feature[at, :].astype(WIDE)
        spread = slope * query
        spread_back[at, :] = spread.astype(LOW)
        leading = (labels_down[at, 0:1] == first).astype(WIDE)
        state[...] += dot_left((query * leading).astype(LOW), low)
        total[0:1, :] += jnp.sum(spread * leading, axis=0, keepdims=True)

    write_message(s, messages.at[0], state, total[0:1, :], first)
    send_messages(p, messages, message_send, message_recv)
    push(AHEAD - 1)

    @pl.loop(0, s.chunks)
    def _(i):
        at = chunk_rows(s, i)
        query_back[at, :] = denominator_back[at, :] * key_sum[at, :]

        def over(j, carry):
            to = chunk_rows(s, j)
            mask = block_mask(s, labels_down, labels_across, i, j, False)
            value = query_back[at, :]
            for head in range(s.here):
                lanes = head_lanes(s.width, head)
                scores = dot_right(only(numerator_low[at, :], lanes), values[to, :])
                value = value + dot((scores * mask).astype(LOW), only(key_feature[to, :], lanes))
            query_back[at, :] = value
            return carry

        lax.fori_loop(0, i + 1, over, 0)

    take()

    @pl.loop(0, s.chunks)
    def _(j):
        to = chunk_rows(s, j)
        key_back[to, :] = jnp.zeros((s.chunk, s.width), WIDE)
        value_back[to, :] = jnp.zeros((s.chunk, s.width), WIDE)

        def over(i, carry):
            at = chunk_rows(s, i)
            mask = block_mask(s, labels_down, labels_across, i, j, True)
            key_value = key_back[to, :] + dot(mask.astype(LOW), spread_back[at, :])
            value_value = value_back[to, :]
            for head in range(s.here):
                lanes = head_lanes(s.width, head)
                back = dot_right(only(values[to, :], lanes), numerator_low[at, :])
                key_value = key_value + dot((back * mask).astype(LOW), only(query_feature[at, :], lanes))
                scores = dot_right(only(key_feature[to, :], lanes), query_feature[at, :])
                value_value = value_value + dot((scores * mask).astype(LOW), only(numerator_low[at, :], lanes))
            key_back[to, :] = key_value
            value_back[to, :] = value_value
            return carry

        lax.fori_loop(j, s.chunks, over, 0)

    for load in loads:
        load.wait()
    take()

    @pl.loop(0, s.chunks)
    def _(k):
        value = hidden_share[k] + two.total(k, two_own[k])
        result_wide[k, p.c, p.y] = value.astype(LOW).astype(WIDE)

        @pl.when(k < s.chunks // 2)
        def _():
            result_gather.start(k)

    take_messages(p, messages, message_send, message_recv)
    suffix_total, following = join_messages(p, messages, suffix_low, s.rows - 1, p.row < s.rows - 1, False)

    @pl.loop(0, s.chunks)
    def _(k):
        at = chunk_rows(s, k)
        matching = (labels_down[at, 0:1] == latest[0:1, 0:1]).astype(WIDE)
        later = (labels_down[at, 0:1] == following).astype(WIDE)
        query, key = query_feature[at, :], key_feature[at, :]
        value = query_back[at, :] + matching * dot_right(numerator_low[at, :], prefix_low[...])
        low = (value * jnp.minimum(query.astype(WIDE), 1.0)).astype(LOW)
        numerator_value = value_back[at, :] + later * dot(key, suffix_low[...])
        key_value = key_back[at, :] + later * (dot_right(values[at, :], suffix_low[...]) + suffix_total)
        key_low = (key_value * jnp.minimum(key.astype(WIDE), 1.0)).astype(LOW)
        value_low = numerator_value.astype(LOW)
        narrow_low[0, at, :] = low
        narrow_low[1, at, :] = key_low
        narrow_low[2, at, :] = value_low
        for tile in range(s.model // TILE):
            cols = slice(tile * TILE, (tile + 1) * TILE)
            product = (
                dot_right(low, query_weight[cols, :])
                + dot_right(key_low, key_weight[cols, :])
                + dot_right(value_low, value_weight[cols, :])
            )
            parts[k, :, :, :, cols] = product.reshape(shares)
        four.start(k)

    @pl.loop(0, s.chunks)
    def _(k):
        four.middle(k)

    take()
    for m in split.order:
        pairs_load(m).wait()
        split.join_pair(m, own_pairs[m >> 1])
    flight["ready"] = len(wide.order) + len(split.order)

    span = s.nx * s.cut
    for piece in range(s.nz):
        cols = slice(piece * span, (piece + 1) * span)
        shape = (s.nx, s.cut, s.width)
        product = dot_left(hidden_low[:, cols], attended[...].astype(LOW))
        narrow_gradient[piece, :, :, 0 : s.width] = product.reshape(shape)
        for part in range(3):
            product = dot_left(normed[:, cols], narrow_low[part])
            narrow_gradient[piece, :, :, (part + 1) * s.width : (part + 2) * s.width] = product.reshape(shape)
    flight["ready"] = len(steps)

    def take_until_left(count):
        while len(steps) - flight["taken"] > count:
            take()

    left = 2 * s.nz
    take_until_left(left + len(split.order))
    gain_x[0] = gain_part[...]

    def result_copy(k):
        rows = pl.ds(k * s.chunk, s.chunk)
        return pltpu.make_async_copy(result_low.at[rows], result_out.at[rows], result_sem.at[k])

    def pixel_copy(k):
        return pltpu.make_async_copy(pixel_gradient.at[k], pixel_out.at[k], pixel_sem.at[k])

    def first_norm_back(k):
        grad = four.total(k)
        unit, scale = normalise(pixel_share[k].astype(WIDE))
        gain_x[0, 1:2, :] += jnp.sum(grad * unit, axis=0, keepdims=True)
        pixel_gradient[k, p.c, p.y] = gradient_share[k] + normalise_back(unit, scale, first_gain[...], grad)
        pixel_gather.start(k)

    for k in range(s.chunks // 2):
        first_norm_back(k)
    take_until_left(left + len(split.order) // 2)
    for k in range(s.chunks // 2, s.chunks):
        first_norm_back(k)

    def gain_copies(index, buffer, device):
        return [
            remote(buffer.at[0], buffer.at[step], gain_send.at[index, step], gain_recv.at[index, step], device(step))
            for step in range(1, buffer.shape[0])
        ]

    def gain_start(*what):
        for copy in gain_copies(*what):
            copy.start()

    def gain_total(*what):
        for copy in gain_copies(*what):
            copy.wait()
        value = what[1][0]
        for step in range(1, what[1].shape[0]):
            value = value + what[1][step]
        return value

    rounds = (
        (0, gain_x, p.along_x),
        (1, gain_z, p.along_z),
        (2, gain_heads, p.along_heads),
    )
    gain_start(*rounds[0])
    for k in range(s.chunks // 2, s.chunks):
        result_gather.start(k)
    take_until_left(left)
    for k in range(s.chunks // 2):
        result_gather.forward(k)
    take_until_left(left - 2)
    gain_z[0] = gain_total(*rounds[0])
    gain_start(*rounds[1])
    for k in range(s.chunks // 2):
        pixel_gather.forward(k)
    take_until_left(left - 4)
    gain_heads[0] = gain_total(*rounds[1])
    gain_start(*rounds[2])
    for k in range(s.chunks // 2, s.chunks):
        pixel_gather.forward(k)
    for k in range(s.chunks // 2, s.chunks):
        result_gather.forward(k)
    take_until_left(2)
    for k in range(s.chunks):
        pixel_gather.finish(k)
        pixel_copy(k).start()
    for k in range(s.chunks):
        result_gather.finish(k)
        result_low[k * s.chunk : (k + 1) * s.chunk, :] = result_wide[k].reshape(s.chunk, s.model).astype(LOW)
        result_copy(k).start()
    gains[...] = gain_total(*rounds[2])
    take_until_left(0)
    wide_out[:, s.split :] = wide.total()
    wide_out[:, 0 : s.split] = split.total()
    settle_ready(len(steps) + 2)
    for job, side in zip(narrow, sides):
        narrow_out[:, side] = job.total()
    for k in range(s.chunks):
        result_copy(k).wait()
        pixel_copy(k).wait()
        pixel_gather.sent(k)
        result_gather.sent(k)
        two.far_sent(k)
        four.near_sent(k)
        four.far_sent(k)
    for job in jobs:
        job.sent()


def finish_kernel(
    s,
    first_out,
    wide_out,
    narrow_out,
    gains,
    pixel_source,
    result_source,
    up_gradient,
    down_gradient,
    out_gradient,
    query_gradient,
    key_gradient,
    value_gradient,
    first_gain,
    second_gain,
    pixel_gradient,
    result,
    pixel_rows,
    result_rows,
    read_sem,
    write_sem,
):
    row = lax.axis_index("rows")

    def places(i, k):
        rows = pl.ds(k * s.chunk, s.chunk)
        if i == 0:
            return pixel_source.at[k], pixel_rows.at[k], pixel_gradient.at[k]
        return result_source.at[rows], result_rows.at[rows], result.at[rows]

    def read(i, k):
        source, between, unused = places(i, k)
        return pltpu.make_async_copy(source, between, read_sem.at[i, k])

    def write(i, k):
        unused, between, target = places(i, k)
        return pltpu.make_async_copy(between, target, write_sem.at[i, k])

    moves = [(i, k) for k in range(s.chunks) for i in range(2)]
    for move in moves:
        read(*move).start()
    rest = s.units - s.first
    up_gradient[:, 0 : s.first] = first_out[...]
    up_gradient[:, s.first :] = wide_out[:, 0:rest]
    down_gradient[...] = wide_out[:, rest:].T
    out_gradient[...] = narrow_out[:, 0 : s.width].T
    for i, target in enumerate((query_gradient, key_gradient, value_gradient)):
        target[...] = narrow_out[:, (i + 1) * s.width : (i + 2) * s.width]
    own = jnp.zeros((8, s.cut), WIDE)
    for at in range(s.rows):
        own = own + jnp.where(row == at, gains[:, at * s.cut : (at + 1) * s.cut], 0.0)
    second_gain[...] = own[0:1]
    first_gain[...] = own[1:2]
    for move in moves:
        read(*move).wait()
        write(*move).start()
    for move in moves:
        write(*move).wait()


def vmem(count):
    return [pl.BlockSpec(memory_space=pltpu.VMEM)] * count


def dma(*shape):
    return pltpu.SemaphoreType.DMA(shape)


def on_device(
    rows,
    heads,
    pixels,
    crop_ids,
    first_gain,
    query_weight,
    key_weight,
    value_weight,
    out_weight,
    second_gain,
    up_weight,
    down_weight,
    cotangent,
):
    tokens, model = pixels.shape
    s = Sizes(rows, heads, tokens, model, query_weight.shape[1], up_weight.shape[1])
    whole = (s.chunks, 2, s.ny, s.sub, model)
    share = (s.chunks, s.sub, model)
    labels = crop_ids.reshape(s.chunks, 1, s.chunk)
    shape = jax.ShapeDtypeStruct
    any_space = pl.BlockSpec(memory_space=pl.ANY)

    def reduce_sems():
        return [
            dma(s.chunks),
            dma(s.chunks),
            dma(s.ny - 1, s.chunks),
            dma(s.ny - 1, s.chunks),
        ]

    def gather_sems():
        return [dma(2 * s.ny - 1, s.chunks), dma(heads, s.chunks)]

    def scatter_sems():
        return [
            dma(s.nx - 1, s.nz),
            dma(s.nx - 1, s.nz),
            dma(s.nz - 1),
            dma(s.nz - 1),
        ]

    def scatter_buffers(width, pieces=s.nz):
        return [
            pltpu.VMEM((s.nx - 1, pieces, s.cut, width), WIDE),
            pltpu.VMEM((pieces - 1, s.cut, width), WIDE),
        ]

    half = s.nz // 2

    lows = [(tokens, model)] + [(tokens, s.width)] * 3
    wides = [(tokens, s.width)] * 3
    near = (s.chunks, s.ny, s.sub, model)
    far = (s.ny - 1,) + share
    label_buffers = [
        pltpu.VMEM((s.chunks, 1, s.chunk), WIDE),
        pltpu.VMEM((tokens, LANES), WIDE),
    ]
    outs = [
        shape((tokens, model), LOW),
        shape(share, WIDE),
        shape(share, WIDE),
        shape(share, LOW),
        shape((8, model), WIDE),
        shape((s.width, s.width), LOW),
        shape((8, LANES), WIDE),
        shape(near, WIDE),
        shape((s.cut, s.first), WIDE),
        *[shape(size, LOW) for size in lows],
        *[shape(size, WIDE) for size in wides],
        shape((s.nz, s.nx, s.cut, s.wide), WIDE),
    ]
    shared = WeightGather.halves
    (
        hidden_low,
        hidden_share,
        gradient_share,
        pixel_share,
        gain_part,
        prefix_low,
        latest,
        near_two,
        first_out,
        normed,
        query_feature,
        key_feature,
        values,
        attended,
        denominator,
        key_sum,
        wide_gradient,
    ) = pl.pallas_call(
        functools.partial(forward_kernel, s),
        out_shape=outs,
        in_specs=vmem(8) + [any_space] * 3,
        out_specs=vmem(9) + [any_space] * 8,
        scratch_shapes=[
            *[pltpu.VMEM(size, LOW) for size in lows],
            *[pltpu.VMEM(size, WIDE) for size in wides],
            pltpu.VMEM((model, s.units), LOW),
            pltpu.VMEM((s.units, model), LOW),
            pltpu.VMEM(whole, LOW),
            *label_buffers,
            pltpu.VMEM((heads, s.chunks, s.chunk, s.width), WIDE),
            pltpu.VMEM((max(tokens, model), model), WIDE),
            pltpu.VMEM((model, model), LOW),
            pltpu.VMEM((s.chunk, model), LOW),
            pltpu.VMEM(whole[1:], WIDE),
            pltpu.VMEM((tokens, model), LOW),
            pltpu.VMEM((tokens, s.units), LOW),
            pltpu.VMEM((tokens, s.units), LOW),
            pltpu.VMEM(whole, WIDE),
            pltpu.VMEM(near, WIDE),
            pltpu.VMEM(far, WIDE),
            pltpu.VMEM((rows, s.message, LANES), WIDE),
            pltpu.VMEM((s.width, s.width), WIDE),
            pltpu.VMEM((8, s.width), WIDE),
            pltpu.VMEM((s.width, s.width), LOW),
            pltpu.VMEM((2, s.nx, s.cut, s.wide), WIDE),
            pltpu.VMEM((s.nz, s.nx, s.cut, s.first), WIDE),
            *scatter_buffers(s.first),
            dma(3),
            dma(7),
            dma(2),
            *[dma(s.ny - 1, shared)] * 2,
            *[dma(s.ny - 1, s.nx - 1, shared)] * 2,
            *[dma(s.ny)] * 2,
            *gather_sems(),
            *gather_sems(),
            dma(rows),
            dma(rows),
            *reduce_sems(),
            dma(s.chunks),
            dma(s.chunks),
            *scatter_sems(),
        ],
        compiler_params=pltpu.CompilerParams(
            collective_id=0, has_side_effects=True, vmem_limit_bytes=60 << 20
        ),
        name="forward_part",
    )(
        pixels.reshape(whole),
        labels,
        first_gain.reshape(1, model),
        query_weight,
        key_weight,
        value_weight,
        out_weight,
        second_gain.reshape(1, model),
        up_weight,
        down_weight,
        cotangent.reshape(whole),
    )
    outs = [
        shape((8, model), WIDE),
        shape((s.cut, s.wide), WIDE),
        shape((s.cut, s.narrow), WIDE),
        shape(whole, WIDE),
        shape((tokens, model), LOW),
    ]
    gains, wide_out, narrow_out, pixel_wide, result_low = pl.pallas_call(
        functools.partial(backward_kernel, s),
        out_shape=outs,
        in_specs=vmem(16) + [any_space] * 6,
        out_specs=vmem(3) + [any_space] * 2,
        scratch_shapes=[
            pltpu.VMEM((tokens, model), LOW),
            pltpu.VMEM(share, WIDE),
            pltpu.VMEM(share, WIDE),
            pltpu.VMEM(share, LOW),
            pltpu.VMEM(share, WIDE),
            *label_buffers,
            pltpu.VMEM(whole, WIDE),
            pltpu.VMEM(far, WIDE),
            pltpu.VMEM(near, WIDE),
            pltpu.VMEM(far, WIDE),
            pltpu.VMEM(whole, WIDE),
            pltpu.VMEM((tokens, model), LOW),
            pltpu.VMEM(whole, WIDE),
            pltpu.VMEM((tokens, s.width), LOW),
            pltpu.VMEM((tokens, s.width), WIDE),
            pltpu.VMEM((tokens, s.width), LOW),
            *[pltpu.VMEM((tokens, s.width), WIDE)] * 3,
            pltpu.VMEM((3, tokens, s.width), LOW),
            pltpu.VMEM((s.width, s.width), LOW),
            pltpu.VMEM((s.width, s.width), WIDE),
            pltpu.VMEM((8, s.width), WIDE),
            pltpu.VMEM((s.width, s.width), LOW),
            pltpu.VMEM((rows, s.message, LANES), WIDE),
            pltpu.VMEM((s.nz, s.nx, s.cut, s.narrow), WIDE),
            pltpu.VMEM((2, s.cut, s.wide - s.split), WIDE),
            pltpu.VMEM((half, s.nx, s.cut, s.split), WIDE),
            *scatter_buffers(s.wide - s.split),
            *scatter_buffers(s.split, half),
            pltpu.VMEM((half, s.nx, s.cut, s.split), WIDE),
            pltpu.VMEM((2, s.nx - 1, s.nz, s.cut, s.narrow // 2), WIDE),
            pltpu.VMEM((2, s.nz - 1, s.cut, s.narrow // 2), WIDE),
            pltpu.VMEM((heads, 8, model), WIDE),
            pltpu.VMEM((s.nx, 8, model), WIDE),
            pltpu.VMEM((s.nz, 8, model), WIDE),
            dma(5),
            dma(rows),
            dma(rows),
            *reduce_sems()[2:],
            *reduce_sems(),
            *gather_sems(),
            *gather_sems(),
            *scatter_sems(),
            *scatter_sems(),
            dma(half),
            dma(half),
            *[dma(2, s.nx - 1, s.nz)] * 2,
            *[dma(2, s.nz - 1)] * 2,
            dma(3, max(heads, s.nx, s.nz)),
            dma(3, max(heads, s.nx, s.nz)),
            dma(2),
            dma(half),
            dma(s.chunks),
            dma(s.chunks),
        ],
        compiler_params=pltpu.CompilerParams(
            collective_id=1, has_side_effects=True, vmem_limit_bytes=60 << 20
        ),
        name="backward_part",
    )(
        labels,
        query_feature,
        key_feature,
        values,
        attended,
        denominator,
        key_sum,
        hidden_low,
        gain_part,
        prefix_low,
        latest,
        query_weight,
        key_weight,
        value_weight,
        out_weight,
        first_gain.reshape(1, model),
        near_two,
        normed,
        hidden_share,
        gradient_share,
        pixel_share,
        wide_gradient,
    )
    outs = [
        shape((s.cut, s.units), WIDE),
        shape((s.units, s.cut), WIDE),
        shape((s.width, s.cut), WIDE),
        *[shape((s.cut, s.width), WIDE)] * 3,
        *[shape((1, s.cut), WIDE)] * 2,
        shape(whole, WIDE),
        shape((tokens, model), LOW),
    ]
    up_part, down_part, out_part, query_part, key_part, value_part, first_part, second_part, pixel_part, result = (
        pl.pallas_call(
            functools.partial(finish_kernel, s),
            out_shape=outs,
            in_specs=vmem(4) + [any_space] * 2,
            out_specs=vmem(8) + [any_space] * 2,
            scratch_shapes=[
                pltpu.VMEM(whole, WIDE),
                pltpu.VMEM((tokens, model), LOW),
                dma(2, s.chunks),
                dma(2, s.chunks),
            ],
            compiler_params=pltpu.CompilerParams(vmem_limit_bytes=60 << 20),
            name="finish_part",
        )(first_out, wide_out, narrow_out, gains, pixel_wide, result_low)
    )
    return (
        result,
        pixel_part.reshape(tokens, model),
        first_part.reshape(s.cut),
        query_part,
        key_part,
        value_part,
        out_part,
        second_part.reshape(s.cut),
        up_part,
        down_part,
    )


def solution(mesh):
    return jax.shard_map(
        functools.partial(on_device, mesh.shape["rows"], mesh.shape["heads"]),
        mesh=mesh,
        in_specs=(
            P("rows", None),
            P("rows"),
            P(),
            P(None, "heads"),
            P(None, "heads"),
            P(None, "heads"),
            P("heads", None),
            P(),
            P(None, "heads"),
            P("heads", None),
            P("rows", None),
        ),
        out_specs=(
            P("rows", None),
            P("rows", None),
            P("rows"),
            P("rows", "heads"),
            P("rows", "heads"),
            P("rows", "heads"),
            P("heads", "rows"),
            P("rows"),
            P("rows", "heads"),
            P("heads", "rows"),
        ),
        check_vma=False,
    )
```

```python
import functools
import math

import jax
import jax.numpy as jnp
from jax import lax
from jax.experimental import pallas as pl
from jax.experimental.pallas import tpu as pltpu
from jax.sharding import PartitionSpec as P

HEAD = 64
EPSILON = 1e-05
MESH = pl.DeviceIdType.MESH
LOW = jnp.bfloat16
WIDE = jnp.float32
LANES = 128
TILE = 256
AHEAD = 3
FIRST = 6


def dot(left, right):
    return jnp.dot(left, right, preferred_element_type=WIDE)


def dot_left(left, right):
    return lax.dot_general(left, right, (((0,), (0,)), ((), ())), preferred_element_type=WIDE)


def dot_right(left, right):
    return lax.dot_general(left, right, (((1,), (1,)), ((), ())), preferred_element_type=WIDE)


def normalise(value):
    middle = jnp.mean(value, axis=-1, keepdims=True)
    centred = value - middle
    spread = jnp.mean(centred * centred, axis=-1, keepdims=True)
    scale = lax.rsqrt(spread + EPSILON)
    return centred * scale, scale


def normalise_back(unit, scale, gain, grad):
    scaled = grad * gain
    along = jnp.mean(scaled * unit, axis=-1, keepdims=True)
    return scale * (scaled - jnp.mean(scaled, axis=-1, keepdims=True) - unit * along)


class Sizes:
    def __init__(self, rows, heads, tokens, model, width, units):
        self.rows, self.heads = rows, heads
        self.ny = heads // 2
        self.nx = self.ny if rows % self.ny == 0 else 1
        self.nz = rows // self.nx
        self.tokens, self.model, self.width, self.units = tokens, model, width, units
        self.chunk = min(TILE, tokens)
        self.chunks = tokens // self.chunk
        self.sub = self.chunk // heads
        self.here = width // HEAD
        self.pairs = width // LANES
        self.tiles = (self.pairs + 1) // 2
        self.message = self.tiles * LANES + 8
        self.cut = model // rows
        self.first = units // LANES * FIRST // 8 * LANES
        self.step = TILE if self.first % TILE == 0 and units % TILE == 0 else LANES
        self.wide = 2 * units - self.first
        self.narrow = 4 * width
        self.split = round((self.wide + self.narrow) / (4 * LANES)) * LANES


class Place:
    def __init__(self, sizes):
        s = self.s = sizes
        self.row = lax.axis_index("rows")
        self.head = lax.axis_index("heads")
        self.y, self.c = self.head // 2, lax.rem(self.head, 2)
        self.x, self.z = lax.rem(self.row, s.nx), self.row // s.nx

    def other(self):
        return (self.row, self.y * 2 + 1 - self.c)

    def group(self, step):
        return lax.rem(self.y + self.s.ny - step, self.s.ny) * 2 + self.c

    def along_y(self, step):
        return (self.row, lax.rem(self.y + step, self.s.ny) * 2 + self.c)

    def along_x(self, step):
        return (self.z * self.s.nx + lax.rem(self.x + step, self.s.nx), self.head)

    def along_z(self, step):
        return (lax.rem(self.z + step, self.s.nz) * self.s.nx + self.x, self.head)

    def along_rows(self, step):
        return (lax.rem(self.row + step, self.s.rows), self.head)

    def along_heads(self, step):
        return (self.row, lax.rem(self.head + step, self.s.heads))

    def meet(self):
        barrier = pltpu.get_barrier_semaphore()
        for step in range(1, self.s.heads):
            pl.semaphore_signal(barrier, inc=1, device_id=self.along_heads(step), device_id_type=MESH)
        for step in range(1, self.s.rows):
            pl.semaphore_signal(barrier, inc=1, device_id=self.along_rows(step), device_id_type=MESH)
        pl.semaphore_wait(barrier, self.s.heads + self.s.rows - 2)


def remote(source, target, send, receive, device):
    return pltpu.make_async_remote_copy(
        src_ref=source, dst_ref=target, send_sem=send, recv_sem=receive, device_id=device, device_id_type=MESH
    )


class Gather:
    def __init__(self, place, view, send, receive, own=None):
        self.p, self.view, self.send, self.receive = place, view, send, receive
        self.own = own

    def copy(self, group, k, slot, device):
        source = self.view(group, k)
        return remote(source, self.view(group, k), self.send.at[slot, k], self.receive.at[group, k], device)

    def own_copy(self, k, slot, device):
        group = self.p.head
        source = self.view(group, k) if self.own is None else self.own(k)
        return remote(source, self.view(group, k), self.send.at[slot, k], self.receive.at[group, k], device)

    def start(self, k):
        for step in range(1, self.p.s.ny):
            self.own_copy(k, step, self.p.along_y(step)).start()
        self.own_copy(k, 0, self.p.other()).start()

    def forward(self, k):
        ny = self.p.s.ny
        for step in range(1, ny):
            group = self.p.group(step)
            self.copy(group, k, 0, self.p.along_y(step)).wait_recv()
            self.copy(group, k, ny - 1 + step, self.p.other()).start()

    def finish(self, k):
        for step in range(self.p.s.ny):
            own = self.p.group(step)
            group = own + 1 - 2 * self.p.c
            self.copy(group, k, 0, self.p.other()).wait_recv()

    def sent(self, k):
        ny = self.p.s.ny
        for step in range(ny):
            self.own_copy(k, step, self.p.other()).wait_send()
        for step in range(1, ny):
            self.copy(self.p.group(step), k, ny - 1 + step, self.p.other()).wait_send()


class WeightGather:
    halves = 2

    def __init__(self, place, rows, sems):
        self.p, self.rows = place, rows
        self.y_send, self.y_recv, self.x_send, self.x_recv, self.c_send, self.c_recv = sems
        self.size = place.s.width // (place.s.nx * self.halves)

    def share(self, group, x, half):
        start = (group * self.p.s.nx + x) * (self.size * self.halves) + half * self.size
        return self.rows.at[pl.ds(pl.multiple_of(start, self.size), self.size)]

    def slice(self, group):
        width = self.p.s.width
        return self.rows.at[pl.ds(pl.multiple_of(group * width, width), width)]

    def y_copy(self, step, half, group):
        ref = self.share(group, self.p.x, half)
        at = (step - 1, half)
        return remote(ref, ref, self.y_send.at[at], self.y_recv.at[at], self.p.along_y(step))

    def x_copy(self, step, side, half, x):
        ref = self.share(self.p.group(step), x, half)
        at = (step - 1, side - 1, half)
        return remote(ref, ref, self.x_send.at[at], self.x_recv.at[at], self.p.along_x(side))

    def c_copy(self, step, group):
        ref = self.slice(group)
        return remote(ref, ref, self.c_send.at[step], self.c_recv.at[step], self.p.other())

    def start(self):
        for half in range(self.halves):
            for step in range(1, self.p.s.ny):
                self.y_copy(step, half, self.p.head).start()
        self.c_copy(0, self.p.head).start()

    def pass_x(self, half):
        for step in range(1, self.p.s.ny):
            self.y_copy(step, half, self.p.group(step)).wait_recv()
            for side in range(1, self.p.s.nx):
                self.x_copy(step, side, half, self.p.x).start()

    def pass_core(self):
        nx = self.p.s.nx
        for step in range(1, self.p.s.ny):
            for half in range(self.halves):
                for side in range(1, nx):
                    self.x_copy(step, side, half, lax.rem(self.p.x + nx - side, nx)).wait_recv()
            self.c_copy(step, self.p.group(step)).start()

    def finish(self):
        for step in range(self.p.s.ny):
            self.c_copy(step, self.p.group(step) + 1 - 2 * self.p.c).wait_recv()

    def sent(self):
        for step in range(self.p.s.ny):
            self.c_copy(step, self.p.group(step)).wait_send()
            if step == 0:
                continue
            for half in range(self.halves):
                self.y_copy(step, half, self.p.head).wait_send()
                for side in range(1, self.p.s.nx):
                    self.x_copy(step, side, half, self.p.x).wait_send()


class Reduce:
    def __init__(self, place, parts, near, far, sems):
        self.p, self.parts, self.near, self.far = place, parts, near, far
        self.near_send, self.near_recv, self.far_send, self.far_recv = sems

    def near_copy(self, k):
        return remote(
            self.parts.at[k, 1 - self.p.c],
            self.near.at[k],
            self.near_send.at[k],
            self.near_recv.at[k],
            self.p.other(),
        )

    def far_copy(self, k, step):
        share = lax.rem(self.p.y + step, self.p.s.ny)
        return remote(
            self.near.at[k, share],
            self.far.at[step - 1, k],
            self.far_send.at[step - 1, k],
            self.far_recv.at[step - 1, k],
            self.p.along_y(step),
        )

    def start(self, k):
        self.near_copy(k).start()

    def join(self, k):
        self.near_copy(k).wait_recv()
        self.near[k] = self.near[k] + self.parts[k, self.p.c]

    def spread(self, k):
        for step in range(1, self.p.s.ny):
            self.far_copy(k, step).start()

    def middle(self, k):
        self.join(k)
        self.spread(k)

    def total(self, k, own=None):
        value = self.near[k, self.p.y] if own is None else own
        for step in range(1, self.p.s.ny):
            self.far_copy(k, step).wait_recv()
            value = value + self.far[step - 1, k]
        return value

    def near_sent(self, k):
        self.near_copy(k).wait_send()

    def far_sent(self, k):
        for step in range(1, self.p.s.ny):
            self.far_copy(k, step).wait_send()


def flipped(value, mask):
    bit = 0
    out = value
    while mask >> bit:
        if (mask >> bit) & 1:
            out = out + (1 - 2 * lax.rem(value // (1 << bit), 2)) * (1 << bit)
        bit += 1
    return out


def low_zeros(mask, count):
    return count if mask == 0 else (mask & -mask).bit_length() - 1


class Halving:
    def __init__(self, place, source, near, far, sems, pairs=None, pair_sems=None):
        self.p, self.source, self.near, self.far = place, source, near, far
        self.near_send, self.near_recv, self.far_send, self.far_recv = sems
        self.pairs, self.pair_sems = pairs, pair_sems
        self.bits = place.s.nz.bit_length() - 1
        self.first_bit = 0 if pairs is None else 1
        self.order = list(reversed(range(0, place.s.nz, 1 << self.first_bit)))
        self.odd = [m for m in reversed(range(place.s.nz)) if m % 2]

    def piece(self, m):
        return flipped(self.p.z, m)

    def to_z(self, bit):
        return (flipped(self.p.z, 1 << bit) * self.p.s.nx + self.p.x, self.p.head)

    def at(self, m):
        return m >> self.first_bit

    def pair_copy(self, m, x):
        send, receive = self.pair_sems
        at = (m >> 1, x)
        return remote(self.source(self.piece(m)).at[x], self.pairs.at[at], send.at[at], receive.at[at], self.to_z(0))

    def join_pair(self, m, own):
        for x in range(self.p.s.nx):
            self.pair_copy(m + 1, x).wait_recv()
        self.pairs[m >> 1] = self.pairs[m >> 1] + own

    def near_copy(self, m, step):
        to = lax.rem(self.p.x + step, self.p.s.nx)
        source = self.source(self.piece(m)) if self.pairs is None else self.pairs.at[m >> 1]
        at = (step - 1, self.at(m))
        return remote(
            source.at[to], self.near.at[at], self.near_send.at[at], self.near_recv.at[at], self.p.along_x(step)
        )

    def start(self, m):
        for step in range(1, self.p.s.nx):
            self.near_copy(m, step).start()

    def join(self, m, own=None):
        value = self.pairs[m >> 1, self.p.x] if own is None else own
        for step in range(1, self.p.s.nx):
            self.near_copy(m, step).wait_recv()
            value = value + self.near[step - 1, self.at(m)]
        self.near[0, self.at(m)] = value

    def far_copy(self, m, bit):
        nz = self.p.s.nz
        slot = (nz >> self.first_bit) - (nz >> bit) + (m >> (bit + 1))
        return slot, remote(
            self.near.at[0, self.at(m)], self.far.at[slot], self.far_send.at[slot], self.far_recv.at[slot], self.to_z(bit)
        )

    def settle(self, m):
        for bit in range(self.first_bit, self.bits):
            slot, copy = self.far_copy(m, bit)
            if (m >> bit) & 1:
                copy.start()
                return
            copy.wait_recv()
            self.near[0, self.at(m)] = self.near[0, self.at(m)] + self.far[slot]

    def total(self):
        return self.near[0, 0]

    def sent(self):
        if self.pairs is not None:
            for m in self.odd:
                for x in range(self.p.s.nx):
                    self.pair_copy(m, x).wait_send()
        for m in self.order:
            for step in range(1, self.p.s.nx):
                self.near_copy(m, step).wait_send()
            if m:
                self.far_copy(m, low_zeros(m, self.bits))[1].wait_send()


def iota(shape, axis):
    return lax.broadcasted_iota(jnp.int32, shape, axis)


def head_lanes(width, head):
    lanes = iota((1, width), 1) // HEAD
    return (lanes == head).astype(WIDE)


def only(value, lanes):
    return (value.astype(WIDE) * lanes).astype(LOW)


def block_ones(width):
    return (iota((width, width), 0) // HEAD == iota((width, width), 1) // HEAD).astype(WIDE).astype(LOW)


def over_heads(product, ones):
    high = product.astype(LOW)
    rest = (product - high.astype(WIDE)).astype(LOW)
    return dot(high, ones) + dot(rest, ones)


def same_head():
    return iota((LANES, LANES), 0) // HEAD == iota((LANES, LANES), 1) // HEAD


def write_message(s, message, state, total, label):
    same = same_head()
    for tile in range(s.tiles):
        first = 2 * tile * LANES
        block = jnp.where(same, state[first : first + LANES, first : first + LANES], 0.0)
        if 2 * tile + 1 < s.pairs:
            second = first + LANES
            more = jnp.where(same, state[second : second + LANES, second : second + LANES], 0.0)
            block = block + pltpu.roll(more, HEAD, 1)
        message[tile * LANES : (tile + 1) * LANES, :] = block
    at = iota((8, LANES), 0)
    tail = jnp.where(at == s.pairs, label, 0.0)
    for pair in range(s.pairs):
        tail = tail + jnp.where(at == pair, total[:, pair * LANES : (pair + 1) * LANES], 0.0)
    message[s.tiles * LANES :, :] = tail


def join_messages(place, messages, state_low, first, have_first, earlier):
    s = place.s
    tail_at = s.tiles * LANES
    label = jnp.where(have_first, messages[first, tail_at + s.pairs : tail_at + s.pairs + 1, :], -1.0)

    def one(step, carry):
        block, tail = carry
        counts = (place.row - step >= 0) if earlier else (place.row - step < 0)
        here = messages[step, tail_at + s.pairs : tail_at + s.pairs + 1, :]
        weight = jnp.where(counts, (here == label).astype(WIDE), 0.0)
        return (
            block + messages[step, 0:tail_at, :] * weight,
            tail + messages[step, tail_at : tail_at + 8, :] * weight,
        )

    start = (jnp.zeros((tail_at, LANES), WIDE), jnp.zeros((8, LANES), WIDE))
    block, tail = lax.fori_loop(1, s.rows, one, start)
    same = same_head()
    state_low[...] = jnp.zeros_like(state_low)
    for tile in range(s.tiles):
        part = block[tile * LANES : (tile + 1) * LANES]
        first_at = 2 * tile * LANES
        state_low[first_at : first_at + LANES, first_at : first_at + LANES] = jnp.where(same, part, 0.0).astype(LOW)
        if 2 * tile + 1 < s.pairs:
            at = first_at + LANES
            more = pltpu.roll(jnp.where(same, 0.0, part), HEAD, 1)
            state_low[at : at + LANES, at : at + LANES] = more.astype(LOW)
    total = jnp.concatenate([tail[pair : pair + 1] for pair in range(s.pairs)], axis=1)
    return total, label[:, 0:1]


def send_messages(place, messages, send, receive):
    for step in range(1, place.s.rows):
        remote(
            messages.at[0], messages.at[step], send.at[step], receive.at[step], place.along_rows(step)
        ).start()


def take_messages(place, messages, send, receive):
    for step in range(1, place.s.rows):
        copy = remote(messages.at[0], messages.at[step], send.at[step], receive.at[step], place.along_rows(step))
        copy.wait()


def spread_labels(s, crop_ids, labels_across, labels_down):
    for k in range(s.chunks):
        labels = crop_ids[k].astype(WIDE)
        labels_across[k] = labels
        labels_down[k * s.chunk : (k + 1) * s.chunk, :] = jnp.broadcast_to(labels, (LANES, s.chunk)).T


def block_mask(s, labels_down, labels_across, i, j, turned):
    shape = (s.chunk, s.chunk)
    down, across = iota(shape, 0), iota(shape, 1)
    if turned:
        ordered = (i * s.chunk + across) >= (j * s.chunk + down)
        equal = labels_down[chunk_rows(s, j), 0:1] == labels_across[i]
    else:
        ordered = (i * s.chunk + down) >= (j * s.chunk + across)
        equal = labels_down[chunk_rows(s, i), 0:1] == labels_across[j]
    return jnp.where(ordered & equal, 1.0, 0.0)


def chunk_rows(s, k):
    return pl.ds(pl.multiple_of(k * s.chunk, s.chunk), s.chunk)


def forward_kernel(
    s,
    pixels,
    crop_ids,
    first_gain,
    query_weight,
    key_weight,
    value_weight,
    out_weight,
    second_gain,
    up_source,
    down_source,
    cotangent_source,
    hidden_low,
    hidden_share,
    gradient_share,
    pixel_share,
    gain_part,
    prefix_low,
    latest,
    near_two,
    first_out,
    normed_out,
    query_out,
    key_out,
    values_out,
    attended_out,
    denominator_out,
    key_sum_out,
    wide_gradient,
    normed,
    query_feature,
    key_feature,
    values,
    attended,
    denominator,
    key_sum,
    up_weight,
    down_weight,
    cotangent,
    labels_across,
    labels_down,
    gathered,
    wide_rows,
    weight_full,
    joined,
    hidden,
    normed_again,
    upward_low,
    middle,
    parts,
    near,
    far,
    messages,
    state,
    total,
    ones,
    staging,
    first_gradient,
    first_near,
    first_far,
    load_sem,
    save_sem,
    staging_sem,
    weight_y_send,
    weight_y_recv,
    weight_x_send,
    weight_x_recv,
    weight_c_send,
    weight_c_recv,
    att_send,
    att_recv,
    low_send,
    low_recv,
    message_send,
    message_recv,
    near_send,
    near_recv,
    far_send,
    far_recv,
    two_send,
    two_recv,
    first_near_send,
    first_near_recv,
    first_far_send,
    first_far_recv,
):
    p = Place(s)
    loads = [
        pltpu.make_async_copy(source, target, load_sem.at[i])
        for i, (source, target) in enumerate(
            ((up_source, up_weight), (down_source, down_weight), (cotangent_source, cotangent))
        )
    ]
    saves = [
        pltpu.make_async_copy(source, target, save_sem.at[i])
        for i, (source, target) in enumerate(
            (
                (normed, normed_out),
                (query_feature, query_out),
                (key_feature, key_out),
                (values, values_out),
                (attended, attended_out),
                (denominator, denominator_out),
                (key_sum, key_sum_out),
            )
        )
    ]
    own_rows = pl.ds(pl.multiple_of(p.head * s.width, s.width), s.width)
    wide_rows[own_rows, :] = out_weight[...].astype(WIDE)
    p.meet()
    weights = WeightGather(
        p, wide_rows, (weight_y_send, weight_y_recv, weight_x_send, weight_x_recv, weight_c_send, weight_c_recv)
    )
    weights.start()
    for load in loads:
        load.start()

    spread_labels(s, crop_ids, labels_across, labels_down)
    last = labels_across[s.chunks - 1][:, s.chunk - 1 : s.chunk]
    state[...] = jnp.zeros_like(state)
    total[...] = jnp.zeros_like(total)
    ones[...] = block_ones(s.width)

    @pl.loop(0, s.chunks)
    def _(k):
        at = chunk_rows(s, k)
        unit, scale = normalise(pixels[k].reshape(s.chunk, s.model).astype(WIDE))
        low = (unit * first_gain[...]).astype(LOW)
        normed[at, :] = low
        for weight, out in ((query_weight, query_feature), (key_weight, key_feature)):
            raw = dot(low, weight[...])
            out[at, :] = jnp.where(raw > 0, raw + 1.0, jnp.exp(jnp.minimum(raw, 0.0))).astype(LOW)
        values[at, :] = dot(low, value_weight[...]).astype(LOW)
        ending = (labels_down[at, 0:1] == last).astype(WIDE)
        kept = key_feature[at, :].astype(WIDE) * ending
        state[...] += dot_left(kept.astype(LOW), values[at, :])
        total[0:1, :] += jnp.sum(kept, axis=0, keepdims=True)

    write_message(s, messages.at[0], state, total[0:1, :], last)
    send_messages(p, messages, message_send, message_recv)
    for save in saves[:4]:
        save.start()
    weights.pass_x(0)

    @pl.loop(0, s.chunks)
    def _(i):
        at = chunk_rows(s, i)
        attended[at, :] = jnp.zeros((s.chunk, s.width), WIDE)
        key_sum[at, :] = jnp.zeros((s.chunk, s.width), WIDE)

        def over(j, carry):
            to = chunk_rows(s, j)
            mask = block_mask(s, labels_down, labels_across, i, j, False)
            key_sum[at, :] += dot(mask.astype(LOW), key_feature[to, :])
            numerator = attended[at, :]
            for head in range(s.here):
                lanes = head_lanes(s.width, head)
                scores = dot_right(only(query_feature[at, :], lanes), key_feature[to, :])
                numerator = numerator + dot((scores * mask).astype(LOW), only(values[to, :], lanes))
            attended[at, :] = numerator
            return carry

        lax.fori_loop(0, i + 1, over, 0)

    weights.pass_x(1)
    take_messages(p, messages, message_send, message_recv)
    prefix_total, label = join_messages(p, messages, prefix_low, 1, p.row > 0, True)
    latest[...] = jnp.broadcast_to(label, latest.shape)

    attention = Gather(p, lambda g, k: gathered.at[g, k], att_send, att_recv)

    @pl.loop(0, s.chunks)
    def _(i):
        at = chunk_rows(s, i)
        matching = (labels_down[at, 0:1] == latest[0:1, 0:1]).astype(WIDE)
        query = query_feature[at, :].astype(WIDE)
        numerator = attended[at, :] + dot((query * matching).astype(LOW), prefix_low[...])
        sums = key_sum[at, :] + matching * prefix_total
        key_sum[at, :] = sums
        below = over_heads(query * sums, ones[...])
        denominator[at, :] = below
        value = numerator / below
        attended[at, :] = value
        gathered[p.head, i] = value.astype(LOW).astype(WIDE)
        attention.start(i)

    for save in saves[4:]:
        save.start()
    weights.pass_core()
    weights.finish()
    for group in range(s.heads):
        rows = slice(group * s.width, (group + 1) * s.width)
        weight_full[rows, :] = wide_rows[rows, :].astype(LOW)
    weights.sent()
    attention.forward(0)
    for load in loads:
        load.wait()

    def low_rows(g, k):
        start = k * s.chunk + (lax.rem(g, 2) * s.ny + g // 2) * s.sub
        return pl.ds(pl.multiple_of(start, s.sub), s.sub)

    hidden_gather = Gather(p, lambda g, k: wide_rows.at[low_rows(g, k)], low_send, low_recv)
    reduced = Reduce(p, parts, near, far, (near_send, near_recv, far_send, far_recv))
    two = Reduce(p, parts, near_two, None, (two_send, two_recv, None, None))
    first = Halving(
        p,
        lambda piece: first_gradient.at[piece],
        first_near,
        first_far,
        (first_near_send, first_near_recv, first_far_send, first_far_recv),
    )
    order = first.order
    gain_part[...] = jnp.zeros_like(gain_part)
    shares = (2, s.ny, s.sub, TILE)

    def feed_forward(k):
        at = chunk_rows(s, k)
        attention.finish(k)
        for group in range(s.heads):
            joined[:, group * s.width : (group + 1) * s.width] = gathered[group, k].astype(LOW)
        for tile in range(s.model // TILE):
            cols = slice(tile * TILE, (tile + 1) * TILE)
            product = dot(joined[...], weight_full[:, cols])
            hidden[:, :, :, cols] = product.reshape(shares) + pixels[k, :, :, :, cols].astype(WIDE)
        hidden_share[k] = hidden[p.c, p.y]
        unit, scale = normalise(hidden[...].reshape(s.chunk, s.model))
        normed_again[at, :] = (unit * second_gain[...]).astype(LOW)

        @pl.when(k + 1 < s.chunks)
        def _():
            attention.forward(k + 1)

        low = normed_again[at, :]
        back = cotangent[k].reshape(s.chunk, s.model)
        for tile in range(s.units // TILE):
            cols = slice(tile * TILE, (tile + 1) * TILE)
            upward = dot(low, up_weight[:, cols])
            middle_back = dot_right(back, down_weight[cols, :])
            root = math.sqrt(2.0 / math.pi)
            square = upward * upward
            bent = jnp.tanh(root * upward * (1.0 + 0.044715 * square))
            half = 0.5 + 0.5 * bent
            slope = half + 0.5 * upward * (1.0 - bent * bent) * (root * (1.0 + 3.0 * 0.044715 * square))
            middle[at, cols] = (upward * half).astype(LOW)
            upward_low[at, cols] = (middle_back * slope).astype(LOW)
        low = upward_low[at, :]
        for tile in range(s.model // TILE):
            cols = slice(tile * TILE, (tile + 1) * TILE)
            parts[k, :, :, :, cols] = dot_right(low, up_weight[cols, :]).reshape(shares)
        reduced.start(k)

    def second_norm_back(k):
        grad = reduced.total(k)
        unit, scale = normalise(hidden_share[k])
        gain_part[0:1, :] += jnp.sum(grad * unit, axis=0, keepdims=True)
        part = normalise_back(unit, scale, second_gain[...], grad)
        value = cotangent[k, p.c, p.y].astype(WIDE) + part
        gradient_share[k] = value
        wide_rows[low_rows(p.head, k), :] = value.astype(LOW).astype(WIDE)
        hidden_gather.start(k)

    span = s.nx * s.cut

    def span_of(turn):
        return pl.ds(pl.multiple_of(first.piece(order[turn]) * span, span), span)

    def first_outer(turn):
        block = normed_again[:, span_of(turn)]
        target = first_gradient.at[first.piece(order[turn])]
        for at in range(0, s.first, s.step):
            cols = slice(at, at + s.step)
            target[:, :, cols] = dot_left(block, upward_low[:, cols]).reshape(s.nx, s.cut, s.step)
        first.start(order[turn])

    def first_join(turn):
        first.join(order[turn], first_gradient[first.piece(order[turn]), p.x])
        if order[turn] % 2:
            first.settle(order[turn])

    def staged(turn):
        slot = turn % 2
        return pltpu.make_async_copy(staging.at[slot], wide_gradient.at[first.piece(order[turn])], staging_sem.at[slot])

    def rest_outer(turn):
        if turn >= 2:
            staged(turn - 2).wait()
        target = staging.at[turn % 2]
        block = normed_again[:, span_of(turn)]
        for at in range(s.first, s.units, s.step):
            cols = slice(at - s.first, at - s.first + s.step)
            value = dot_left(block, upward_low[:, at : at + s.step])
            target[:, :, cols] = value.reshape(s.nx, s.cut, s.step)
        block = cotangent[:, :, :, :, span_of(turn)].reshape(s.tokens, span)
        for at in range(0, s.units, TILE):
            cols = slice(s.units - s.first + at, s.units - s.first + at + TILE)
            value = dot_left(block, middle[:, at : at + TILE])
            target[:, :, cols] = value.reshape(s.nx, s.cut, TILE)
        staged(turn).start()

    @pl.loop(0, s.chunks)
    def _(k):
        feed_forward(k)

        @pl.when(k >= 1)
        def _():
            reduced.middle(k - 1)

    end = s.chunks
    first_outer(0)
    reduced.middle(end - 1)
    for turn in range(1, s.nz):
        first_outer(turn)
    for k in range(end - 2):
        second_norm_back(k)
    rest_outer(0)
    for k in range(end - 2, end):
        second_norm_back(k)
        first_join(k - end + 2)
        rest_outer(k - end + 3)
    first.settle(order[1])
    for turn in range(3, s.nz):
        rest_outer(turn)

    @pl.loop(0, s.chunks)
    def _(k):
        reduced.near_sent(k)
        low = middle[chunk_rows(s, k), :]
        for tile in range(s.model // TILE):
            cols = slice(tile * TILE, (tile + 1) * TILE)
            parts[k, :, :, :, cols] = dot(low, down_weight[:, cols]).reshape(shares)
        two.start(k)

    for turn in range(2, s.nz - 1):
        first_join(turn)
        if order[turn] % 2 == 0:
            first.settle(order[turn])
    for k in range(end - 2):
        hidden_gather.forward(k)
    for k in range(s.chunks):
        two.join(k)
        pixel_share[k] = pixels[k, p.c, p.y]
    first_join(s.nz - 1)
    hidden_gather.forward(end - 2)
    first.settle(0)
    hidden_gather.forward(end - 1)

    for k in range(s.chunks):
        hidden_gather.finish(k)
        rows = slice(k * s.chunk, (k + 1) * s.chunk)
        hidden_low[rows, :] = wide_rows[rows, :].astype(LOW)
    first_out[...] = first.total()
    first.sent()
    for turn in range(max(0, s.nz - 2), s.nz):
        staged(turn).wait()
    for k in range(s.chunks):
        attention.sent(k)
        hidden_gather.sent(k)
        reduced.far_sent(k)
        two.near_sent(k)
    for save in saves:
        save.wait()


def backward_kernel(
    s,
    crop_ids,
    gain_part,
    prefix_low,
    latest,
    first_gain,
    near_two,
    normed_source,
    hidden_source,
    gradient_source,
    pixel_source,
    wide_gradient,
    query_feature_source,
    key_feature_source,
    values_source,
    attended_source,
    denominator_source,
    key_sum_source,
    hidden_low_source,
    query_weight_source,
    key_weight_source,
    value_weight_source,
    out_weight_source,
    gains,
    wide_out,
    narrow_out,
    pixel_out,
    result_out,
    query_feature,
    key_feature,
    values,
    attended,
    denominator,
    key_sum,
    hidden_low,
    query_weight,
    key_weight,
    value_weight,
    out_weight,
    normed,
    hidden_share,
    gradient_share,
    pixel_share,
    two_own,
    labels_across,
    labels_down,
    parts,
    far_two,
    near_four,
    far_four,
    result_wide,
    result_low,
    pixel_gradient,
    numerator_low,
    denominator_back,
    spread_back,
    query_back,
    key_back,
    value_back,
    narrow_low,
    suffix_low,
    state,
    total,
    ones,
    messages,
    narrow_gradient,
    own_wide,
    own_pairs,
    near_wide,
    far_wide,
    near_split,
    far_split,
    pairs_split,
    near_narrow,
    far_narrow,
    gain_heads,
    gain_x,
    gain_z,
    load_sem,
    input_sem,
    message_send,
    message_recv,
    two_far_send,
    two_far_recv,
    four_near_send,
    four_near_recv,
    four_far_send,
    four_far_recv,
    result_send,
    result_recv,
    pixel_send,
    pixel_recv,
    wide_near_send,
    wide_near_recv,
    wide_far_send,
    wide_far_recv,
    split_near_send,
    split_near_recv,
    split_far_send,
    split_far_recv,
    split_send,
    split_recv,
    narrow_near_send,
    narrow_near_recv,
    narrow_far_send,
    narrow_far_recv,
    gain_send,
    gain_recv,
    own_sem,
    pairs_sem,
    result_sem,
    pixel_sem,
):
    p = Place(s)
    inputs = [
        pltpu.make_async_copy(source, target, input_sem.at[i])
        for i, (source, target) in enumerate(
            (
                (hidden_low_source, hidden_low),
                (out_weight_source, out_weight),
                (denominator_source, denominator),
                (attended_source, attended),
                (query_feature_source, query_feature),
                (key_feature_source, key_feature),
                (values_source, values),
                (key_sum_source, key_sum),
                (query_weight_source, query_weight),
                (key_weight_source, key_weight),
                (value_weight_source, value_weight),
            )
        )
    ]
    for load in inputs:
        load.start()
    p.meet()
    two = Reduce(p, None, near_two, far_two, (None, None, two_far_send, two_far_recv))
    four = Reduce(p, parts, near_four, far_four, (four_near_send, four_near_recv, four_far_send, four_far_recv))
    wide = Halving(
        p,
        lambda piece: wide_gradient.at[piece, :, :, s.split :],
        near_wide,
        far_wide,
        (wide_near_send, wide_near_recv, wide_far_send, wide_far_recv),
    )
    split = Halving(
        p,
        lambda piece: wide_gradient.at[piece, :, :, 0 : s.split],
        near_split,
        far_split,
        (split_near_send, split_near_recv, split_far_send, split_far_recv),
        pairs_split,
        (split_send, split_recv),
    )
    sides = (slice(0, s.narrow // 2), slice(s.narrow // 2, s.narrow))

    def narrow_job(i):
        sems = (narrow_near_send.at[i], narrow_near_recv.at[i], narrow_far_send.at[i], narrow_far_recv.at[i])
        return Halving(
            p, lambda piece: narrow_gradient.at[piece, :, :, sides[i]], near_narrow.at[i], far_narrow.at[i], sems
        )

    narrow = (narrow_job(0), narrow_job(1))
    jobs = (wide, split) + narrow
    whole_wide = [(wide, m) for m in wide.order]
    whole_split = [(split, m) for m in split.order]
    whole_narrow = [(job, m) for job in narrow for m in job.order]
    steps = whole_wide + whole_split[:1] + whole_narrow[:1] + whole_split[1:] + whole_narrow[1:]
    flight = {"next": 0, "taken": 0}
    ready = list(whole_wide)
    pending = []

    def push(limit):
        while flight["next"] <= min(limit, len(steps) - 1) and steps[flight["next"]] in ready:
            job, m = steps[flight["next"]]
            job.start(m)
            flight["next"] += 1

    def admit(entries):
        ready.extend(entries)
        push(flight["taken"] + AHEAD - 1)

    def settle_ready(at):
        for entry in list(pending):
            if entry[0] <= at:
                entry[1].settle(entry[2])
                pending.remove(entry)

    def own_load(turn):
        source = wide_gradient.at[wide.piece(wide.order[turn]), p.x, :, s.split :]
        return pltpu.make_async_copy(source, own_wide.at[turn % 2], own_sem.at[turn % 2])

    def pairs_load(m):
        source = wide_gradient.at[split.piece(m), :, :, 0 : s.split]
        return pltpu.make_async_copy(source, own_pairs.at[m >> 1], pairs_sem.at[m >> 1])

    def take():
        at = flight["taken"]
        assert flight["next"] > at
        job, m = steps[at]
        flight["taken"] = at + 1
        if job is wide:
            own_load(at).wait()
            wide.join(m, own_wide[at % 2])
            if at + 2 < s.nz:
                own_load(at + 2).start()
        elif job is split:
            split.join(m)
        else:
            job.join(m, narrow_gradient[job.piece(m), p.x, :, sides[narrow.index(job)]])
        push(at + AHEAD)
        if (m >> job.first_bit) & 1:
            job.settle(m)
        else:
            pending.append((at + 2 if m else at + 4, job, m))
        settle_ready(at)

    def take_while(*names):
        while flight["taken"] < len(steps) and steps[flight["taken"]][0] in names:
            take()

    pair_copies = [(m, x) for m in split.odd for x in range(s.nx)]
    split.pair_copy(*pair_copies[0]).start()
    push(0)
    for k in range(s.chunks):
        two.spread(k)
    loads = [
        pltpu.make_async_copy(source, target, load_sem.at[i])
        for i, (source, target) in enumerate(
            (
                (near_two.at[:, p.y], two_own),
                (hidden_source, hidden_share),
                (gradient_source, gradient_share),
                (pixel_source, pixel_share),
                (normed_source, normed),
            )
        )
    ]
    for load in loads:
        load.start()
    own_load(0).start()
    own_load(1).start()
    for m in split.order:
        pairs_load(m).start()
    result_gather = Gather(p, lambda g, k: result_wide.at[k, lax.rem(g, 2), g // 2], result_send, result_recv)
    pixel_gather = Gather(p, lambda g, k: pixel_gradient.at[k, lax.rem(g, 2), g // 2], pixel_send, pixel_recv)
    shares = (2, s.ny, s.sub, TILE)
    spread_labels(s, crop_ids, labels_across, labels_down)
    first = labels_across[0][:, 0:1]
    state[...] = jnp.zeros_like(state)
    total[...] = jnp.zeros_like(total)
    ones[...] = block_ones(s.width)

    for load in inputs:
        load.wait()

    @pl.loop(0, s.chunks)
    def _(k):
        at = chunk_rows(s, k)
        back = dot_right(hidden_low[at, :], out_weight[...])
        below = denominator[at, :]
        low = (back / below).astype(LOW)
        numerator_low[at, :] = low
        slope = -over_heads(back * attended[at, :], ones[...]) / below
        denominator_back[at, :] = slope
        query = query_feature[at, :].astype(WIDE)
        spread = slope * query
        spread_back[at, :] = spread.astype(LOW)
        leading = (labels_down[at, 0:1] == first).astype(WIDE)
        state[...] += dot_left((query * leading).astype(LOW), low)
        total[0:1, :] += jnp.sum(spread * leading, axis=0, keepdims=True)

    write_message(s, messages.at[0], state, total[0:1, :], first)
    send_messages(p, messages, message_send, message_recv)
    for entry in pair_copies[1 : s.nx]:
        split.pair_copy(*entry).start()
    push(1)

    @pl.loop(0, s.chunks)
    def _(i):
        at = chunk_rows(s, i)
        query_back[at, :] = denominator_back[at, :] * key_sum[at, :]

        def over(j, carry):
            to = chunk_rows(s, j)
            mask = block_mask(s, labels_down, labels_across, i, j, False)
            value = query_back[at, :]
            for head in range(s.here):
                lanes = head_lanes(s.width, head)
                scores = dot_right(only(numerator_low[at, :], lanes), values[to, :])
                value = value + dot((scores * mask).astype(LOW), only(key_feature[to, :], lanes))
            query_back[at, :] = value
            return carry

        lax.fori_loop(0, i + 1, over, 0)

    take()
    for entry in pair_copies[s.nx :]:
        split.pair_copy(*entry).start()

    @pl.loop(0, s.chunks)
    def _(j):
        to = chunk_rows(s, j)
        key_back[to, :] = jnp.zeros((s.chunk, s.width), WIDE)
        value_back[to, :] = jnp.zeros((s.chunk, s.width), WIDE)

        def over(i, carry):
            at = chunk_rows(s, i)
            mask = block_mask(s, labels_down, labels_across, i, j, True)
            key_value = key_back[to, :] + dot(mask.astype(LOW), spread_back[at, :])
            value_value = value_back[to, :]
            for head in range(s.here):
                lanes = head_lanes(s.width, head)
                back = dot_right(only(values[to, :], lanes), numerator_low[at, :])
                key_value = key_value + dot((back * mask).astype(LOW), only(query_feature[at, :], lanes))
                scores = dot_right(only(key_feature[to, :], lanes), query_feature[at, :])
                value_value = value_value + dot((scores * mask).astype(LOW), only(numerator_low[at, :], lanes))
            key_back[to, :] = key_value
            value_back[to, :] = value_value
            return carry

        lax.fori_loop(j, s.chunks, over, 0)

    for load in loads:
        load.wait()

    @pl.loop(0, s.chunks)
    def _(k):
        value = hidden_share[k] + two.total(k, two_own[k])
        result_wide[k, p.c, p.y] = value.astype(LOW).astype(WIDE)

        @pl.when(k < s.chunks // 2)
        def _():
            result_gather.start(k)

    take()
    take_messages(p, messages, message_send, message_recv)
    suffix_total, following = join_messages(p, messages, suffix_low, s.rows - 1, p.row < s.rows - 1, False)

    @pl.loop(0, s.chunks)
    def _(k):
        at = chunk_rows(s, k)
        matching = (labels_down[at, 0:1] == latest[0:1, 0:1]).astype(WIDE)
        later = (labels_down[at, 0:1] == following).astype(WIDE)
        query, key = query_feature[at, :], key_feature[at, :]
        value = query_back[at, :] + matching * dot_right(numerator_low[at, :], prefix_low[...])
        low = (value * jnp.minimum(query.astype(WIDE), 1.0)).astype(LOW)
        numerator_value = value_back[at, :] + later * dot(key, suffix_low[...])
        key_value = key_back[at, :] + later * (dot_right(values[at, :], suffix_low[...]) + suffix_total)
        key_low = (key_value * jnp.minimum(key.astype(WIDE), 1.0)).astype(LOW)
        value_low = numerator_value.astype(LOW)
        narrow_low[0, at, :] = low
        narrow_low[1, at, :] = key_low
        narrow_low[2, at, :] = value_low
        for tile in range(s.model // TILE):
            cols = slice(tile * TILE, (tile + 1) * TILE)
            product = (
                dot_right(low, query_weight[cols, :])
                + dot_right(key_low, key_weight[cols, :])
                + dot_right(value_low, value_weight[cols, :])
            )
            parts[k, :, :, :, cols] = product.reshape(shares)
        four.start(k)

    @pl.loop(0, s.chunks)
    def _(k):
        four.middle(k)

    for k in range(s.chunks // 2, s.chunks):
        result_gather.start(k)
    take()

    def split_ready(m):
        pairs_load(m).wait()
        split.join_pair(m, own_pairs[m >> 1])
        admit([(split, m)])

    split_ready(split.order[0])
    span = s.nx * s.cut
    for piece in range(s.nz):
        cols = slice(piece * span, (piece + 1) * span)
        shape = (s.nx, s.cut, s.width)
        product = dot_left(hidden_low[:, cols], attended[...].astype(LOW))
        narrow_gradient[piece, :, :, 0 : s.width] = product.reshape(shape)
        for part in range(3):
            product = dot_left(normed[:, cols], narrow_low[part])
            narrow_gradient[piece, :, :, (part + 1) * s.width : (part + 2) * s.width] = product.reshape(shape)
    admit(whole_narrow)
    take_while(wide)
    for m in split.order[1:]:
        split_ready(m)
    gain_x[0] = gain_part[...]

    def take_until_left(count):
        while len(steps) - flight["taken"] > count:
            take()

    def result_copy(k):
        rows = pl.ds(k * s.chunk, s.chunk)
        return pltpu.make_async_copy(result_low.at[rows], result_out.at[rows], result_sem.at[k])

    def pixel_copy(k):
        return pltpu.make_async_copy(pixel_gradient.at[k], pixel_out.at[k], pixel_sem.at[k])

    def first_norm_back(k):
        grad = four.total(k)
        unit, scale = normalise(pixel_share[k].astype(WIDE))
        gain_x[0, 1:2, :] += jnp.sum(grad * unit, axis=0, keepdims=True)
        pixel_gradient[k, p.c, p.y] = gradient_share[k] + normalise_back(unit, scale, first_gain[...], grad)
        pixel_gather.start(k)

    first_norm_back(0)
    take()
    for k in range(1, s.chunks - 1):
        first_norm_back(k)
        take_while(split)
    take_until_left(2 * s.nz - 1)
    first_norm_back(s.chunks - 1)

    def gain_copies(index, buffer, device):
        return [
            remote(buffer.at[0], buffer.at[step], gain_send.at[index, step], gain_recv.at[index, step], device(step))
            for step in range(1, buffer.shape[0])
        ]

    def gain_start(*what):
        for copy in gain_copies(*what):
            copy.start()

    def gain_total(*what):
        for copy in gain_copies(*what):
            copy.wait()
        value = what[1][0]
        for step in range(1, what[1].shape[0]):
            value = value + what[1][step]
        return value

    rounds = (
        (0, gain_x, p.along_x),
        (1, gain_z, p.along_z),
        (2, gain_heads, p.along_heads),
    )
    gain_start(*rounds[0])
    for k in range(s.chunks // 2):
        result_gather.forward(k)
    take_until_left(2 * s.nz - 3)
    for k in range(s.chunks // 2, s.chunks):
        result_gather.forward(k)
    gain_z[0] = gain_total(*rounds[0])
    gain_start(*rounds[1])
    for k in range(s.chunks // 2):
        pixel_gather.forward(k)
    take_until_left(3)
    gain_heads[0] = gain_total(*rounds[1])
    gain_start(*rounds[2])
    for k in range(s.chunks // 2, s.chunks):
        pixel_gather.forward(k)
    take_until_left(2)
    for k in range(s.chunks):
        pixel_gather.finish(k)
        pixel_copy(k).start()
    for k in range(s.chunks):
        result_gather.finish(k)
        result_low[k * s.chunk : (k + 1) * s.chunk, :] = result_wide[k].reshape(s.chunk, s.model).astype(LOW)
        result_copy(k).start()
    gains[...] = gain_total(*rounds[2])
    take_until_left(0)
    settle_ready(len(steps) + 4)
    wide_out[:, s.split :] = wide.total()
    wide_out[:, 0 : s.split] = split.total()
    for job, side in zip(narrow, sides):
        narrow_out[:, side] = job.total()
    for k in range(s.chunks):
        result_copy(k).wait()
        pixel_copy(k).wait()
        pixel_gather.sent(k)
        result_gather.sent(k)
        two.far_sent(k)
        four.near_sent(k)
        four.far_sent(k)
    for job in jobs:
        job.sent()


def finish_kernel(
    s,
    gains,
    first_source,
    wide_source,
    narrow_source,
    pixel_source,
    result_source,
    first_gain,
    second_gain,
    up_gradient,
    down_gradient,
    out_gradient,
    query_gradient,
    key_gradient,
    value_gradient,
    pixel_gradient,
    result,
    pixel_rows,
    result_rows,
    first_out,
    wide_out,
    narrow_out,
    down_turned,
    out_turned,
    read_sem,
    write_sem,
    small_sem,
):
    row = lax.axis_index("rows")
    rest = s.units - s.first

    def places(i, k):
        rows = pl.ds(k * s.chunk, s.chunk)
        if i == 0:
            return pixel_source.at[k], pixel_rows.at[k], pixel_gradient.at[k]
        return result_source.at[rows], result_rows.at[rows], result.at[rows]

    def read(i, k):
        source, between, unused = places(i, k)
        return pltpu.make_async_copy(source, between, read_sem.at[i, k])

    def write(i, k):
        unused, between, target = places(i, k)
        return pltpu.make_async_copy(between, target, write_sem.at[i, k])

    def small(at, source, target):
        return pltpu.make_async_copy(source, target, small_sem.at[at])

    reads = [
        small(0, wide_source, wide_out),
        small(1, narrow_source, narrow_out),
        small(2, first_source, first_out),
    ]
    moves = [(i, k) for k in range(s.chunks) for i in range(2)]
    for copy in reads:
        copy.start()
    for move in moves:
        read(*move).start()
    own = jnp.zeros((8, s.cut), WIDE)
    for at in range(s.rows):
        own = own + jnp.where(row == at, gains[:, at * s.cut : (at + 1) * s.cut], 0.0)
    second_gain[...] = own[0:1]
    first_gain[...] = own[1:2]
    for copy in reads:
        copy.wait()
    writes = [
        small(3, first_out, up_gradient.at[:, 0 : s.first]),
        small(4, wide_out.at[:, 0:rest], up_gradient.at[:, s.first :]),
    ]
    for i, target in enumerate((query_gradient, key_gradient, value_gradient)):
        writes.append(small(5 + i, narrow_out.at[:, (i + 1) * s.width : (i + 2) * s.width], target))
    for copy in writes:
        copy.start()
    down_turned[...] = wide_out[:, rest:].T
    out_turned[...] = narrow_out[:, 0 : s.width].T
    for at, source, target in ((8, down_turned, down_gradient), (9, out_turned, out_gradient)):
        writes.append(small(at, source, target))
        writes[-1].start()
    for move in moves:
        read(*move).wait()
        write(*move).start()
    for move in moves:
        write(*move).wait()
    for copy in writes:
        copy.wait()


def vmem(count):
    return [pl.BlockSpec(memory_space=pltpu.VMEM)] * count


def dma(*shape):
    return pltpu.SemaphoreType.DMA(shape)


def on_device(
    rows,
    heads,
    pixels,
    crop_ids,
    first_gain,
    query_weight,
    key_weight,
    value_weight,
    out_weight,
    second_gain,
    up_weight,
    down_weight,
    cotangent,
):
    tokens, model = pixels.shape
    s = Sizes(rows, heads, tokens, model, query_weight.shape[1], up_weight.shape[1])
    whole = (s.chunks, 2, s.ny, s.sub, model)
    share = (s.chunks, s.sub, model)
    labels = crop_ids.reshape(s.chunks, 1, s.chunk)
    shape = jax.ShapeDtypeStruct
    any_space = pl.BlockSpec(memory_space=pl.ANY)

    def reduce_sems():
        return [
            dma(s.chunks),
            dma(s.chunks),
            dma(s.ny - 1, s.chunks),
            dma(s.ny - 1, s.chunks),
        ]

    def gather_sems():
        return [dma(2 * s.ny - 1, s.chunks), dma(heads, s.chunks)]

    def scatter_sems():
        return [
            dma(s.nx - 1, s.nz),
            dma(s.nx - 1, s.nz),
            dma(s.nz - 1),
            dma(s.nz - 1),
        ]

    def scatter_buffers(width, pieces=s.nz):
        return [
            pltpu.VMEM((s.nx - 1, pieces, s.cut, width), WIDE),
            pltpu.VMEM((pieces - 1, s.cut, width), WIDE),
        ]

    half = s.nz // 2

    lows = [(tokens, model)] + [(tokens, s.width)] * 3
    wides = [(tokens, s.width)] * 3
    near = (s.chunks, s.ny, s.sub, model)
    far = (s.ny - 1,) + share
    label_buffers = [
        pltpu.VMEM((s.chunks, 1, s.chunk), WIDE),
        pltpu.VMEM((tokens, LANES), WIDE),
    ]
    outs = [
        shape((tokens, model), LOW),
        shape(share, WIDE),
        shape(share, WIDE),
        shape(share, LOW),
        shape((8, model), WIDE),
        shape((s.width, s.width), LOW),
        shape((8, LANES), WIDE),
        shape(near, WIDE),
        shape((s.cut, s.first), WIDE),
        *[shape(size, LOW) for size in lows],
        *[shape(size, WIDE) for size in wides],
        shape((s.nz, s.nx, s.cut, s.wide), WIDE),
    ]
    shared = WeightGather.halves
    (
        hidden_low,
        hidden_share,
        gradient_share,
        pixel_share,
        gain_part,
        prefix_low,
        latest,
        near_two,
        first_out,
        normed,
        query_feature,
        key_feature,
        values,
        attended,
        denominator,
        key_sum,
        wide_gradient,
    ) = pl.pallas_call(
        functools.partial(forward_kernel, s),
        out_shape=outs,
        in_specs=vmem(8) + [any_space] * 3,
        out_specs=vmem(9) + [any_space] * 8,
        scratch_shapes=[
            *[pltpu.VMEM(size, LOW) for size in lows],
            *[pltpu.VMEM(size, WIDE) for size in wides],
            pltpu.VMEM((model, s.units), LOW),
            pltpu.VMEM((s.units, model), LOW),
            pltpu.VMEM(whole, LOW),
            *label_buffers,
            pltpu.VMEM((heads, s.chunks, s.chunk, s.width), WIDE),
            pltpu.VMEM((max(tokens, model), model), WIDE),
            pltpu.VMEM((model, model), LOW),
            pltpu.VMEM((s.chunk, model), LOW),
            pltpu.VMEM(whole[1:], WIDE),
            pltpu.VMEM((tokens, model), LOW),
            pltpu.VMEM((tokens, s.units), LOW),
            pltpu.VMEM((tokens, s.units), LOW),
            pltpu.VMEM(whole, WIDE),
            pltpu.VMEM(near, WIDE),
            pltpu.VMEM(far, WIDE),
            pltpu.VMEM((rows, s.message, LANES), WIDE),
            pltpu.VMEM((s.width, s.width), WIDE),
            pltpu.VMEM((8, s.width), WIDE),
            pltpu.VMEM((s.width, s.width), LOW),
            pltpu.VMEM((2, s.nx, s.cut, s.wide), WIDE),
            pltpu.VMEM((s.nz, s.nx, s.cut, s.first), WIDE),
            *scatter_buffers(s.first),
            dma(3),
            dma(7),
            dma(2),
            *[dma(s.ny - 1, shared)] * 2,
            *[dma(s.ny - 1, s.nx - 1, shared)] * 2,
            *[dma(s.ny)] * 2,
            *gather_sems(),
            *gather_sems(),
            dma(rows),
            dma(rows),
            *reduce_sems(),
            dma(s.chunks),
            dma(s.chunks),
            *scatter_sems(),
        ],
        compiler_params=pltpu.CompilerParams(
            collective_id=0, has_side_effects=True, vmem_limit_bytes=60 << 20
        ),
        name="forward_part",
    )(
        pixels.reshape(whole),
        labels,
        first_gain.reshape(1, model),
        query_weight,
        key_weight,
        value_weight,
        out_weight,
        second_gain.reshape(1, model),
        up_weight,
        down_weight,
        cotangent.reshape(whole),
    )
    outs = [
        shape((8, model), WIDE),
        shape((s.cut, s.wide), WIDE),
        shape((s.cut, s.narrow), WIDE),
        shape(whole, WIDE),
        shape((tokens, model), LOW),
    ]
    gains, wide_out, narrow_out, pixel_wide, result_low = pl.pallas_call(
        functools.partial(backward_kernel, s),
        out_shape=outs,
        in_specs=vmem(5) + [any_space] * 17,
        out_specs=vmem(3) + [any_space] * 2,
        scratch_shapes=[
            *[pltpu.VMEM(size, LOW) for size in lows[1:]],
            *[pltpu.VMEM(size, WIDE) for size in wides],
            pltpu.VMEM((tokens, model), LOW),
            *[pltpu.VMEM((model, s.width), LOW)] * 3,
            pltpu.VMEM((s.width, model), LOW),
            pltpu.VMEM((tokens, model), LOW),
            pltpu.VMEM(share, WIDE),
            pltpu.VMEM(share, WIDE),
            pltpu.VMEM(share, LOW),
            pltpu.VMEM(share, WIDE),
            *label_buffers,
            pltpu.VMEM(whole, WIDE),
            pltpu.VMEM(far, WIDE),
            pltpu.VMEM(near, WIDE),
            pltpu.VMEM(far, WIDE),
            pltpu.VMEM(whole, WIDE),
            pltpu.VMEM((tokens, model), LOW),
            pltpu.VMEM(whole, WIDE),
            pltpu.VMEM((tokens, s.width), LOW),
            pltpu.VMEM((tokens, s.width), WIDE),
            pltpu.VMEM((tokens, s.width), LOW),
            *[pltpu.VMEM((tokens, s.width), WIDE)] * 3,
            pltpu.VMEM((3, tokens, s.width), LOW),
            pltpu.VMEM((s.width, s.width), LOW),
            pltpu.VMEM((s.width, s.width), WIDE),
            pltpu.VMEM((8, s.width), WIDE),
            pltpu.VMEM((s.width, s.width), LOW),
            pltpu.VMEM((rows, s.message, LANES), WIDE),
            pltpu.VMEM((s.nz, s.nx, s.cut, s.narrow), WIDE),
            pltpu.VMEM((2, s.cut, s.wide - s.split), WIDE),
            pltpu.VMEM((half, s.nx, s.cut, s.split), WIDE),
            *scatter_buffers(s.wide - s.split),
            *scatter_buffers(s.split, half),
            pltpu.VMEM((half, s.nx, s.cut, s.split), WIDE),
            pltpu.VMEM((2, s.nx - 1, s.nz, s.cut, s.narrow // 2), WIDE),
            pltpu.VMEM((2, s.nz - 1, s.cut, s.narrow // 2), WIDE),
            pltpu.VMEM((heads, 8, model), WIDE),
            pltpu.VMEM((s.nx, 8, model), WIDE),
            pltpu.VMEM((s.nz, 8, model), WIDE),
            dma(5),
            dma(11),
            dma(rows),
            dma(rows),
            *reduce_sems()[2:],
            *reduce_sems(),
            *gather_sems(),
            *gather_sems(),
            *scatter_sems(),
            *scatter_sems(),
            dma(half, s.nx),
            dma(half, s.nx),
            *[dma(2, s.nx - 1, s.nz)] * 2,
            *[dma(2, s.nz - 1)] * 2,
            dma(3, max(heads, s.nx, s.nz)),
            dma(3, max(heads, s.nx, s.nz)),
            dma(2),
            dma(half),
            dma(s.chunks),
            dma(s.chunks),
        ],
        compiler_params=pltpu.CompilerParams(
            collective_id=1, has_side_effects=True, vmem_limit_bytes=60 << 20
        ),
        name="backward_part",
    )(
        labels,
        gain_part,
        prefix_low,
        latest,
        first_gain.reshape(1, model),
        near_two,
        normed,
        hidden_share,
        gradient_share,
        pixel_share,
        wide_gradient,
        query_feature,
        key_feature,
        values,
        attended,
        denominator,
        key_sum,
        hidden_low,
        query_weight,
        key_weight,
        value_weight,
        out_weight,
    )
    outs = [
        *[shape((1, s.cut), WIDE)] * 2,
        shape((s.cut, s.units), WIDE),
        shape((s.units, s.cut), WIDE),
        shape((s.width, s.cut), WIDE),
        *[shape((s.cut, s.width), WIDE)] * 3,
        shape(whole, WIDE),
        shape((tokens, model), LOW),
    ]
    first_part, second_part, up_part, down_part, out_part, query_part, key_part, value_part, pixel_part, result = (
        pl.pallas_call(
            functools.partial(finish_kernel, s),
            out_shape=outs,
            in_specs=vmem(1) + [any_space] * 5,
            out_specs=vmem(2) + [any_space] * 8,
            scratch_shapes=[
                pltpu.VMEM(whole, WIDE),
                pltpu.VMEM((tokens, model), LOW),
                pltpu.VMEM((s.cut, s.first), WIDE),
                pltpu.VMEM((s.cut, s.wide), WIDE),
                pltpu.VMEM((s.cut, s.narrow), WIDE),
                pltpu.VMEM((s.units, s.cut), WIDE),
                pltpu.VMEM((s.width, s.cut), WIDE),
                dma(2, s.chunks),
                dma(2, s.chunks),
                dma(10),
            ],
            compiler_params=pltpu.CompilerParams(vmem_limit_bytes=60 << 20),
            name="finish_part",
        )(gains, first_out, wide_out, narrow_out, pixel_wide, result_low)
    )
    return (
        result,
        pixel_part.reshape(tokens, model),
        first_part.reshape(s.cut),
        query_part,
        key_part,
        value_part,
        out_part,
        second_part.reshape(s.cut),
        up_part,
        down_part,
    )


def solution(mesh):
    return jax.shard_map(
        functools.partial(on_device, mesh.shape["rows"], mesh.shape["heads"]),
        mesh=mesh,
        in_specs=(
            P("rows", None),
            P("rows"),
            P(),
            P(None, "heads"),
            P(None, "heads"),
            P(None, "heads"),
            P("heads", None),
            P(),
            P(None, "heads"),
            P("heads", None),
            P("rows", None),
        ),
        out_specs=(
            P("rows", None),
            P("rows", None),
            P("rows"),
            P("rows", "heads"),
            P("rows", "heads"),
            P("rows", "heads"),
            P("heads", "rows"),
            P("rows"),
            P("rows", "heads"),
            P("heads", "rows"),
        ),
        check_vma=False,
    )
```

```python
import functools
import math

import jax
import jax.numpy as jnp
from jax import lax
from jax.experimental import pallas as pl
from jax.experimental.pallas import tpu as pltpu
from jax.sharding import PartitionSpec as P

HEAD = 64
EPSILON = 1e-05
MESH = pl.DeviceIdType.MESH
LOW = jnp.bfloat16
WIDE = jnp.float32
LANES = 128
TILE = 256
AHEAD = 2
FIRST = 6


def dot(left, right):
    return jnp.dot(left, right, preferred_element_type=WIDE)


def dot_left(left, right):
    return lax.dot_general(left, right, (((0,), (0,)), ((), ())), preferred_element_type=WIDE)


def dot_right(left, right):
    return lax.dot_general(left, right, (((1,), (1,)), ((), ())), preferred_element_type=WIDE)


def normalise(value):
    middle = jnp.mean(value, axis=-1, keepdims=True)
    centred = value - middle
    spread = jnp.mean(centred * centred, axis=-1, keepdims=True)
    scale = lax.rsqrt(spread + EPSILON)
    return centred * scale, scale


def normalise_back(unit, scale, gain, grad):
    scaled = grad * gain
    along = jnp.mean(scaled * unit, axis=-1, keepdims=True)
    return scale * (scaled - jnp.mean(scaled, axis=-1, keepdims=True) - unit * along)


class Sizes:
    def __init__(self, rows, heads, tokens, model, width, units):
        self.rows, self.heads = rows, heads
        self.ny = heads // 2
        self.nx = self.ny if rows % self.ny == 0 else 1
        self.nz = rows // self.nx
        self.tokens, self.model, self.width, self.units = tokens, model, width, units
        self.chunk = min(TILE, tokens)
        self.chunks = tokens // self.chunk
        self.sub = self.chunk // heads
        self.here = width // HEAD
        self.pairs = width // LANES
        self.tiles = (self.pairs + 1) // 2
        self.message = self.tiles * LANES + 8
        self.cut = model // rows
        self.first = units // LANES * FIRST // 8 * LANES
        self.step = TILE if self.first % TILE == 0 and units % TILE == 0 else LANES
        self.wide = 2 * units - self.first
        self.narrow = 4 * width
        self.split = round((self.wide + self.narrow) / (4 * LANES)) * LANES


class Place:
    def __init__(self, sizes):
        s = self.s = sizes
        self.row = lax.axis_index("rows")
        self.head = lax.axis_index("heads")
        self.y, self.c = self.head // 2, lax.rem(self.head, 2)
        self.x, self.z = lax.rem(self.row, s.nx), self.row // s.nx

    def other(self):
        return (self.row, self.y * 2 + 1 - self.c)

    def group(self, step):
        return lax.rem(self.y + self.s.ny - step, self.s.ny) * 2 + self.c

    def along_y(self, step):
        return (self.row, lax.rem(self.y + step, self.s.ny) * 2 + self.c)

    def along_x(self, step):
        return (self.z * self.s.nx + lax.rem(self.x + step, self.s.nx), self.head)

    def along_z(self, step):
        return (lax.rem(self.z + step, self.s.nz) * self.s.nx + self.x, self.head)

    def along_rows(self, step):
        return (lax.rem(self.row + step, self.s.rows), self.head)

    def along_heads(self, step):
        return (self.row, lax.rem(self.head + step, self.s.heads))

    def meet(self):
        barrier = pltpu.get_barrier_semaphore()
        for step in range(1, self.s.heads):
            pl.semaphore_signal(barrier, inc=1, device_id=self.along_heads(step), device_id_type=MESH)
        for step in range(1, self.s.rows):
            pl.semaphore_signal(barrier, inc=1, device_id=self.along_rows(step), device_id_type=MESH)
        pl.semaphore_wait(barrier, self.s.heads + self.s.rows - 2)


def remote(source, target, send, receive, device):
    return pltpu.make_async_remote_copy(
        src_ref=source, dst_ref=target, send_sem=send, recv_sem=receive, device_id=device, device_id_type=MESH
    )


class Gather:
    def __init__(self, place, view, send, receive, own=None):
        self.p, self.view, self.send, self.receive = place, view, send, receive
        self.own = own

    def copy(self, group, k, slot, device):
        source = self.view(group, k)
        return remote(source, self.view(group, k), self.send.at[slot, k], self.receive.at[group, k], device)

    def own_copy(self, k, slot, device):
        group = self.p.head
        source = self.view(group, k) if self.own is None else self.own(k)
        return remote(source, self.view(group, k), self.send.at[slot, k], self.receive.at[group, k], device)

    def start(self, k):
        for step in range(1, self.p.s.ny):
            self.own_copy(k, step, self.p.along_y(step)).start()
        self.own_copy(k, 0, self.p.other()).start()

    def forward(self, k):
        ny = self.p.s.ny
        for step in range(1, ny):
            group = self.p.group(step)
            self.copy(group, k, 0, self.p.along_y(step)).wait_recv()
            self.copy(group, k, ny - 1 + step, self.p.other()).start()

    def finish(self, k):
        for step in range(self.p.s.ny):
            own = self.p.group(step)
            group = own + 1 - 2 * self.p.c
            self.copy(group, k, 0, self.p.other()).wait_recv()

    def sent(self, k):
        ny = self.p.s.ny
        for step in range(ny):
            self.own_copy(k, step, self.p.other()).wait_send()
        for step in range(1, ny):
            self.copy(self.p.group(step), k, ny - 1 + step, self.p.other()).wait_send()


class WeightGather:
    halves = 2

    def __init__(self, place, rows, sems):
        self.p, self.rows = place, rows
        self.y_send, self.y_recv, self.x_send, self.x_recv, self.c_send, self.c_recv = sems
        self.size = place.s.width // (place.s.nx * self.halves)

    def share(self, group, x, half):
        start = (group * self.p.s.nx + x) * (self.size * self.halves) + half * self.size
        return self.rows.at[pl.ds(pl.multiple_of(start, self.size), self.size)]

    def slice(self, group):
        width = self.p.s.width
        return self.rows.at[pl.ds(pl.multiple_of(group * width, width), width)]

    def y_copy(self, step, half, group):
        ref = self.share(group, self.p.x, half)
        at = (step - 1, half)
        return remote(ref, ref, self.y_send.at[at], self.y_recv.at[at], self.p.along_y(step))

    def x_copy(self, step, side, half, x):
        ref = self.share(self.p.group(step), x, half)
        at = (step - 1, side - 1, half)
        return remote(ref, ref, self.x_send.at[at], self.x_recv.at[at], self.p.along_x(side))

    def c_copy(self, step, group):
        ref = self.slice(group)
        return remote(ref, ref, self.c_send.at[step], self.c_recv.at[step], self.p.other())

    def start(self):
        for half in range(self.halves):
            for step in range(1, self.p.s.ny):
                self.y_copy(step, half, self.p.head).start()
        self.c_copy(0, self.p.head).start()

    def pass_x(self, half):
        for step in range(1, self.p.s.ny):
            self.y_copy(step, half, self.p.group(step)).wait_recv()
            for side in range(1, self.p.s.nx):
                self.x_copy(step, side, half, self.p.x).start()

    def pass_core(self):
        nx = self.p.s.nx
        for step in range(1, self.p.s.ny):
            for half in range(self.halves):
                for side in range(1, nx):
                    self.x_copy(step, side, half, lax.rem(self.p.x + nx - side, nx)).wait_recv()
            self.c_copy(step, self.p.group(step)).start()

    def finish(self):
        for step in range(self.p.s.ny):
            self.c_copy(step, self.p.group(step) + 1 - 2 * self.p.c).wait_recv()

    def sent(self):
        for step in range(self.p.s.ny):
            self.c_copy(step, self.p.group(step)).wait_send()
            if step == 0:
                continue
            for half in range(self.halves):
                self.y_copy(step, half, self.p.head).wait_send()
                for side in range(1, self.p.s.nx):
                    self.x_copy(step, side, half, self.p.x).wait_send()


class Reduce:
    def __init__(self, place, parts, near, far, sems):
        self.p, self.parts, self.near, self.far = place, parts, near, far
        self.near_send, self.near_recv, self.far_send, self.far_recv = sems

    def near_copy(self, k):
        return remote(
            self.parts.at[k, 1 - self.p.c],
            self.near.at[k],
            self.near_send.at[k],
            self.near_recv.at[k],
            self.p.other(),
        )

    def far_copy(self, k, step):
        share = lax.rem(self.p.y + step, self.p.s.ny)
        return remote(
            self.near.at[k, share],
            self.far.at[step - 1, k],
            self.far_send.at[step - 1, k],
            self.far_recv.at[step - 1, k],
            self.p.along_y(step),
        )

    def start(self, k):
        self.near_copy(k).start()

    def join(self, k):
        self.near_copy(k).wait_recv()
        self.near[k] = self.near[k] + self.parts[k, self.p.c]

    def spread(self, k):
        for step in range(1, self.p.s.ny):
            self.far_copy(k, step).start()

    def middle(self, k):
        self.join(k)
        self.spread(k)

    def total(self, k, own=None):
        value = self.near[k, self.p.y] if own is None else own
        for step in range(1, self.p.s.ny):
            self.far_copy(k, step).wait_recv()
            value = value + self.far[step - 1, k]
        return value

    def near_sent(self, k):
        self.near_copy(k).wait_send()

    def far_sent(self, k):
        for step in range(1, self.p.s.ny):
            self.far_copy(k, step).wait_send()


def flipped(value, mask):
    bit = 0
    out = value
    while mask >> bit:
        if (mask >> bit) & 1:
            out = out + (1 - 2 * lax.rem(value // (1 << bit), 2)) * (1 << bit)
        bit += 1
    return out


def low_zeros(mask, count):
    return count if mask == 0 else (mask & -mask).bit_length() - 1


class Halving:
    def __init__(self, place, source, near, far, sems, pairs=None, pair_sems=None):
        self.p, self.source, self.near, self.far = place, source, near, far
        self.near_send, self.near_recv, self.far_send, self.far_recv = sems
        self.pairs, self.pair_sems = pairs, pair_sems
        self.bits = place.s.nz.bit_length() - 1
        self.first_bit = 0 if pairs is None else 1
        self.order = list(reversed(range(0, place.s.nz, 1 << self.first_bit)))
        self.odd = [m for m in reversed(range(place.s.nz)) if m % 2]

    def piece(self, m):
        return flipped(self.p.z, m)

    def to_z(self, bit):
        return (flipped(self.p.z, 1 << bit) * self.p.s.nx + self.p.x, self.p.head)

    def at(self, m):
        return m >> self.first_bit

    def pair_copy(self, m, x):
        send, receive = self.pair_sems
        at = (m >> 1, x)
        return remote(self.source(self.piece(m)).at[x], self.pairs.at[at], send.at[at], receive.at[at], self.to_z(0))

    def join_pair(self, m, own):
        for x in range(self.p.s.nx):
            self.pair_copy(m + 1, x).wait_recv()
        self.pairs[m >> 1] = self.pairs[m >> 1] + own

    def near_copy(self, m, step):
        to = lax.rem(self.p.x + step, self.p.s.nx)
        source = self.source(self.piece(m)) if self.pairs is None else self.pairs.at[m >> 1]
        at = (step - 1, self.at(m))
        return remote(
            source.at[to], self.near.at[at], self.near_send.at[at], self.near_recv.at[at], self.p.along_x(step)
        )

    def start(self, m):
        for step in range(1, self.p.s.nx):
            self.near_copy(m, step).start()

    def join(self, m, own=None):
        value = self.pairs[m >> 1, self.p.x] if own is None else own
        for step in range(1, self.p.s.nx):
            self.near_copy(m, step).wait_recv()
            value = value + self.near[step - 1, self.at(m)]
        self.near[0, self.at(m)] = value

    def far_copy(self, m, bit):
        nz = self.p.s.nz
        slot = (nz >> self.first_bit) - (nz >> bit) + (m >> (bit + 1))
        return slot, remote(
            self.near.at[0, self.at(m)], self.far.at[slot], self.far_send.at[slot], self.far_recv.at[slot], self.to_z(bit)
        )

    def settle(self, m):
        for bit in range(self.first_bit, self.bits):
            slot, copy = self.far_copy(m, bit)
            if (m >> bit) & 1:
                copy.start()
                return
            copy.wait_recv()
            self.near[0, self.at(m)] = self.near[0, self.at(m)] + self.far[slot]

    def total(self):
        return self.near[0, 0]

    def sent(self):
        if self.pairs is not None:
            for m in self.odd:
                for x in range(self.p.s.nx):
                    self.pair_copy(m, x).wait_send()
        for m in self.order:
            for step in range(1, self.p.s.nx):
                self.near_copy(m, step).wait_send()
            if m:
                self.far_copy(m, low_zeros(m, self.bits))[1].wait_send()


def iota(shape, axis):
    return lax.broadcasted_iota(jnp.int32, shape, axis)


def head_lanes(width, head):
    lanes = iota((1, width), 1) // HEAD
    return (lanes == head).astype(WIDE)


def only(value, lanes):
    return (value.astype(WIDE) * lanes).astype(LOW)


def block_ones(width):
    return (iota((width, width), 0) // HEAD == iota((width, width), 1) // HEAD).astype(WIDE).astype(LOW)


def over_heads(product, ones):
    high = product.astype(LOW)
    rest = (product - high.astype(WIDE)).astype(LOW)
    return dot(high, ones) + dot(rest, ones)


def same_head():
    return iota((LANES, LANES), 0) // HEAD == iota((LANES, LANES), 1) // HEAD


def write_message(s, message, state, total, label):
    same = same_head()
    for tile in range(s.tiles):
        first = 2 * tile * LANES
        block = jnp.where(same, state[first : first + LANES, first : first + LANES], 0.0)
        if 2 * tile + 1 < s.pairs:
            second = first + LANES
            more = jnp.where(same, state[second : second + LANES, second : second + LANES], 0.0)
            block = block + pltpu.roll(more, HEAD, 1)
        message[tile * LANES : (tile + 1) * LANES, :] = block
    at = iota((8, LANES), 0)
    tail = jnp.where(at == s.pairs, label, 0.0)
    for pair in range(s.pairs):
        tail = tail + jnp.where(at == pair, total[:, pair * LANES : (pair + 1) * LANES], 0.0)
    message[s.tiles * LANES :, :] = tail


def join_messages(place, messages, state_low, first, have_first, earlier):
    s = place.s
    tail_at = s.tiles * LANES
    label = jnp.where(have_first, messages[first, tail_at + s.pairs : tail_at + s.pairs + 1, :], -1.0)

    def one(step, carry):
        block, tail = carry
        counts = (place.row - step >= 0) if earlier else (place.row - step < 0)
        here = messages[step, tail_at + s.pairs : tail_at + s.pairs + 1, :]
        weight = jnp.where(counts, (here == label).astype(WIDE), 0.0)
        return (
            block + messages[step, 0:tail_at, :] * weight,
            tail + messages[step, tail_at : tail_at + 8, :] * weight,
        )

    start = (jnp.zeros((tail_at, LANES), WIDE), jnp.zeros((8, LANES), WIDE))
    block, tail = lax.fori_loop(1, s.rows, one, start)
    same = same_head()
    state_low[...] = jnp.zeros_like(state_low)
    for tile in range(s.tiles):
        part = block[tile * LANES : (tile + 1) * LANES]
        first_at = 2 * tile * LANES
        state_low[first_at : first_at + LANES, first_at : first_at + LANES] = jnp.where(same, part, 0.0).astype(LOW)
        if 2 * tile + 1 < s.pairs:
            at = first_at + LANES
            more = pltpu.roll(jnp.where(same, 0.0, part), HEAD, 1)
            state_low[at : at + LANES, at : at + LANES] = more.astype(LOW)
    total = jnp.concatenate([tail[pair : pair + 1] for pair in range(s.pairs)], axis=1)
    return total, label[:, 0:1]


def send_messages(place, messages, send, receive):
    for step in range(1, place.s.rows):
        remote(
            messages.at[0], messages.at[step], send.at[step], receive.at[step], place.along_rows(step)
        ).start()


def take_messages(place, messages, send, receive):
    for step in range(1, place.s.rows):
        copy = remote(messages.at[0], messages.at[step], send.at[step], receive.at[step], place.along_rows(step))
        copy.wait()


def spread_labels(s, crop_ids, labels_across, labels_down):
    for k in range(s.chunks):
        labels = crop_ids[k].astype(WIDE)
        labels_across[k] = labels
        labels_down[k * s.chunk : (k + 1) * s.chunk, :] = jnp.broadcast_to(labels, (LANES, s.chunk)).T


def block_mask(s, labels_down, labels_across, i, j, turned):
    shape = (s.chunk, s.chunk)
    down, across = iota(shape, 0), iota(shape, 1)
    if turned:
        ordered = (i * s.chunk + across) >= (j * s.chunk + down)
        equal = labels_down[chunk_rows(s, j), 0:1] == labels_across[i]
    else:
        ordered = (i * s.chunk + down) >= (j * s.chunk + across)
        equal = labels_down[chunk_rows(s, i), 0:1] == labels_across[j]
    return jnp.where(ordered & equal, 1.0, 0.0)


def chunk_rows(s, k):
    return pl.ds(pl.multiple_of(k * s.chunk, s.chunk), s.chunk)


def forward_kernel(
    s,
    pixels,
    crop_ids,
    first_gain,
    query_weight,
    key_weight,
    value_weight,
    out_weight,
    second_gain,
    up_source,
    down_source,
    cotangent_source,
    hidden_low,
    hidden_share,
    gradient_share,
    pixel_share,
    gain_part,
    prefix_low,
    latest,
    near_two,
    first_out,
    normed_out,
    query_out,
    key_out,
    values_out,
    attended_out,
    denominator_out,
    key_sum_out,
    wide_gradient,
    normed,
    query_feature,
    key_feature,
    values,
    attended,
    denominator,
    key_sum,
    up_weight,
    down_weight,
    cotangent,
    labels_across,
    labels_down,
    gathered,
    wide_rows,
    weight_full,
    joined,
    hidden,
    normed_again,
    upward_low,
    middle,
    parts,
    near,
    far,
    messages,
    state,
    total,
    ones,
    staging,
    first_gradient,
    first_near,
    first_far,
    load_sem,
    save_sem,
    staging_sem,
    weight_y_send,
    weight_y_recv,
    weight_x_send,
    weight_x_recv,
    weight_c_send,
    weight_c_recv,
    att_send,
    att_recv,
    low_send,
    low_recv,
    message_send,
    message_recv,
    near_send,
    near_recv,
    far_send,
    far_recv,
    two_send,
    two_recv,
    first_near_send,
    first_near_recv,
    first_far_send,
    first_far_recv,
):
    p = Place(s)
    loads = [
        pltpu.make_async_copy(source, target, load_sem.at[i])
        for i, (source, target) in enumerate(
            ((up_source, up_weight), (down_source, down_weight), (cotangent_source, cotangent))
        )
    ]
    saves = [
        pltpu.make_async_copy(source, target, save_sem.at[i])
        for i, (source, target) in enumerate(
            (
                (normed, normed_out),
                (query_feature, query_out),
                (key_feature, key_out),
                (values, values_out),
                (attended, attended_out),
                (denominator, denominator_out),
                (key_sum, key_sum_out),
            )
        )
    ]
    own_rows = pl.ds(pl.multiple_of(p.head * s.width, s.width), s.width)
    wide_rows[own_rows, :] = out_weight[...].astype(WIDE)
    p.meet()
    weights = WeightGather(
        p, wide_rows, (weight_y_send, weight_y_recv, weight_x_send, weight_x_recv, weight_c_send, weight_c_recv)
    )
    weights.start()
    for load in loads:
        load.start()

    spread_labels(s, crop_ids, labels_across, labels_down)
    last = labels_across[s.chunks - 1][:, s.chunk - 1 : s.chunk]
    state[...] = jnp.zeros_like(state)
    total[...] = jnp.zeros_like(total)
    ones[...] = block_ones(s.width)

    @pl.loop(0, s.chunks)
    def _(k):
        at = chunk_rows(s, k)
        unit, scale = normalise(pixels[k].reshape(s.chunk, s.model).astype(WIDE))
        low = (unit * first_gain[...]).astype(LOW)
        normed[at, :] = low
        for weight, out in ((query_weight, query_feature), (key_weight, key_feature)):
            raw = dot(low, weight[...])
            out[at, :] = jnp.where(raw > 0, raw + 1.0, jnp.exp(jnp.minimum(raw, 0.0))).astype(LOW)
        values[at, :] = dot(low, value_weight[...]).astype(LOW)
        ending = (labels_down[at, 0:1] == last).astype(WIDE)
        kept = key_feature[at, :].astype(WIDE) * ending
        state[...] += dot_left(kept.astype(LOW), values[at, :])
        total[0:1, :] += jnp.sum(kept, axis=0, keepdims=True)

    write_message(s, messages.at[0], state, total[0:1, :], last)
    send_messages(p, messages, message_send, message_recv)
    for save in saves[:4]:
        save.start()
    weights.pass_x(0)

    @pl.loop(0, s.chunks)
    def _(i):
        at = chunk_rows(s, i)
        attended[at, :] = jnp.zeros((s.chunk, s.width), WIDE)
        key_sum[at, :] = jnp.zeros((s.chunk, s.width), WIDE)

        def over(j, carry):
            to = chunk_rows(s, j)
            mask = block_mask(s, labels_down, labels_across, i, j, False)
            key_sum[at, :] += dot(mask.astype(LOW), key_feature[to, :])
            numerator = attended[at, :]
            for head in range(s.here):
                lanes = head_lanes(s.width, head)
                scores = dot_right(only(query_feature[at, :], lanes), key_feature[to, :])
                numerator = numerator + dot((scores * mask).astype(LOW), only(values[to, :], lanes))
            attended[at, :] = numerator
            return carry

        lax.fori_loop(0, i + 1, over, 0)

    weights.pass_x(1)
    take_messages(p, messages, message_send, message_recv)
    prefix_total, label = join_messages(p, messages, prefix_low, 1, p.row > 0, True)
    latest[...] = jnp.broadcast_to(label, latest.shape)

    attention = Gather(p, lambda g, k: gathered.at[g, k], att_send, att_recv)

    @pl.loop(0, s.chunks)
    def _(i):
        at = chunk_rows(s, i)
        matching = (labels_down[at, 0:1] == latest[0:1, 0:1]).astype(WIDE)
        query = query_feature[at, :].astype(WIDE)
        numerator = attended[at, :] + dot((query * matching).astype(LOW), prefix_low[...])
        sums = key_sum[at, :] + matching * prefix_total
        key_sum[at, :] = sums
        below = over_heads(query * sums, ones[...])
        denominator[at, :] = below
        value = numerator / below
        attended[at, :] = value
        gathered[p.head, i] = value.astype(LOW).astype(WIDE)
        attention.start(i)

    for save in saves[4:]:
        save.start()
    weights.pass_core()
    weights.finish()
    for group in range(s.heads):
        rows = slice(group * s.width, (group + 1) * s.width)
        weight_full[rows, :] = wide_rows[rows, :].astype(LOW)
    weights.sent()
    attention.forward(0)
    for load in loads:
        load.wait()

    def low_rows(g, k):
        start = k * s.chunk + (lax.rem(g, 2) * s.ny + g // 2) * s.sub
        return pl.ds(pl.multiple_of(start, s.sub), s.sub)

    hidden_gather = Gather(p, lambda g, k: wide_rows.at[low_rows(g, k)], low_send, low_recv)
    reduced = Reduce(p, parts, near, far, (near_send, near_recv, far_send, far_recv))
    two = Reduce(p, parts, near_two, None, (two_send, two_recv, None, None))
    first = Halving(
        p,
        lambda piece: first_gradient.at[piece],
        first_near,
        first_far,
        (first_near_send, first_near_recv, first_far_send, first_far_recv),
    )
    order = first.order
    gain_part[...] = jnp.zeros_like(gain_part)
    shares = (2, s.ny, s.sub, TILE)

    def feed_forward(k):
        at = chunk_rows(s, k)
        attention.finish(k)
        for group in range(s.heads):
            joined[:, group * s.width : (group + 1) * s.width] = gathered[group, k].astype(LOW)
        for tile in range(s.model // TILE):
            cols = slice(tile * TILE, (tile + 1) * TILE)
            product = dot(joined[...], weight_full[:, cols])
            hidden[:, :, :, cols] = product.reshape(shares) + pixels[k, :, :, :, cols].astype(WIDE)
        hidden_share[k] = hidden[p.c, p.y]
        unit, scale = normalise(hidden[...].reshape(s.chunk, s.model))
        normed_again[at, :] = (unit * second_gain[...]).astype(LOW)

        @pl.when(k + 1 < s.chunks)
        def _():
            attention.forward(k + 1)

        low = normed_again[at, :]
        back = cotangent[k].reshape(s.chunk, s.model)
        for tile in range(s.units // TILE):
            cols = slice(tile * TILE, (tile + 1) * TILE)
            upward = dot(low, up_weight[:, cols])
            middle_back = dot_right(back, down_weight[cols, :])
            root = math.sqrt(2.0 / math.pi)
            square = upward * upward
            bent = jnp.tanh(root * upward * (1.0 + 0.044715 * square))
            half = 0.5 + 0.5 * bent
            slope = half + 0.5 * upward * (1.0 - bent * bent) * (root * (1.0 + 3.0 * 0.044715 * square))
            middle[at, cols] = (upward * half).astype(LOW)
            upward_low[at, cols] = (middle_back * slope).astype(LOW)
        low = upward_low[at, :]
        for tile in range(s.model // TILE):
            cols = slice(tile * TILE, (tile + 1) * TILE)
            parts[k, :, :, :, cols] = dot_right(low, up_weight[cols, :]).reshape(shares)
        reduced.start(k)

    def second_norm_back(k):
        grad = reduced.total(k)
        unit, scale = normalise(hidden_share[k])
        gain_part[0:1, :] += jnp.sum(grad * unit, axis=0, keepdims=True)
        part = normalise_back(unit, scale, second_gain[...], grad)
        value = cotangent[k, p.c, p.y].astype(WIDE) + part
        gradient_share[k] = value
        wide_rows[low_rows(p.head, k), :] = value.astype(LOW).astype(WIDE)
        hidden_gather.start(k)

    span = s.nx * s.cut

    def span_of(turn):
        return pl.ds(pl.multiple_of(first.piece(order[turn]) * span, span), span)

    def first_outer(turn):
        block = normed_again[:, span_of(turn)]
        target = first_gradient.at[first.piece(order[turn])]
        for at in range(0, s.first, s.step):
            cols = slice(at, at + s.step)
            target[:, :, cols] = dot_left(block, upward_low[:, cols]).reshape(s.nx, s.cut, s.step)
        first.start(order[turn])

    def first_join(turn):
        first.join(order[turn], first_gradient[first.piece(order[turn]), p.x])
        if order[turn] % 2:
            first.settle(order[turn])

    def staged(turn):
        slot = turn % 2
        return pltpu.make_async_copy(staging.at[slot], wide_gradient.at[first.piece(order[turn])], staging_sem.at[slot])

    def rest_outer(turn):
        if turn >= 2:
            staged(turn - 2).wait()
        target = staging.at[turn % 2]
        block = normed_again[:, span_of(turn)]
        for at in range(s.first, s.units, s.step):
            cols = slice(at - s.first, at - s.first + s.step)
            value = dot_left(block, upward_low[:, at : at + s.step])
            target[:, :, cols] = value.reshape(s.nx, s.cut, s.step)
        block = cotangent[:, :, :, :, span_of(turn)].reshape(s.tokens, span)
        for at in range(0, s.units, TILE):
            cols = slice(s.units - s.first + at, s.units - s.first + at + TILE)
            value = dot_left(block, middle[:, at : at + TILE])
            target[:, :, cols] = value.reshape(s.nx, s.cut, TILE)
        staged(turn).start()

    @pl.loop(0, s.chunks)
    def _(k):
        feed_forward(k)

        @pl.when(k >= 1)
        def _():
            reduced.middle(k - 1)

    end = s.chunks
    first_outer(0)
    reduced.middle(end - 1)
    for turn in range(1, s.nz):
        first_outer(turn)
    for k in range(end - 2):
        second_norm_back(k)
    rest_outer(0)
    for k in range(end - 2, end):
        second_norm_back(k)
        first_join(k - end + 2)
        rest_outer(k - end + 3)
    first.settle(order[1])
    for turn in range(3, s.nz):
        rest_outer(turn)

    @pl.loop(0, s.chunks)
    def _(k):
        reduced.near_sent(k)
        low = middle[chunk_rows(s, k), :]
        for tile in range(s.model // TILE):
            cols = slice(tile * TILE, (tile + 1) * TILE)
            parts[k, :, :, :, cols] = dot(low, down_weight[:, cols]).reshape(shares)
        two.start(k)

    for turn in range(2, s.nz - 1):
        first_join(turn)
        if order[turn] % 2 == 0:
            first.settle(order[turn])
    for k in range(end - 2):
        hidden_gather.forward(k)
    for k in range(s.chunks):
        two.join(k)
        pixel_share[k] = pixels[k, p.c, p.y]
    first_join(s.nz - 1)
    hidden_gather.forward(end - 2)
    first.settle(0)
    hidden_gather.forward(end - 1)

    for k in range(s.chunks):
        hidden_gather.finish(k)
        rows = slice(k * s.chunk, (k + 1) * s.chunk)
        hidden_low[rows, :] = wide_rows[rows, :].astype(LOW)
    first_out[...] = first.total()
    first.sent()
    for turn in range(max(0, s.nz - 2), s.nz):
        staged(turn).wait()
    for k in range(s.chunks):
        attention.sent(k)
        hidden_gather.sent(k)
        reduced.far_sent(k)
        two.near_sent(k)
    for save in saves:
        save.wait()


def backward_kernel(
    s,
    crop_ids,
    gain_part,
    prefix_low,
    latest,
    first_gain,
    near_two,
    normed_source,
    hidden_source,
    gradient_source,
    pixel_source,
    wide_gradient,
    query_feature_source,
    key_feature_source,
    values_source,
    attended_source,
    denominator_source,
    key_sum_source,
    hidden_low_source,
    query_weight_source,
    key_weight_source,
    value_weight_source,
    out_weight_source,
    gains,
    wide_out,
    narrow_out,
    pixel_out,
    result_out,
    query_feature,
    key_feature,
    values,
    attended,
    denominator,
    key_sum,
    hidden_low,
    query_weight,
    key_weight,
    value_weight,
    out_weight,
    normed,
    hidden_share,
    gradient_share,
    pixel_share,
    two_own,
    labels_across,
    labels_down,
    parts,
    far_two,
    near_four,
    far_four,
    result_wide,
    result_low,
    pixel_gradient,
    numerator_low,
    denominator_back,
    spread_back,
    query_back,
    key_back,
    value_back,
    narrow_low,
    suffix_low,
    state,
    total,
    ones,
    messages,
    narrow_gradient,
    own_wide,
    own_pairs,
    near_wide,
    far_wide,
    near_split,
    far_split,
    pairs_split,
    near_narrow,
    far_narrow,
    gain_heads,
    gain_x,
    gain_z,
    load_sem,
    input_sem,
    message_send,
    message_recv,
    two_far_send,
    two_far_recv,
    four_near_send,
    four_near_recv,
    four_far_send,
    four_far_recv,
    result_send,
    result_recv,
    pixel_send,
    pixel_recv,
    wide_near_send,
    wide_near_recv,
    wide_far_send,
    wide_far_recv,
    split_near_send,
    split_near_recv,
    split_far_send,
    split_far_recv,
    split_send,
    split_recv,
    narrow_near_send,
    narrow_near_recv,
    narrow_far_send,
    narrow_far_recv,
    gain_send,
    gain_recv,
    own_sem,
    pairs_sem,
    result_sem,
    pixel_sem,
):
    p = Place(s)
    inputs = [
        pltpu.make_async_copy(source, target, input_sem.at[i])
        for i, (source, target) in enumerate(
            (
                (hidden_low_source, hidden_low),
                (out_weight_source, out_weight),
                (denominator_source, denominator),
                (attended_source, attended),
                (query_feature_source, query_feature),
                (key_feature_source, key_feature),
                (values_source, values),
                (key_sum_source, key_sum),
                (query_weight_source, query_weight),
                (key_weight_source, key_weight),
                (value_weight_source, value_weight),
            )
        )
    ]
    for load in inputs:
        load.start()
    p.meet()
    two = Reduce(p, None, near_two, far_two, (None, None, two_far_send, two_far_recv))
    four = Reduce(p, parts, near_four, far_four, (four_near_send, four_near_recv, four_far_send, four_far_recv))
    wide = Halving(
        p,
        lambda piece: wide_gradient.at[piece, :, :, s.split :],
        near_wide,
        far_wide,
        (wide_near_send, wide_near_recv, wide_far_send, wide_far_recv),
    )
    split = Halving(
        p,
        lambda piece: wide_gradient.at[piece, :, :, 0 : s.split],
        near_split,
        far_split,
        (split_near_send, split_near_recv, split_far_send, split_far_recv),
        pairs_split,
        (split_send, split_recv),
    )
    sides = (slice(0, s.narrow // 2), slice(s.narrow // 2, s.narrow))

    def narrow_job(i):
        sems = (narrow_near_send.at[i], narrow_near_recv.at[i], narrow_far_send.at[i], narrow_far_recv.at[i])
        return Halving(
            p, lambda piece: narrow_gradient.at[piece, :, :, sides[i]], near_narrow.at[i], far_narrow.at[i], sems
        )

    narrow = (narrow_job(0), narrow_job(1))
    jobs = (wide, split) + narrow
    whole_wide = [(wide, m) for m in wide.order]
    whole_split = [(split, m) for m in split.order]
    whole_narrow = [(job, m) for job in narrow for m in job.order]
    steps = whole_wide + whole_split[:1] + whole_narrow[:1] + whole_split[1:] + whole_narrow[1:]
    flight = {"next": 0, "taken": 0}
    ready = list(whole_wide)
    pending = []

    def push(limit):
        while flight["next"] <= min(limit, len(steps) - 1) and steps[flight["next"]] in ready:
            job, m = steps[flight["next"]]
            job.start(m)
            flight["next"] += 1

    def admit(entries):
        ready.extend(entries)
        push(flight["taken"] + AHEAD - 1)

    def settle_ready(at):
        for entry in list(pending):
            if entry[0] <= at:
                entry[1].settle(entry[2])
                pending.remove(entry)

    def own_load(turn):
        source = wide_gradient.at[wide.piece(wide.order[turn]), p.x, :, s.split :]
        return pltpu.make_async_copy(source, own_wide.at[turn % 2], own_sem.at[turn % 2])

    def pairs_load(m):
        source = wide_gradient.at[split.piece(m), :, :, 0 : s.split]
        return pltpu.make_async_copy(source, own_pairs.at[m >> 1], pairs_sem.at[m >> 1])

    def take():
        at = flight["taken"]
        assert flight["next"] > at
        job, m = steps[at]
        flight["taken"] = at + 1
        if job is wide:
            own_load(at).wait()
            wide.join(m, own_wide[at % 2])
            if at + 2 < s.nz:
                own_load(at + 2).start()
        elif job is split:
            split.join(m)
        else:
            job.join(m, narrow_gradient[job.piece(m), p.x, :, sides[narrow.index(job)]])
        push(at + AHEAD)
        if (m >> job.first_bit) & 1:
            job.settle(m)
        else:
            pending.append((at + 2 if m else at + 4, job, m))
        settle_ready(at)

    def take_while(*names):
        while flight["taken"] < len(steps) and steps[flight["taken"]][0] in names:
            take()

    pair_copies = [(m, x) for m in split.odd for x in range(s.nx)]
    split.pair_copy(*pair_copies[0]).start()
    push(0)
    for k in range(s.chunks):
        two.spread(k)
    loads = [
        pltpu.make_async_copy(source, target, load_sem.at[i])
        for i, (source, target) in enumerate(
            (
                (near_two.at[:, p.y], two_own),
                (hidden_source, hidden_share),
                (gradient_source, gradient_share),
                (pixel_source, pixel_share),
                (normed_source, normed),
            )
        )
    ]
    for load in loads:
        load.start()
    own_load(0).start()
    own_load(1).start()
    for m in split.order:
        pairs_load(m).start()
    result_gather = Gather(p, lambda g, k: result_wide.at[k, lax.rem(g, 2), g // 2], result_send, result_recv)
    pixel_gather = Gather(p, lambda g, k: pixel_gradient.at[k, lax.rem(g, 2), g // 2], pixel_send, pixel_recv)
    shares = (2, s.ny, s.sub, TILE)
    spread_labels(s, crop_ids, labels_across, labels_down)
    first = labels_across[0][:, 0:1]
    state[...] = jnp.zeros_like(state)
    total[...] = jnp.zeros_like(total)
    ones[...] = block_ones(s.width)

    for load in inputs:
        load.wait()

    @pl.loop(0, s.chunks)
    def _(k):
        at = chunk_rows(s, k)
        back = dot_right(hidden_low[at, :], out_weight[...])
        below = denominator[at, :]
        low = (back / below).astype(LOW)
        numerator_low[at, :] = low
        slope = -over_heads(back * attended[at, :], ones[...]) / below
        denominator_back[at, :] = slope
        query = query_feature[at, :].astype(WIDE)
        spread = slope * query
        spread_back[at, :] = spread.astype(LOW)
        leading = (labels_down[at, 0:1] == first).astype(WIDE)
        state[...] += dot_left((query * leading).astype(LOW), low)
        total[0:1, :] += jnp.sum(spread * leading, axis=0, keepdims=True)

    write_message(s, messages.at[0], state, total[0:1, :], first)
    send_messages(p, messages, message_send, message_recv)
    for entry in pair_copies[1 : s.nx]:
        split.pair_copy(*entry).start()
    push(1)

    @pl.loop(0, s.chunks)
    def _(i):
        at = chunk_rows(s, i)
        query_back[at, :] = denominator_back[at, :] * key_sum[at, :]

        def over(j, carry):
            to = chunk_rows(s, j)
            mask = block_mask(s, labels_down, labels_across, i, j, False)
            value = query_back[at, :]
            for head in range(s.here):
                lanes = head_lanes(s.width, head)
                scores = dot_right(only(numerator_low[at, :], lanes), values[to, :])
                value = value + dot((scores * mask).astype(LOW), only(key_feature[to, :], lanes))
            query_back[at, :] = value
            return carry

        lax.fori_loop(0, i + 1, over, 0)

    take()
    for entry in pair_copies[s.nx :]:
        split.pair_copy(*entry).start()

    @pl.loop(0, s.chunks)
    def _(j):
        to = chunk_rows(s, j)
        key_back[to, :] = jnp.zeros((s.chunk, s.width), WIDE)
        value_back[to, :] = jnp.zeros((s.chunk, s.width), WIDE)

        def over(i, carry):
            at = chunk_rows(s, i)
            mask = block_mask(s, labels_down, labels_across, i, j, True)
            key_value = key_back[to, :] + dot(mask.astype(LOW), spread_back[at, :])
            value_value = value_back[to, :]
            for head in range(s.here):
                lanes = head_lanes(s.width, head)
                back = dot_right(only(values[to, :], lanes), numerator_low[at, :])
                key_value = key_value + dot((back * mask).astype(LOW), only(query_feature[at, :], lanes))
                scores = dot_right(only(key_feature[to, :], lanes), query_feature[at, :])
                value_value = value_value + dot((scores * mask).astype(LOW), only(numerator_low[at, :], lanes))
            key_back[to, :] = key_value
            value_back[to, :] = value_value
            return carry

        lax.fori_loop(j, s.chunks, over, 0)

    for load in loads:
        load.wait()

    @pl.loop(0, s.chunks)
    def _(k):
        value = hidden_share[k] + two.total(k, two_own[k])
        result_wide[k, p.c, p.y] = value.astype(LOW).astype(WIDE)

        @pl.when(k < s.chunks // 2)
        def _():
            result_gather.start(k)

    take()
    take_messages(p, messages, message_send, message_recv)
    suffix_total, following = join_messages(p, messages, suffix_low, s.rows - 1, p.row < s.rows - 1, False)

    @pl.loop(0, s.chunks)
    def _(k):
        at = chunk_rows(s, k)
        matching = (labels_down[at, 0:1] == latest[0:1, 0:1]).astype(WIDE)
        later = (labels_down[at, 0:1] == following).astype(WIDE)
        query, key = query_feature[at, :], key_feature[at, :]
        value = query_back[at, :] + matching * dot_right(numerator_low[at, :], prefix_low[...])
        low = (value * jnp.minimum(query.astype(WIDE), 1.0)).astype(LOW)
        numerator_value = value_back[at, :] + later * dot(key, suffix_low[...])
        key_value = key_back[at, :] + later * (dot_right(values[at, :], suffix_low[...]) + suffix_total)
        key_low = (key_value * jnp.minimum(key.astype(WIDE), 1.0)).astype(LOW)
        value_low = numerator_value.astype(LOW)
        narrow_low[0, at, :] = low
        narrow_low[1, at, :] = key_low
        narrow_low[2, at, :] = value_low
        for tile in range(s.model // TILE):
            cols = slice(tile * TILE, (tile + 1) * TILE)
            product = (
                dot_right(low, query_weight[cols, :])
                + dot_right(key_low, key_weight[cols, :])
                + dot_right(value_low, value_weight[cols, :])
            )
            parts[k, :, :, :, cols] = product.reshape(shares)
        four.start(k)

    @pl.loop(0, s.chunks)
    def _(k):
        four.middle(k)

    for k in range(s.chunks // 2, s.chunks):
        result_gather.start(k)
    take()

    def split_ready(m):
        pairs_load(m).wait()
        split.join_pair(m, own_pairs[m >> 1])
        admit([(split, m)])

    split_ready(split.order[0])
    span = s.nx * s.cut
    for piece in range(s.nz):
        cols = slice(piece * span, (piece + 1) * span)
        shape = (s.nx, s.cut, s.width)
        product = dot_left(hidden_low[:, cols], attended[...].astype(LOW))
        narrow_gradient[piece, :, :, 0 : s.width] = product.reshape(shape)
        for part in range(3):
            product = dot_left(normed[:, cols], narrow_low[part])
            narrow_gradient[piece, :, :, (part + 1) * s.width : (part + 2) * s.width] = product.reshape(shape)
    admit(whole_narrow)
    take_while(wide)
    for m in split.order[1:]:
        split_ready(m)
    gain_x[0] = gain_part[...]

    def take_until_left(count):
        while len(steps) - flight["taken"] > count:
            take()

    def result_copy(k):
        rows = pl.ds(k * s.chunk, s.chunk)
        return pltpu.make_async_copy(result_low.at[rows], result_out.at[rows], result_sem.at[k])

    def pixel_copy(k):
        return pltpu.make_async_copy(pixel_gradient.at[k], pixel_out.at[k], pixel_sem.at[k])

    def first_norm_back(k):
        grad = four.total(k)
        unit, scale = normalise(pixel_share[k].astype(WIDE))
        gain_x[0, 1:2, :] += jnp.sum(grad * unit, axis=0, keepdims=True)
        pixel_gradient[k, p.c, p.y] = gradient_share[k] + normalise_back(unit, scale, first_gain[...], grad)
        pixel_gather.start(k)

    first_norm_back(0)
    take()
    for k in range(1, s.chunks - 1):
        first_norm_back(k)
        take_while(split)
    take_until_left(2 * s.nz - 1)
    first_norm_back(s.chunks - 1)

    def gain_copies(index, buffer, device):
        return [
            remote(buffer.at[0], buffer.at[step], gain_send.at[index, step], gain_recv.at[index, step], device(step))
            for step in range(1, buffer.shape[0])
        ]

    def gain_start(*what):
        for copy in gain_copies(*what):
            copy.start()

    def gain_total(*what):
        for copy in gain_copies(*what):
            copy.wait()
        value = what[1][0]
        for step in range(1, what[1].shape[0]):
            value = value + what[1][step]
        return value

    rounds = (
        (0, gain_x, p.along_x),
        (1, gain_z, p.along_z),
        (2, gain_heads, p.along_heads),
    )
    gain_start(*rounds[0])
    for k in range(s.chunks // 2):
        result_gather.forward(k)
    take_until_left(2 * s.nz - 3)
    for k in range(s.chunks // 2, s.chunks):
        result_gather.forward(k)
    gain_z[0] = gain_total(*rounds[0])
    gain_start(*rounds[1])
    for k in range(s.chunks // 2):
        pixel_gather.forward(k)
    take_until_left(3)
    gain_heads[0] = gain_total(*rounds[1])
    gain_start(*rounds[2])
    for k in range(s.chunks // 2, s.chunks):
        pixel_gather.forward(k)
    take_until_left(2)
    for k in range(s.chunks):
        pixel_gather.finish(k)
        pixel_copy(k).start()
    for k in range(s.chunks):
        result_gather.finish(k)
        result_low[k * s.chunk : (k + 1) * s.chunk, :] = result_wide[k].reshape(s.chunk, s.model).astype(LOW)
        result_copy(k).start()
    gains[...] = gain_total(*rounds[2])
    take_until_left(0)
    settle_ready(len(steps) + 4)
    wide_out[:, s.split :] = wide.total()
    wide_out[:, 0 : s.split] = split.total()
    for job, side in zip(narrow, sides):
        narrow_out[:, side] = job.total()
    for k in range(s.chunks):
        result_copy(k).wait()
        pixel_copy(k).wait()
        pixel_gather.sent(k)
        result_gather.sent(k)
        two.far_sent(k)
        four.near_sent(k)
        four.far_sent(k)
    for job in jobs:
        job.sent()


def finish_kernel(
    s,
    gains,
    first_source,
    wide_source,
    narrow_source,
    pixel_source,
    result_source,
    first_gain,
    second_gain,
    up_gradient,
    down_gradient,
    out_gradient,
    query_gradient,
    key_gradient,
    value_gradient,
    pixel_gradient,
    result,
    pixel_rows,
    result_rows,
    first_out,
    wide_out,
    narrow_out,
    down_turned,
    out_turned,
    read_sem,
    write_sem,
    small_sem,
):
    row = lax.axis_index("rows")
    rest = s.units - s.first

    def places(i, k):
        rows = pl.ds(k * s.chunk, s.chunk)
        if i == 0:
            return pixel_source.at[k], pixel_rows.at[k], pixel_gradient.at[k]
        return result_source.at[rows], result_rows.at[rows], result.at[rows]

    def read(i, k):
        source, between, unused = places(i, k)
        return pltpu.make_async_copy(source, between, read_sem.at[i, k])

    def write(i, k):
        unused, between, target = places(i, k)
        return pltpu.make_async_copy(between, target, write_sem.at[i, k])

    def small(at, source, target):
        return pltpu.make_async_copy(source, target, small_sem.at[at])

    reads = [
        small(0, wide_source, wide_out),
        small(1, narrow_source, narrow_out),
        small(2, first_source, first_out),
    ]
    moves = [(i, k) for k in range(s.chunks) for i in range(2)]
    for copy in reads:
        copy.start()
    for move in moves:
        read(*move).start()
    own = jnp.zeros((8, s.cut), WIDE)
    for at in range(s.rows):
        own = own + jnp.where(row == at, gains[:, at * s.cut : (at + 1) * s.cut], 0.0)
    second_gain[...] = own[0:1]
    first_gain[...] = own[1:2]
    for copy in reads:
        copy.wait()
    writes = [
        small(3, first_out, up_gradient.at[:, 0 : s.first]),
        small(4, wide_out.at[:, 0:rest], up_gradient.at[:, s.first :]),
    ]
    for i, target in enumerate((query_gradient, key_gradient, value_gradient)):
        writes.append(small(5 + i, narrow_out.at[:, (i + 1) * s.width : (i + 2) * s.width], target))
    for copy in writes:
        copy.start()
    down_turned[...] = wide_out[:, rest:].T
    out_turned[...] = narrow_out[:, 0 : s.width].T
    for at, source, target in ((8, down_turned, down_gradient), (9, out_turned, out_gradient)):
        writes.append(small(at, source, target))
        writes[-1].start()
    for move in moves:
        read(*move).wait()
        write(*move).start()
    for move in moves:
        write(*move).wait()
    for copy in writes:
        copy.wait()


def vmem(count):
    return [pl.BlockSpec(memory_space=pltpu.VMEM)] * count


def dma(*shape):
    return pltpu.SemaphoreType.DMA(shape)


def on_device(
    rows,
    heads,
    pixels,
    crop_ids,
    first_gain,
    query_weight,
    key_weight,
    value_weight,
    out_weight,
    second_gain,
    up_weight,
    down_weight,
    cotangent,
):
    tokens, model = pixels.shape
    s = Sizes(rows, heads, tokens, model, query_weight.shape[1], up_weight.shape[1])
    whole = (s.chunks, 2, s.ny, s.sub, model)
    share = (s.chunks, s.sub, model)
    labels = crop_ids.reshape(s.chunks, 1, s.chunk)
    shape = jax.ShapeDtypeStruct
    any_space = pl.BlockSpec(memory_space=pl.ANY)

    def reduce_sems():
        return [
            dma(s.chunks),
            dma(s.chunks),
            dma(s.ny - 1, s.chunks),
            dma(s.ny - 1, s.chunks),
        ]

    def gather_sems():
        return [dma(2 * s.ny - 1, s.chunks), dma(heads, s.chunks)]

    def scatter_sems():
        return [
            dma(s.nx - 1, s.nz),
            dma(s.nx - 1, s.nz),
            dma(s.nz - 1),
            dma(s.nz - 1),
        ]

    def scatter_buffers(width, pieces=s.nz):
        return [
            pltpu.VMEM((s.nx - 1, pieces, s.cut, width), WIDE),
            pltpu.VMEM((pieces - 1, s.cut, width), WIDE),
        ]

    half = s.nz // 2

    lows = [(tokens, model)] + [(tokens, s.width)] * 3
    wides = [(tokens, s.width)] * 3
    near = (s.chunks, s.ny, s.sub, model)
    far = (s.ny - 1,) + share
    label_buffers = [
        pltpu.VMEM((s.chunks, 1, s.chunk), WIDE),
        pltpu.VMEM((tokens, LANES), WIDE),
    ]
    outs = [
        shape((tokens, model), LOW),
        shape(share, WIDE),
        shape(share, WIDE),
        shape(share, LOW),
        shape((8, model), WIDE),
        shape((s.width, s.width), LOW),
        shape((8, LANES), WIDE),
        shape(near, WIDE),
        shape((s.cut, s.first), WIDE),
        *[shape(size, LOW) for size in lows],
        *[shape(size, WIDE) for size in wides],
        shape((s.nz, s.nx, s.cut, s.wide), WIDE),
    ]
    shared = WeightGather.halves
    (
        hidden_low,
        hidden_share,
        gradient_share,
        pixel_share,
        gain_part,
        prefix_low,
        latest,
        near_two,
        first_out,
        normed,
        query_feature,
        key_feature,
        values,
        attended,
        denominator,
        key_sum,
        wide_gradient,
    ) = pl.pallas_call(
        functools.partial(forward_kernel, s),
        out_shape=outs,
        in_specs=vmem(8) + [any_space] * 3,
        out_specs=vmem(9) + [any_space] * 8,
        scratch_shapes=[
            *[pltpu.VMEM(size, LOW) for size in lows],
            *[pltpu.VMEM(size, WIDE) for size in wides],
            pltpu.VMEM((model, s.units), LOW),
            pltpu.VMEM((s.units, model), LOW),
            pltpu.VMEM(whole, LOW),
            *label_buffers,
            pltpu.VMEM((heads, s.chunks, s.chunk, s.width), WIDE),
            pltpu.VMEM((max(tokens, model), model), WIDE),
            pltpu.VMEM((model, model), LOW),
            pltpu.VMEM((s.chunk, model), LOW),
            pltpu.VMEM(whole[1:], WIDE),
            pltpu.VMEM((tokens, model), LOW),
            pltpu.VMEM((tokens, s.units), LOW),
            pltpu.VMEM((tokens, s.units), LOW),
            pltpu.VMEM(whole, WIDE),
            pltpu.VMEM(near, WIDE),
            pltpu.VMEM(far, WIDE),
            pltpu.VMEM((rows, s.message, LANES), WIDE),
            pltpu.VMEM((s.width, s.width), WIDE),
            pltpu.VMEM((8, s.width), WIDE),
            pltpu.VMEM((s.width, s.width), LOW),
            pltpu.VMEM((2, s.nx, s.cut, s.wide), WIDE),
            pltpu.VMEM((s.nz, s.nx, s.cut, s.first), WIDE),
            *scatter_buffers(s.first),
            dma(3),
            dma(7),
            dma(2),
            *[dma(s.ny - 1, shared)] * 2,
            *[dma(s.ny - 1, s.nx - 1, shared)] * 2,
            *[dma(s.ny)] * 2,
            *gather_sems(),
            *gather_sems(),
            dma(rows),
            dma(rows),
            *reduce_sems(),
            dma(s.chunks),
            dma(s.chunks),
            *scatter_sems(),
        ],
        compiler_params=pltpu.CompilerParams(
            collective_id=0, has_side_effects=True, vmem_limit_bytes=60 << 20
        ),
        name="forward_part",
    )(
        pixels.reshape(whole),
        labels,
        first_gain.reshape(1, model),
        query_weight,
        key_weight,
        value_weight,
        out_weight,
        second_gain.reshape(1, model),
        up_weight,
        down_weight,
        cotangent.reshape(whole),
    )
    outs = [
        shape((8, model), WIDE),
        shape((s.cut, s.wide), WIDE),
        shape((s.cut, s.narrow), WIDE),
        shape(whole, WIDE),
        shape((tokens, model), LOW),
    ]
    gains, wide_out, narrow_out, pixel_wide, result_low = pl.pallas_call(
        functools.partial(backward_kernel, s),
        out_shape=outs,
        in_specs=vmem(5) + [any_space] * 17,
        out_specs=vmem(3) + [any_space] * 2,
        scratch_shapes=[
            *[pltpu.VMEM(size, LOW) for size in lows[1:]],
            *[pltpu.VMEM(size, WIDE) for size in wides],
            pltpu.VMEM((tokens, model), LOW),
            *[pltpu.VMEM((model, s.width), LOW)] * 3,
            pltpu.VMEM((s.width, model), LOW),
            pltpu.VMEM((tokens, model), LOW),
            pltpu.VMEM(share, WIDE),
            pltpu.VMEM(share, WIDE),
            pltpu.VMEM(share, LOW),
            pltpu.VMEM(share, WIDE),
            *label_buffers,
            pltpu.VMEM(whole, WIDE),
            pltpu.VMEM(far, WIDE),
            pltpu.VMEM(near, WIDE),
            pltpu.VMEM(far, WIDE),
            pltpu.VMEM(whole, WIDE),
            pltpu.VMEM((tokens, model), LOW),
            pltpu.VMEM(whole, WIDE),
            pltpu.VMEM((tokens, s.width), LOW),
            pltpu.VMEM((tokens, s.width), WIDE),
            pltpu.VMEM((tokens, s.width), LOW),
            *[pltpu.VMEM((tokens, s.width), WIDE)] * 3,
            pltpu.VMEM((3, tokens, s.width), LOW),
            pltpu.VMEM((s.width, s.width), LOW),
            pltpu.VMEM((s.width, s.width), WIDE),
            pltpu.VMEM((8, s.width), WIDE),
            pltpu.VMEM((s.width, s.width), LOW),
            pltpu.VMEM((rows, s.message, LANES), WIDE),
            pltpu.VMEM((s.nz, s.nx, s.cut, s.narrow), WIDE),
            pltpu.VMEM((2, s.cut, s.wide - s.split), WIDE),
            pltpu.VMEM((half, s.nx, s.cut, s.split), WIDE),
            *scatter_buffers(s.wide - s.split),
            *scatter_buffers(s.split, half),
            pltpu.VMEM((half, s.nx, s.cut, s.split), WIDE),
            pltpu.VMEM((2, s.nx - 1, s.nz, s.cut, s.narrow // 2), WIDE),
            pltpu.VMEM((2, s.nz - 1, s.cut, s.narrow // 2), WIDE),
            pltpu.VMEM((heads, 8, model), WIDE),
            pltpu.VMEM((s.nx, 8, model), WIDE),
            pltpu.VMEM((s.nz, 8, model), WIDE),
            dma(5),
            dma(11),
            dma(rows),
            dma(rows),
            *reduce_sems()[2:],
            *reduce_sems(),
            *gather_sems(),
            *gather_sems(),
            *scatter_sems(),
            *scatter_sems(),
            dma(half, s.nx),
            dma(half, s.nx),
            *[dma(2, s.nx - 1, s.nz)] * 2,
            *[dma(2, s.nz - 1)] * 2,
            dma(3, max(heads, s.nx, s.nz)),
            dma(3, max(heads, s.nx, s.nz)),
            dma(2),
            dma(half),
            dma(s.chunks),
            dma(s.chunks),
        ],
        compiler_params=pltpu.CompilerParams(
            collective_id=1, has_side_effects=True, vmem_limit_bytes=60 << 20
        ),
        name="backward_part",
    )(
        labels,
        gain_part,
        prefix_low,
        latest,
        first_gain.reshape(1, model),
        near_two,
        normed,
        hidden_share,
        gradient_share,
        pixel_share,
        wide_gradient,
        query_feature,
        key_feature,
        values,
        attended,
        denominator,
        key_sum,
        hidden_low,
        query_weight,
        key_weight,
        value_weight,
        out_weight,
    )
    outs = [
        *[shape((1, s.cut), WIDE)] * 2,
        shape((s.cut, s.units), WIDE),
        shape((s.units, s.cut), WIDE),
        shape((s.width, s.cut), WIDE),
        *[shape((s.cut, s.width), WIDE)] * 3,
        shape(whole, WIDE),
        shape((tokens, model), LOW),
    ]
    first_part, second_part, up_part, down_part, out_part, query_part, key_part, value_part, pixel_part, result = (
        pl.pallas_call(
            functools.partial(finish_kernel, s),
            out_shape=outs,
            in_specs=vmem(1) + [any_space] * 5,
            out_specs=vmem(2) + [any_space] * 8,
            scratch_shapes=[
                pltpu.VMEM(whole, WIDE),
                pltpu.VMEM((tokens, model), LOW),
                pltpu.VMEM((s.cut, s.first), WIDE),
                pltpu.VMEM((s.cut, s.wide), WIDE),
                pltpu.VMEM((s.cut, s.narrow), WIDE),
                pltpu.VMEM((s.units, s.cut), WIDE),
                pltpu.VMEM((s.width, s.cut), WIDE),
                dma(2, s.chunks),
                dma(2, s.chunks),
                dma(10),
            ],
            compiler_params=pltpu.CompilerParams(vmem_limit_bytes=60 << 20),
            name="finish_part",
        )(gains, first_out, wide_out, narrow_out, pixel_wide, result_low)
    )
    return (
        result,
        pixel_part.reshape(tokens, model),
        first_part.reshape(s.cut),
        query_part,
        key_part,
        value_part,
        out_part,
        second_part.reshape(s.cut),
        up_part,
        down_part,
    )


def solution(mesh):
    return jax.shard_map(
        functools.partial(on_device, mesh.shape["rows"], mesh.shape["heads"]),
        mesh=mesh,
        in_specs=(
            P("rows", None),
            P("rows"),
            P(),
            P(None, "heads"),
            P(None, "heads"),
            P(None, "heads"),
            P("heads", None),
            P(),
            P(None, "heads"),
            P("heads", None),
            P("rows", None),
        ),
        out_specs=(
            P("rows", None),
            P("rows", None),
            P("rows"),
            P("rows", "heads"),
            P("rows", "heads"),
            P("rows", "heads"),
            P("heads", "rows"),
            P("rows"),
            P("rows", "heads"),
            P("heads", "rows"),
        ),
        check_vma=False,
    )
```
